32 devices in a mesh: seq: 16 (over z, x, core), fsdp: 2 (over y).
Axes of the slice: x: 2, y: 2, z: 4, core: 2. Of those that a mesh axis runs over, the one named last changes fastest.
Arguments:
- inputs: bfloat16 [2, 16384, 1024], P(None, 'seq', 'fsdp'), may hold values from -6 to 6
- first_factor: bfloat16 [128, 128, 128], P('seq'), may hold values from -0.5 to 0.5
- second_factor: bfloat16 [128, 128, 128], P('seq'), may hold values from -0.5 to 0.5
- gate_scale: float32 [1024], P('fsdp'), may hold values from -2 to 2
- gate_bias: float32 [1024], P('fsdp'), may hold values from -3 to 3
- in_weight: bfloat16 [1024, 4096], P('seq', 'fsdp'), may hold values from -0.1875 to 0.1875
- out_weight: bfloat16 [4096, 1024], P('fsdp', 'seq'), may hold values from -0.09375 to 0.09375
- cotangent: bfloat16 [2, 16384, 1024], P(None, 'seq', 'fsdp'), may hold values from -6 to 6
Outputs:
- result: bfloat16 [2, 16384, 1024], P(None, 'seq', 'fsdp')
- input_grad: bfloat16 [2, 16384, 1024], P(None, 'seq', 'fsdp')
- grad_in: float32 [1024, 4096], P('seq', 'fsdp')
- grad_out: float32 [4096, 1024], P('fsdp', 'seq')
The draws below stay inside these ranges and needn't reach their ends.
All inputs are finite; a program needn't handle non-finite values.
Results may differ from the reference program's by a relative error of at most 0.0075.
Values may be sent and summed in bfloat16 or wider, within the bound.
A program may use at most 192 MiB of HBM per device.

```python
import jax
import jax.numpy as jnp
from jax import lax

CH = 1024
FF = 4096
NB = 128
BS = 128
NSEQ = 2
SEQLEN = 16384


def with_spikes(array, rng, source, target, blocks, factor):
    owner, partner = [(jnp.arange(array.shape[position]) // (array.shape[position] // blocks)).reshape([-1 if axis == position else 1 for axis in range(array.ndim)]) for position in (source, target)]
    chosen = jax.random.permutation(rng, blocks)[partner]
    strong = (owner == chosen) | (owner == (partner + blocks // 2) % blocks)
    return jnp.where(strong, factor * array, array)


def level_of(key, extent, shards, least, high):
    def one(dim, blocks):
        draws = jax.random.uniform(jax.random.fold_in(jax.random.fold_in(key, 6), dim), (blocks,), jnp.float32, least / len(shards), high / len(shards))
        return jnp.repeat(jnp.exp(draws), extent[dim] // blocks).reshape((-1,) + (1,) * (len(extent) - dim - 1))

    level = one(*shards[0])
    for cut in shards[1:]:
        level = level * one(*cut)
    return level


def centred(rng, shape, deviation, bound, pieces=(), held_as=jnp.bfloat16):
    values = jax.random.normal(rng, shape, jnp.float32) * deviation
    if len(pieces) > 0:
        values = level_of(rng, shape, pieces, -0.22, 0.18) * values
    return jnp.clip(values, min=-bound, max=bound).astype(held_as)


def heavy_noise(key, extent, scale, reach, shards, heavy, dtype=jnp.bfloat16):
    values = scale * jax.random.normal(key, extent, jnp.float32)
    if shards:
        values = values * level_of(key, extent, shards, -0.22, 0.18)
    return jnp.clip(with_spikes(values, jax.random.fold_in(key, 3), *heavy), -reach, reach).astype(dtype)


def setup_inputs(seed: int = 0) -> dict:
    splits = jax.random.split(jax.random.key(seed), 9)
    return {
        "inputs": centred(splits[0], (NSEQ, SEQLEN, CH), 1.0, 6.0, ((1, 16), (2, 2))),
        "first_factor": centred(splits[1], (NB, BS, BS), BS ** -0.5, 0.5, ((0, 16),)),
        "second_factor": centred(splits[2], (BS, NB, NB), NB ** -0.5, 0.5, ((0, 16),)),
        "gate_scale": jnp.clip(jax.random.uniform(splits[3], (CH,), jnp.float32, -2.0, 2.0) * level_of(splits[3], (CH,), ((0, 2),), -0.4, 0.0), -2.0, 2.0),
        "gate_bias": centred(splits[4], (CH,), 0.7, 3.0, ((0, 2),), jnp.float32),
        "in_weight": centred(splits[5], (CH, FF), CH ** -0.5, 0.1875, ((0, 16), (1, 2))),
        "out_weight": centred(splits[6], (FF, CH), FF ** -0.5, 0.09375, ((0, 2), (1, 16))),
        "cotangent": heavy_noise(splits[7], (NSEQ, SEQLEN, CH), 1.0, 6.0, ((1, 16), (2, 2)), (1, 2, 16, 2.0)),
    }


def reference(inputs, first_factor, second_factor, gate_scale, gate_bias, in_weight, out_weight, cotangent):
    factor_one = first_factor.astype(jnp.float32)
    factor_two = second_factor.astype(jnp.float32)

    def one_sequence(carry, pair):
        source, upstream = pair
        grid = source.reshape(NB, BS, CH)
        section_one = jnp.einsum("mkn,mnc->mkc", factor_one, grid.astype(jnp.float32)).astype(jnp.bfloat16)
        section_two = jnp.einsum("kjm,mkc->jkc", factor_two, section_one.astype(jnp.float32)).astype(jnp.bfloat16)
        section_two = lax.optimization_barrier(section_two)
        gate = jax.nn.sigmoid(gate_scale * grid.astype(jnp.float32) + gate_bias)
        mixed = (gate * section_two.astype(jnp.float32)).astype(jnp.bfloat16).reshape(SEQLEN, CH)
        pre_act = jnp.dot(mixed, in_weight, preferred_element_type=jnp.float32)
        hidden = jax.nn.silu(pre_act).astype(jnp.bfloat16)
        result = (mixed.astype(jnp.float32) + jnp.dot(hidden, out_weight, preferred_element_type=jnp.float32)).astype(jnp.bfloat16)
        hidden_grad = jnp.dot(upstream, out_weight.T, preferred_element_type=jnp.float32)
        sigma = jax.nn.sigmoid(pre_act)
        pre_grad = (hidden_grad * sigma * (1.0 + pre_act * (1.0 - sigma))).astype(jnp.bfloat16)
        term_out = jnp.dot(hidden.T, upstream, preferred_element_type=jnp.float32)
        term_in = jnp.dot(mixed.T, pre_grad, preferred_element_type=jnp.float32)
        mixed_grad = (upstream.astype(jnp.float32) + jnp.dot(pre_grad, in_weight.T, preferred_element_type=jnp.float32)).astype(jnp.bfloat16)
        grad_grid = mixed_grad.reshape(NB, BS, CH).astype(jnp.float32)
        second_grad = (grad_grid * gate).astype(jnp.bfloat16)
        gate_back = grad_grid * section_two.astype(jnp.float32) * gate * (1.0 - gate) * gate_scale
        first_grad = jnp.einsum("kjm,jkc->mkc", factor_two, second_grad.astype(jnp.float32)).astype(jnp.bfloat16)
        input_grad = (jnp.einsum("mkn,mkc->mnc", factor_one, first_grad.astype(jnp.float32)) + gate_back).astype(jnp.bfloat16)
        return (carry[0] + term_in, carry[1] + term_out), (result, input_grad.reshape(SEQLEN, CH))

    start = (jnp.zeros((CH, FF), jnp.float32), jnp.zeros((FF, CH), jnp.float32))
    (sum_in, sum_out), (result, input_grad) = lax.scan(one_sequence, start, (inputs, cotangent))
    return result, input_grad, sum_in * (1.0 / BS), sum_out * (1.0 / BS)
```

```python
import functools

import jax
import jax.numpy as jnp
from jax import lax
from jax.experimental import pallas as pl
from jax.experimental.pallas import tpu as pltpu
from jax.sharding import PartitionSpec as P

BF = jnp.bfloat16
F32 = jnp.float32


def body(
    inputs, first_factor, second_factor, gate_scale, gate_bias, in_weight, out_weight, cotangent
):
    seq_count, tok_rows, chan = inputs.shape
    blocks, size, _ = first_factor.shape
    offs = second_factor.shape[0]
    owners = lax.axis_size("seq")
    groups = lax.axis_size("fsdp")
    mine = lax.axis_index("fsdp")
    width = chan * groups
    gain = gate_scale.reshape(1, 1, chan)
    shift = gate_bias.reshape(1, 1, chan)

    def swap(x):
        return lax.ppermute(x, "fsdp", [(0, 1), (1, 0)])

    def gather_cols(x):
        if groups != 2:
            return lax.all_gather(x, "fsdp", axis=1, tiled=True)
        return place(x, swap(x))

    def place(x, y):
        first = mine == 0
        return jnp.concatenate([jnp.where(first, x, y), jnp.where(first, y, x)], axis=1)

    def reduce_cols(left, weight, dims):
        if groups != 2:
            full = lax.dot_general(left, weight, dims, preferred_element_type=F32)
            got = lax.all_to_all(full, "fsdp", split_axis=1, concat_axis=0, tiled=True)
            return jnp.sum(got.reshape(groups, -1, chan), axis=0), None
        other = lax.dynamic_slice_in_dim(weight, (1 - mine) * chan, chan, 0)
        own = lax.dynamic_slice_in_dim(weight, mine * chan, chan, 0)
        sent = swap(lax.dot_general(left, other, dims, preferred_element_type=F32).astype(BF))
        kept = lax.dot_general(left, own, dims, preferred_element_type=F32)
        return kept, sent

    def exchange(x):
        return lax.all_to_all(x, "seq", split_axis=0, concat_axis=0, tiled=True)

    bar = lax.optimization_barrier
    nt = (((1,), (1,)), ((), ()))
    tn = (((0,), (0,)), ((), ()))
    seqs = range(seq_count)
    last = seq_count - 1
    both = jnp.stack([in_weight, out_weight.T], axis=0)
    both = lax.all_gather(both, "seq", axis=1, tiled=True)
    full_in, full_out = both[0], both[1]

    sources = [inputs[s].reshape(blocks, size, chan) for s in seqs]
    cots = [cotangent[s] for s in seqs]
    cot_all = [gather_cols(c) for c in cots]

    source = inputs.reshape(seq_count, blocks, size, chan)
    u = jnp.einsum("mkn,smnc->mksc", first_factor, source, preferred_element_type=F32)
    u = u.astype(BF).reshape(blocks, owners, offs, seq_count, chan).transpose(1, 3, 0, 2, 4)
    u, *cot_all = bar((exchange(u), *cot_all))
    turned = [u[:, s].reshape(owners * blocks, offs, chan) for s in seqs]
    mixes, seconds, mixed_all = [], [], []
    for s in seqs:
        w = jnp.einsum("kjm,mkc->kjc", second_factor, turned[s], preferred_element_type=F32)
        w = w.astype(BF).reshape(offs, owners, blocks, chan).transpose(1, 0, 2, 3)
        w = exchange(w)
        if s > 0:
            w, mixed_all[s - 1] = bar((w, mixed_all[s - 1]))
        w = bar(w.reshape(size, blocks, chan).transpose(1, 0, 2))
        gate = jax.nn.sigmoid(gain * sources[s].astype(F32) + shift)
        seconds.append(w)
        mixes.append((gate * w.astype(F32)).astype(BF).reshape(tok_rows, chan))
        if s < last or groups != 2:
            mixed_all.append(gather_cols(mixes[s]))
    swapped = swap(mixes[last]) if groups == 2 else None

    das, hs, sums = [], [], []
    for s in seqs:
        pre = jnp.dot(mixed_all[s], full_in, preferred_element_type=F32)
        dh = jnp.dot(cot_all[s], full_out, preferred_element_type=F32)
        sig = jax.nn.sigmoid(pre)
        hs.append((pre * sig).astype(BF))
        da = (dh * sig * (1.0 + pre * (1.0 - sig))).astype(BF)
        if s < last and groups == 2:
            da, swapped = bar((da, swapped))
            mixed_all.append(place(mixes[last], swapped))
        if s > 0 and groups == 2:
            kept, sent = sums[s - 1]
            da, sent = bar((da, sent))
            sums[s - 1] = kept, sent
        das.append(da)
        sums.append(reduce_cols(da, full_in, nt))

    out_term = sum(lax.dot_general(cot_all[s], hs[s], tn, preferred_element_type=F32) for s in seqs)
    out_term = out_term.astype(BF)
    if groups == 2:
        kept, sent = sums[last]
        sent, out_term = bar((sent, out_term))
        sums[last] = kept, sent
    grad_out = lax.psum_scatter(out_term, "seq", scatter_dimension=0, tiled=True)
    dms, dws, gates = [], [], []
    for s in seqs:
        gate = jax.nn.sigmoid(gain * sources[s].astype(F32) + shift)
        kept, sent = sums[s]
        dm = cots[s].astype(F32) + (kept if sent is None else kept + sent.astype(F32))
        dm = dm.astype(BF).reshape(blocks, size, chan)
        dw = (dm.astype(F32) * gate).astype(BF)
        dms.append(dm)
        gates.append(gate)
        dws.append(dw.reshape(blocks, owners, offs, chan).transpose(1, 0, 2, 3))
    dw = exchange(jnp.stack(dws, axis=1))
    in_term = sum(lax.dot_general(mixed_all[s], das[s], tn, preferred_element_type=F32) for s in seqs)
    dw, in_term = bar((dw, in_term.astype(BF)))
    scale = 1.0 / size
    grad_in = lax.psum_scatter(in_term, "seq", scatter_dimension=0, tiled=True)

    branches = [list(reduce_cols(hs[s], full_out, nt)) for s in seqs]
    dw = dw.transpose(1, 0, 2, 3, 4).reshape(seq_count, owners * blocks, offs, chan)
    du = jnp.einsum("kjm,sjkc->kmsc", second_factor, dw, preferred_element_type=F32)
    du = du.astype(BF).reshape(offs, owners, blocks, seq_count, chan).transpose(1, 3, 0, 2, 4)
    du = exchange(du)
    if groups == 2:
        du, *sents = bar((du, *[pair[1] for pair in branches]))
        branches = [[pair[0], sent] for pair, sent in zip(branches, sents)]
    grads, results = [], []
    for s in seqs:
        rows = du[:, s].reshape(size, blocks, chan)
        back = jnp.einsum("mkn,kmc->mnc", first_factor, rows, preferred_element_type=F32)
        gate = gates[s]
        gate_term = dms[s].astype(F32) * seconds[s].astype(F32) * gate * (1.0 - gate) * gain
        grads.append((back + gate_term).astype(BF).reshape(tok_rows, chan))
        kept, sent = branches[s]
        branch = kept if sent is None else kept + sent.astype(F32)
        results.append((mixes[s].astype(F32) + branch).astype(BF))
    return (
        jnp.stack(results),
        jnp.stack(grads),
        grad_in.astype(F32) * scale,
        grad_out.astype(F32).T * scale,
    )


MESH = pl.DeviceIdType.MESH
NT = (((1,), (1,)), ((), ()))
TN = (((0,), (0,)), ((), ()))
MIB = 1024 * 1024


def mm(a, b, dims=(((1,), (0,)), ((), ()))):
    return lax.dot_general(a, b, dims, preferred_element_type=F32)


def kernel(
    x_in, cot_in, bf_in, m1_in, gain_ref, shift_ref, wi_in, wo_in,
    res_out, ig_out, gi_out, go_out,
    x, bf, bs, wt, ub, uv, wb, wv, cota, mixa, h, da, dms, dmr, dmk, rs, rr, rk, lt,
    ld, a_send, a_recv, y_send, y_recv, w_send, w_recv, g_send, g_recv, o_sem, credit,
):
    me = lax.axis_index("seq")
    mine = lax.axis_index("fsdp")
    oth = 1 - mine
    zc, xc, cc = me // 4, (me // 2) % 2, me % 2
    xpeer = zc * 4 + (1 - xc) * 2 + cc
    cpeer = zc * 4 + xc * 2 + (1 - cc)

    def zpeer(d):
        return ((zc + d) % 4) * 4 + xc * 2 + cc

    def seqdev(i):
        return {"seq": i}

    ydev = {"fsdp": oth}

    def remote(src, dst, ss, rs_, dev):
        return pltpu.make_async_remote_copy(
            src_ref=src, dst_ref=dst, send_sem=ss, recv_sem=rs_, device_id=dev, device_id_type=MESH
        )

    def drain(ref, sem):
        pltpu.make_async_copy(ref, ref, sem).wait()

    loads = [
        pltpu.make_async_copy(cot_in.at[s], cota.at[mine, pl.ds(s * 1024, 1024)], ld.at[s]) for s in range(2)
    ]
    loads += [
        pltpu.make_async_copy(x_in, x, ld.at[2]),
        pltpu.make_async_copy(bf_in, bf, ld.at[3]),
        pltpu.make_async_copy(m1_in, da.at[pl.ds(0, 1024), pl.ds(0, 1024)], ld.at[4]),
        pltpu.make_async_copy(wi_in, wt.at[0, pl.ds(me * 64, 64)], ld.at[5]),
        pltpu.make_async_copy(wo_in, wt.at[1, pl.ds(me * 64, 64)], ld.at[6]),
    ]
    for c in loads:
        c.start()

    barrier = pltpu.get_barrier_semaphore()

    @pl.loop(1, 16)
    def _(d):
        pl.semaphore_signal(barrier, inc=1, device_id=seqdev((me + d) % 16), device_id_type=MESH)

    pl.semaphore_signal(barrier, inc=1, device_id=ydev, device_id_type=MESH)
    pl.semaphore_wait(barrier, 16)

    def yview(ref, q):
        return ref.at[mine, pl.ds(q * 512, 512)]

    def ycopy(kind, q):
        if kind == 0:
            a = b = yview(cota, q)
        elif kind == 1:
            a = b = yview(mixa, q)
        elif kind == 2:
            view = (q // 2, pl.ds((q % 2) * 8, 8))
            a, b = dms.at[view], dmr.at[view]
        else:
            a, b = rs.at[pl.ds(q * 512, 512)], rr.at[pl.ds(q * 512, 512)]
        return remote(a, b, y_send.at[kind, q], y_recv.at[kind, q], ydev)

    pairs = [(ub, uv), (wb, wv), (dms, uv), (wb, ub)]

    def a2a(kind, s):
        src, dst = pairs[kind]
        pltpu.make_async_copy(src.at[s, me], dst.at[s, me], a_recv.at[kind, s]).start()

        @pl.loop(1, 16)
        def _(d):
            e = 16 - d
            peer = ((zc + e // 4) % 4) * 4 + ((xc + (e // 2) % 2) % 2) * 2 + (cc + e % 2) % 2
            remote(src.at[s, peer], dst.at[s, me], a_send.at[kind, s], a_recv.at[kind, s], seqdev(peer)).start()

    def a2a_recv(kind, s):
        drain(pairs[kind][1].at[s], a_recv.at[kind, s])

    def a2a_sent(kind, s):
        drain(pairs[kind][0].at[s, pl.ds(0, 15)], a_send.at[kind, s])

    def gather_z():
        for g in range(2):
            for d in range(1, 4):
                rows = wt.at[g, pl.ds(me * 64, 64)]
                remote(rows, rows, w_send.at[0], w_recv.at[0], seqdev(zpeer(d))).start()

    def gather_x():
        drain(wt.at[0, pl.ds(0, 384)], w_recv.at[0])

        @pl.loop(0, 4)
        def _(i):
            for g in range(2):
                rows = wt.at[g, pl.ds((i * 4 + xc * 2 + cc) * 64, 64)]
                remote(rows, rows, w_send.at[1], w_recv.at[1], seqdev(xpeer)).start()

    def gather_c():
        drain(wt.at[0, pl.ds(0, 512)], w_recv.at[1])

        @pl.loop(0, 8)
        def _(i):
            for g in range(2):
                rows = wt.at[g, pl.ds((i * 2 + cc) * 64, 64)]
                remote(rows, rows, w_send.at[2], w_recv.at[2], seqdev(cpeer)).start()

    def gather_done():
        drain(wt.at[0, pl.ds(0, 1024)], w_recv.at[2])

    gain = gain_ref[...]
    shift = shift_ref[...]

    def big(dst, mat, src, s, dims):
        @pl.loop(0, 4)
        def _(t):
            if dims is TN:
                lhs = mat[:, pl.ds(pl.multiple_of(t * 256, 256), 256)]
            else:
                lhs = mat[pl.ds(pl.multiple_of(t * 256, 256), 256), :]
            out = mm(lhs, src[s].reshape(1024, 512), dims if dims is TN else (((1,), (0,)), ((), ())))
            dst[s, pl.ds(t * 4, 4)] = out.astype(BF).reshape(4, 64, 512)

    def mixer_rows(s, jj):
        w = wv[s, :, pl.ds(pl.multiple_of(jj * 16, 16), 16), :].astype(F32).reshape(16, 2, 8, 512)
        w = jnp.concatenate([w[:, 0].reshape(128, 512), w[:, 1].reshape(128, 512)], axis=0)
        rows = pl.ds(pl.multiple_of(jj * 256, 256), 256)
        gate = jax.nn.sigmoid(gain * x[s, rows, :].astype(F32) + shift)
        return w, gate

    def gate_chunk(q):
        s = q // 2

        @pl.loop((q % 2) * 2, (q % 2) * 2 + 2)
        def _(jj):
            w, gate = mixer_rows(s, jj)
            rows = pl.ds(pl.multiple_of(s * 1024 + jj * 256, 256), 256)
            mixa[mine, rows, :] = (gate * w).astype(BF)

        ycopy(1, q).start()

    def mlp(q):
        rows = pl.ds(q * 512, 512)
        s = q // 2

        @pl.loop(0, 8)
        def _(f):
            cols = pl.ds(pl.multiple_of(f * 256, 256), 256)
            pre = mm(mixa[0, rows, :], wt[0, pl.ds(0, 512), cols]) + mm(mixa[1, rows, :], wt[0, pl.ds(512, 512), cols])
            dh = mm(cota[0, rows, :], wt[1, pl.ds(0, 512), cols]) + mm(cota[1, rows, :], wt[1, pl.ds(512, 512), cols])
            sig = jax.nn.sigmoid(pre)
            h[rows, cols] = (pre * sig).astype(BF)
            da[rows, cols] = (dh * sig * (1.0 + pre * (1.0 - sig))).astype(BF)

        @pl.loop(0, 2)
        def _(n):
            cols = pl.ds(pl.multiple_of(n * 256, 256), 256)
            chans = pl.ds(pl.multiple_of(oth * 512 + n * 256, 256), 256)
            out = mm(da[rows, :], wt[0, chans, :], NT)
            dms[s, pl.ds((q % 2) * 8, 8), :, cols] = out.astype(BF).reshape(8, 64, 256)

        ycopy(2, q).start()

    def own_dm(q):
        rows = pl.ds(q * 512, 512)

        @pl.loop(0, 2)
        def _(n):
            cols = pl.ds(pl.multiple_of(n * 256, 256), 256)
            chans = pl.ds(pl.multiple_of(mine * 512 + n * 256, 256), 256)
            out = mm(da[rows, :], wt[0, chans, :], NT)
            dmk[rows, cols] = (out + cota[mine, rows, cols].astype(F32)).astype(BF)

    def res_send(q):
        rows = pl.ds(q * 512, 512)

        @pl.loop(0, 2)
        def _(n):
            cols = pl.ds(pl.multiple_of(n * 256, 256), 256)
            chans = pl.ds(pl.multiple_of(oth * 512 + n * 256, 256), 256)
            rs[rows, cols] = mm(h[rows, :], wt[1, chans, :], NT).astype(BF)

        ycopy(3, q).start()

    def res_own(q):
        rows = pl.ds(q * 512, 512)

        @pl.loop(0, 2)
        def _(n):
            cols = pl.ds(pl.multiple_of(n * 256, 256), 256)
            chans = pl.ds(pl.multiple_of(mine * 512 + n * 256, 256), 256)
            out = mm(h[rows, :], wt[1, chans, :], NT)
            rk[rows, cols] = (out + mixa[mine, rows, cols].astype(F32)).astype(BF)

    def finish_dm(s):
        a2a_sent(0, s)
        for q in (2 * s, 2 * s + 1):
            ycopy(2, q).wait()

        @pl.loop(0, 4)
        def _(jj):
            w, gate = mixer_rows(s, jj)
            rows = pl.ds(pl.multiple_of(s * 1024 + jj * 256, 256), 256)
            slab = pl.ds(jj * 4, 4)
            dm = dmk[rows, :].astype(F32) + dmr[s, slab].astype(F32).reshape(256, 512)
            dm = dm.astype(BF)
            dmr[s, slab] = dm.reshape(4, 64, 512)
            dw = (dm.astype(F32) * gate).reshape(2, 16, 8, 512)
            dw = jnp.concatenate([dw[0], dw[1]], axis=1)
            dms[s, :, pl.ds(pl.multiple_of(jj * 16, 16), 16), :] = dw.astype(BF)

        a2a(2, s)

    def finish_grad(s):
        @pl.loop(0, 4)
        def _(jj):
            w, gate = mixer_rows(s, jj)
            slab = pl.ds(jj * 4, 4)
            dm = dmr[s, slab].astype(F32).reshape(256, 512)
            term = dm * w * gate * (1.0 - gate) * gain
            cols = pl.ds(pl.multiple_of(jj * 256, 256), 256)
            out = mm(bf[:, cols], ub[s].reshape(1024, 512), TN)
            uv[s, slab] = (out + term).astype(BF).reshape(4, 64, 512)

        return pltpu.make_async_copy(uv.at[s], ig_out.at[s], o_sem.at[s])

    def finish_res(s):
        for q in (2 * s, 2 * s + 1):
            ycopy(3, q).wait()

        @pl.loop(0, 4)
        def _(jj):
            rows = pl.ds(pl.multiple_of(s * 1024 + jj * 256, 256), 256)
            rk[rows, :] = (rk[rows, :].astype(F32) + rr[rows, :].astype(F32)).astype(BF)

        return pltpu.make_async_copy(rk.at[pl.ds(s * 1024, 1024)], res_out.at[s], o_sem.at[2 + s])

    def weight_grad(g):
        src, rhs = (mixa, da) if g == 0 else (cota, h)
        for t in range(4):
            @pl.loop(0, 8)
            def _(i):
                rows = pl.ds(pl.multiple_of(i * 256, 256), 256)
                lt[:, rows] = src[t // 2, rows, pl.ds((t % 2) * 256, 256)].T

            @pl.loop(0, 4)
            def _(f):
                cols = pl.ds(pl.multiple_of(f * 512, 512), 512)
                out = mm(lt[...], rhs[:, cols]).astype(BF)
                for xi in range(2):
                    for ci in range(2):
                        at = (2 * xi + ci) * 64
                        wt[g, pl.ds(ci * 512 + xi * 256 + t * 64, 64), cols] = out[at : at + 64]

    def add_rows(g, base, off, count):
        @pl.loop(0, count)
        def _(i):
            rows = pl.ds(pl.multiple_of(base + i * 64, 64), 64)
            more = h[pl.ds(pl.multiple_of(off + i * 64, 64), 64), :].astype(F32)
            wt[g, rows, :] = (wt[g, rows, :].astype(F32) + more).astype(BF)

    def scatter_c(g):
        return remote(
            wt.at[g, pl.ds((1 - cc) * 512, 512)], h.at[pl.ds(g * 512, 512)],
            g_send.at[0, g], g_recv.at[0, g], seqdev(cpeer),
        )

    def scatter_x(g):
        return remote(
            wt.at[g, pl.ds(cc * 512 + (1 - xc) * 256, 256)], h.at[pl.ds(1024 + g * 256, 256)],
            g_send.at[1, g], g_recv.at[1, g], seqdev(xpeer),
        )

    def scatter_z(g):
        for d in range(1, 4):
            row = cc * 512 + xc * 256 + ((zc + d) % 4) * 64
            remote(
                wt.at[g, pl.ds(row, 64)], h.at[pl.ds(1536 + g * 256 + zc * 64, 64)],
                g_send.at[2, g], g_recv.at[2, g], seqdev(zpeer(d)),
            ).start()

    def scatter_end(g):
        drain(h.at[pl.ds(0, 192)], g_recv.at[2, g])
        out = gi_out if g == 0 else go_out
        total = wt[g, pl.ds(pl.multiple_of(cc * 512 + xc * 256 + zc * 64, 64), 64), :].astype(F32)
        for d in range(1, 4):
            slot = 1536 + g * 256 + ((zc + d) % 4) * 64
            total = total + h[pl.ds(pl.multiple_of(slot, 64), 64), :].astype(F32)
        out[...] = total * (1.0 / 128)

    loads[0].wait()
    loads[1].wait()
    for q in range(4):
        ycopy(0, q).start()
    loads[2].wait()
    loads[3].wait()
    plain = (((1,), (0,)), ((), ()))

    def first(s):
        @pl.loop(0, 4)
        def _(t):
            out = mm(bf[pl.ds(pl.multiple_of(t * 256, 256), 256), :], x[s])
            ub[s, pl.ds(t * 4, 4)] = out.astype(BF).reshape(4, 64, 512)

    first(0)
    a2a(0, 0)
    loads[5].wait()
    loads[6].wait()
    gather_z()
    first(1)
    a2a(0, 1)
    loads[4].wait()

    @pl.loop(0, 4)
    def _(t):
        row = lax.broadcasted_iota(jnp.int32, (1024, 256), 0)
        col = lax.broadcasted_iota(jnp.int32, (1024, 256), 1) + t * 256
        want = ((col // 8) % 8) * 128 + (col // 64) * 8 + col % 8
        pick = jnp.where(row == want, 1.0, 0.0).astype(BF)
        for r in range(2):
            rows = pl.ds(r * 512, 512)
            bs[rows, pl.ds(pl.multiple_of(t * 256, 256), 256)] = mm(da[rows, pl.ds(0, 1024)], pick).astype(BF)

    a2a_recv(0, 0)
    big(wb, bs, uv, 0, plain)
    a2a(1, 0)
    gather_x()
    a2a_recv(0, 1)
    big(wb, bs, uv, 1, plain)
    a2a(1, 1)
    gather_c()
    a2a_recv(1, 0)
    gate_chunk(0)
    gate_chunk(1)
    for q in range(4):
        ycopy(0, q).wait()
    gather_done()
    ycopy(1, 0).wait()
    mlp(0)
    a2a_recv(1, 1)
    gate_chunk(2)
    gate_chunk(3)
    own_dm(0)
    ycopy(1, 1).wait()
    mlp(1)
    own_dm(1)
    ycopy(1, 2).wait()
    mlp(2)
    own_dm(2)
    finish_dm(0)
    ycopy(1, 3).wait()
    mlp(3)
    own_dm(3)
    res_send(0)
    res_send(1)
    a2a_recv(2, 0)
    a2a_sent(1, 0)
    big(wb, bs, uv, 0, TN)
    a2a(3, 0)
    finish_dm(1)
    res_send(2)
    res_send(3)
    for q in range(4):
        res_own(q)
    for k in range(3):
        rows = (384, 512, 1024)[k]
        drain(wt.at[0, pl.ds(0, rows)], w_send.at[k])
    weight_grad(1)
    for d in range(1, 4):
        pl.semaphore_signal(credit, inc=1, device_id=seqdev(zpeer(d)), device_id_type=MESH)
    for peer in (xpeer, cpeer):
        pl.semaphore_signal(credit, inc=1, device_id=seqdev(peer), device_id_type=MESH)
    pl.semaphore_wait(credit, 5)
    scatter_c(1).start()
    a2a_recv(2, 1)
    a2a_sent(1, 1)
    big(wb, bs, uv, 1, TN)
    a2a(3, 1)
    scatter_c(1).wait()
    add_rows(1, cc * 512, 512, 8)
    scatter_x(1).start()
    weight_grad(0)
    scatter_c(0).start()
    scatter_x(1).wait()
    add_rows(1, cc * 512 + xc * 256, 1280, 4)
    scatter_z(1)
    scatter_c(0).wait()
    add_rows(0, cc * 512, 0, 8)
    scatter_x(0).start()
    scatter_x(0).wait()
    add_rows(0, cc * 512 + xc * 256, 1024, 4)
    scatter_z(0)
    a2a_recv(3, 0)
    outs = [finish_grad(0)]
    outs[0].start()
    for s in range(2):
        outs.append(finish_res(s))
        outs[-1].start()
    scatter_end(1)
    scatter_end(0)
    a2a_recv(3, 1)
    outs.append(finish_grad(1))
    outs[-1].start()
    for g in range(2):
        drain(wt.at[0, pl.ds(0, 192)], g_send.at[2, g])
    for kind in (2, 3):
        for s in range(2):
            a2a_sent(kind, s)
    for c in outs:
        c.wait()


def fused(
    inputs, first_factor, second_factor, gate_scale, gate_bias, in_weight, out_weight, cotangent
):
    count, rows, chan = inputs.shape
    hidden = in_weight.shape[1]
    eye = jnp.eye(8, dtype=bool)[None, :, :, None]

    def spread(f):
        return jnp.where(eye, f.transpose(1, 0, 2)[:, None], jnp.zeros((), BF)).reshape(1024, 1024)

    anyspace = pl.BlockSpec(memory_space=pl.ANY)
    vmem = pl.BlockSpec(memory_space=pltpu.VMEM)
    cells = (2, 16, 64, 512)
    dma = pltpu.SemaphoreType.DMA
    buf = pltpu.VMEM
    act = jax.ShapeDtypeStruct(inputs.shape, BF)
    res, ig, gi, go = pl.pallas_call(
        kernel,
        out_shape=(
            jax.ShapeDtypeStruct((2, 1024, 512), BF),
            jax.ShapeDtypeStruct(cells, BF),
            jax.ShapeDtypeStruct((64, hidden), F32),
            jax.ShapeDtypeStruct((64, hidden), F32),
        ),
        in_specs=[anyspace] * 4 + [vmem] * 2 + [anyspace] * 2,
        out_specs=(anyspace, anyspace, vmem, vmem),
        scratch_shapes=[
            buf((2, 1024, 512), BF),
            buf((1024, 1024), BF),
            buf((1024, 1024), BF),
            buf((2, 1024, 2048), BF),
            buf(cells, BF),
            buf(cells, BF),
            buf(cells, BF),
            buf(cells, BF),
            buf((2, 2048, 512), BF),
            buf((2, 2048, 512), BF),
            buf((2048, 2048), BF),
            buf((2048, 2048), BF),
            buf(cells, BF),
            buf(cells, BF),
            buf((2048, 512), BF),
            buf((2048, 512), BF),
            buf((2048, 512), BF),
            buf((2048, 512), BF),
            buf((256, 2048), BF),
            dma((7,)),
            dma((4, 2)),
            dma((4, 2)),
            dma((4, 4)),
            dma((4, 4)),
            dma((3,)),
            dma((3,)),
            dma((3, 2)),
            dma((3, 2)),
            dma((4,)),
            pltpu.SemaphoreType.REGULAR,
        ],
        compiler_params=pltpu.CompilerParams(
            collective_id=0, has_side_effects=True, vmem_limit_bytes=63 * MIB
        ),
        cost_estimate=pl.CostEstimate(flops=60 * 10**9, bytes_accessed=20 * MIB, transcendentals=0),
    )(
        inputs,
        cotangent,
        spread(first_factor),
        spread(second_factor),
        gate_scale.reshape(1, chan),
        gate_bias.reshape(1, chan),
        in_weight,
        out_weight.T,
    )
    return res, ig.reshape(inputs.shape), gi, go.T


def solution(mesh):
    in_specs = (
        P(None, "seq", "fsdp"),
        P("seq", None, None),
        P("seq", None, None),
        P("fsdp"),
        P("fsdp"),
        P("seq", "fsdp"),
        P("fsdp", "seq"),
        P(None, "seq", "fsdp"),
    )
    out_specs = (P(None, "seq", "fsdp"), P(None, "seq", "fsdp"), P("seq", "fsdp"), P("fsdp", "seq"))
    sizes = (mesh.shape["seq"], mesh.shape["fsdp"])
    part = fused if sizes == (16, 2) else body
    return jax.shard_map(part, mesh=mesh, in_specs=in_specs, out_specs=out_specs, check_vma=False)
```

```python
import functools

import jax
import jax.numpy as jnp
from jax import lax
from jax.experimental import pallas as pl
from jax.experimental.pallas import tpu as pltpu
from jax.sharding import PartitionSpec as P

BF = jnp.bfloat16
F32 = jnp.float32


def body(
    inputs, first_factor, second_factor, gate_scale, gate_bias, in_weight, out_weight, cotangent
):
    seq_count, tok_rows, chan = inputs.shape
    blocks, size, _ = first_factor.shape
    offs = second_factor.shape[0]
    owners = lax.axis_size("seq")
    groups = lax.axis_size("fsdp")
    mine = lax.axis_index("fsdp")
    width = chan * groups
    gain = gate_scale.reshape(1, 1, chan)
    shift = gate_bias.reshape(1, 1, chan)

    def swap(x):
        return lax.ppermute(x, "fsdp", [(0, 1), (1, 0)])

    def gather_cols(x):
        if groups != 2:
            return lax.all_gather(x, "fsdp", axis=1, tiled=True)
        return place(x, swap(x))

    def place(x, y):
        first = mine == 0
        return jnp.concatenate([jnp.where(first, x, y), jnp.where(first, y, x)], axis=1)

    def reduce_cols(left, weight, dims):
        if groups != 2:
            full = lax.dot_general(left, weight, dims, preferred_element_type=F32)
            got = lax.all_to_all(full, "fsdp", split_axis=1, concat_axis=0, tiled=True)
            return jnp.sum(got.reshape(groups, -1, chan), axis=0), None
        other = lax.dynamic_slice_in_dim(weight, (1 - mine) * chan, chan, 0)
        own = lax.dynamic_slice_in_dim(weight, mine * chan, chan, 0)
        sent = swap(lax.dot_general(left, other, dims, preferred_element_type=F32).astype(BF))
        kept = lax.dot_general(left, own, dims, preferred_element_type=F32)
        return kept, sent

    def exchange(x):
        return lax.all_to_all(x, "seq", split_axis=0, concat_axis=0, tiled=True)

    bar = lax.optimization_barrier
    nt = (((1,), (1,)), ((), ()))
    tn = (((0,), (0,)), ((), ()))
    seqs = range(seq_count)
    last = seq_count - 1
    both = jnp.stack([in_weight, out_weight.T], axis=0)
    both = lax.all_gather(both, "seq", axis=1, tiled=True)
    full_in, full_out = both[0], both[1]

    sources = [inputs[s].reshape(blocks, size, chan) for s in seqs]
    cots = [cotangent[s] for s in seqs]
    cot_all = [gather_cols(c) for c in cots]

    source = inputs.reshape(seq_count, blocks, size, chan)
    u = jnp.einsum("mkn,smnc->mksc", first_factor, source, preferred_element_type=F32)
    u = u.astype(BF).reshape(blocks, owners, offs, seq_count, chan).transpose(1, 3, 0, 2, 4)
    u, *cot_all = bar((exchange(u), *cot_all))
    turned = [u[:, s].reshape(owners * blocks, offs, chan) for s in seqs]
    mixes, seconds, mixed_all = [], [], []
    for s in seqs:
        w = jnp.einsum("kjm,mkc->kjc", second_factor, turned[s], preferred_element_type=F32)
        w = w.astype(BF).reshape(offs, owners, blocks, chan).transpose(1, 0, 2, 3)
        w = exchange(w)
        if s > 0:
            w, mixed_all[s - 1] = bar((w, mixed_all[s - 1]))
        w = bar(w.reshape(size, blocks, chan).transpose(1, 0, 2))
        gate = jax.nn.sigmoid(gain * sources[s].astype(F32) + shift)
        seconds.append(w)
        mixes.append((gate * w.astype(F32)).astype(BF).reshape(tok_rows, chan))
        if s < last or groups != 2:
            mixed_all.append(gather_cols(mixes[s]))
    swapped = swap(mixes[last]) if groups == 2 else None

    das, hs, sums = [], [], []
    for s in seqs:
        pre = jnp.dot(mixed_all[s], full_in, preferred_element_type=F32)
        dh = jnp.dot(cot_all[s], full_out, preferred_element_type=F32)
        sig = jax.nn.sigmoid(pre)
        hs.append((pre * sig).astype(BF))
        da = (dh * sig * (1.0 + pre * (1.0 - sig))).astype(BF)
        if s < last and groups == 2:
            da, swapped = bar((da, swapped))
            mixed_all.append(place(mixes[last], swapped))
        if s > 0 and groups == 2:
            kept, sent = sums[s - 1]
            da, sent = bar((da, sent))
            sums[s - 1] = kept, sent
        das.append(da)
        sums.append(reduce_cols(da, full_in, nt))

    out_term = sum(lax.dot_general(cot_all[s], hs[s], tn, preferred_element_type=F32) for s in seqs)
    out_term = out_term.astype(BF)
    if groups == 2:
        kept, sent = sums[last]
        sent, out_term = bar((sent, out_term))
        sums[last] = kept, sent
    grad_out = lax.psum_scatter(out_term, "seq", scatter_dimension=0, tiled=True)
    dms, dws, gates = [], [], []
    for s in seqs:
        gate = jax.nn.sigmoid(gain * sources[s].astype(F32) + shift)
        kept, sent = sums[s]
        dm = cots[s].astype(F32) + (kept if sent is None else kept + sent.astype(F32))
        dm = dm.astype(BF).reshape(blocks, size, chan)
        dw = (dm.astype(F32) * gate).astype(BF)
        dms.append(dm)
        gates.append(gate)
        dws.append(dw.reshape(blocks, owners, offs, chan).transpose(1, 0, 2, 3))
    dw = exchange(jnp.stack(dws, axis=1))
    in_term = sum(lax.dot_general(mixed_all[s], das[s], tn, preferred_element_type=F32) for s in seqs)
    dw, in_term = bar((dw, in_term.astype(BF)))
    scale = 1.0 / size
    grad_in = lax.psum_scatter(in_term, "seq", scatter_dimension=0, tiled=True)

    branches = [list(reduce_cols(hs[s], full_out, nt)) for s in seqs]
    dw = dw.transpose(1, 0, 2, 3, 4).reshape(seq_count, owners * blocks, offs, chan)
    du = jnp.einsum("kjm,sjkc->kmsc", second_factor, dw, preferred_element_type=F32)
    du = du.astype(BF).reshape(offs, owners, blocks, seq_count, chan).transpose(1, 3, 0, 2, 4)
    du = exchange(du)
    if groups == 2:
        du, *sents = bar((du, *[pair[1] for pair in branches]))
        branches = [[pair[0], sent] for pair, sent in zip(branches, sents)]
    grads, results = [], []
    for s in seqs:
        rows = du[:, s].reshape(size, blocks, chan)
        back = jnp.einsum("mkn,kmc->mnc", first_factor, rows, preferred_element_type=F32)
        gate = gates[s]
        gate_term = dms[s].astype(F32) * seconds[s].astype(F32) * gate * (1.0 - gate) * gain
        grads.append((back + gate_term).astype(BF).reshape(tok_rows, chan))
        kept, sent = branches[s]
        branch = kept if sent is None else kept + sent.astype(F32)
        results.append((mixes[s].astype(F32) + branch).astype(BF))
    return (
        jnp.stack(results),
        jnp.stack(grads),
        grad_in.astype(F32) * scale,
        grad_out.astype(F32).T * scale,
    )


MESH = pl.DeviceIdType.MESH
NT = (((1,), (1,)), ((), ()))
TN = (((0,), (0,)), ((), ()))
MIB = 1024 * 1024


def mm(a, b, dims=(((1,), (0,)), ((), ()))):
    return lax.dot_general(a, b, dims, preferred_element_type=F32)


def kernel(
    x_in, cot_in, f_in, s_in, gain_ref, shift_ref, wi_in, wo_in,
    res_out, ig_out, gi_out, go_out,
    x, ff, sf, bf, bs, wt, ub, uv, wb, wv, cota, mixa, h, da, dms, dmr, dmk, rs, rr, rk, lt,
    ld, a_send, a_recv, y_send, y_recv, w_send, w_recv, g_send, g_recv, o_sem, credit,
):
    me = lax.axis_index("seq")
    mine = lax.axis_index("fsdp")
    oth = 1 - mine
    zc, xc, cc = me // 4, (me // 2) % 2, me % 2
    xpeer = zc * 4 + (1 - xc) * 2 + cc
    cpeer = zc * 4 + xc * 2 + (1 - cc)

    odd, high = zc % 2, zc // 2
    znear = (zc + 1 - 2 * odd) * 4 + xc * 2 + cc
    zfar = ((zc + 2) % 4) * 4 + xc * 2 + cc

    def seqdev(i):
        return {"seq": i}

    ydev = {"fsdp": oth}

    def remote(src, dst, ss, rs_, dev):
        return pltpu.make_async_remote_copy(
            src_ref=src, dst_ref=dst, send_sem=ss, recv_sem=rs_, device_id=dev, device_id_type=MESH
        )

    def drain(ref, sem):
        pltpu.make_async_copy(ref, ref, sem).wait()

    loads = [
        pltpu.make_async_copy(x_in.at[0], x.at[0], ld.at[0]),
        pltpu.make_async_copy(f_in, ff, ld.at[1]),
        pltpu.make_async_copy(x_in.at[1], x.at[1], ld.at[2]),
        pltpu.make_async_copy(wi_in, wt.at[0, pl.ds(me * 64, 64)], ld.at[3]),
        pltpu.make_async_copy(wo_in, wt.at[1, pl.ds(me * 64, 64)], ld.at[4]),
        pltpu.make_async_copy(cot_in.at[0], cota.at[mine, pl.ds(0, 1024)], ld.at[5]),
        pltpu.make_async_copy(cot_in.at[1], cota.at[mine, pl.ds(1024, 1024)], ld.at[6]),
        pltpu.make_async_copy(s_in, sf, ld.at[7]),
    ]
    barrier = pltpu.get_barrier_semaphore()

    @pl.loop(1, 16)
    def _(d):
        pl.semaphore_signal(barrier, inc=1, device_id=seqdev((me + d) % 16), device_id_type=MESH)

    pl.semaphore_signal(barrier, inc=1, device_id=ydev, device_id_type=MESH)
    for c in loads:
        c.start()

    def yview(ref, q):
        return ref.at[mine, pl.ds(q * 512, 512)]

    def ycopy(kind, q):
        if kind == 0:
            a = b = yview(cota, q)
        elif kind == 1:
            a = b = yview(mixa, q)
        elif kind == 2:
            view = (q // 2, pl.ds((q % 2) * 8, 8))
            a, b = dms.at[view], dmr.at[view]
        else:
            a, b = rs.at[pl.ds(q * 512, 512)], rr.at[pl.ds(q * 512, 512)]
        return remote(a, b, y_send.at[kind, q], y_recv.at[kind, q], ydev)

    pairs = [(ub, uv), (wb, wv), (dms, uv), (wb, ub)]

    def a2a(kind, s):
        src, dst = pairs[kind]
        pltpu.make_async_copy(src.at[s, me], dst.at[s, me], a_recv.at[kind, s]).start()

        @pl.loop(1, 16)
        def _(d):
            e = 16 - d
            peer = ((zc + e // 4) % 4) * 4 + ((xc + (e // 2) % 2) % 2) * 2 + (cc + e % 2) % 2
            remote(src.at[s, peer], dst.at[s, me], a_send.at[kind, s], a_recv.at[kind, s], seqdev(peer)).start()

    def a2a_recv(kind, s):
        drain(pairs[kind][1].at[s], a_recv.at[kind, s])

    def a2a_sent(kind, s):
        drain(pairs[kind][0].at[s, pl.ds(0, 15)], a_send.at[kind, s])

    FAR, NEAR, ACROSS, CORE = range(4)
    peers = (zfar, znear, xpeer, cpeer)

    def shard(g, owner, stages):
        rows = wt.at[g, pl.ds(owner * 64, 64)]
        for k in stages:
            remote(rows, rows, w_send.at[k, g], w_recv.at[k, g], seqdev(peers[k])).start()

    def gathered(g, k):
        count = ((64, 256, 128, 512), (64, 128, 256, 512))[g][k]
        drain(wt.at[0, pl.ds(0, count)], w_recv.at[k, g])

    def gather_own():
        for g in range(2):
            shard(g, me, (FAR, NEAR, ACROSS, CORE))

    def gather_far():
        for g in range(2):
            gathered(g, FAR)
            shard(g, zfar, (NEAR, ACROSS, CORE))

    def gather_mid():
        gathered(1, NEAR)
        gathered(0, ACROSS)
        shard(1, znear, (ACROSS, CORE))
        shard(0, xpeer, (NEAR, CORE))
        shard(1, (znear + 8) % 16, (ACROSS, CORE))
        shard(0, (xpeer + 8) % 16, (NEAR, CORE))

    def gather_last():
        gathered(1, ACROSS)

        @pl.loop(0, 4)
        def _(i):
            shard(1, i * 4 + (1 - xc) * 2 + cc, (CORE,))

        gathered(0, NEAR)

        @pl.loop(0, 2)
        def _(i):
            row = (znear // 4 + 2 * i) % 4 * 4 + cc
            shard(0, row, (CORE,))
            shard(0, row + 2, (CORE,))

    def gather_done():
        for g in range(2):
            gathered(g, CORE)

    gain = gain_ref[...]
    shift = shift_ref[...]

    def big(dst, mat, src, s, dims):
        @pl.loop(0, 4)
        def _(t):
            if dims is TN:
                lhs = mat[:, pl.ds(pl.multiple_of(t * 256, 256), 256)]
            else:
                lhs = mat[pl.ds(pl.multiple_of(t * 256, 256), 256), :]
            out = mm(lhs, src[s].reshape(1024, 512), dims if dims is TN else (((1,), (0,)), ((), ())))
            dst[s, pl.ds(t * 4, 4)] = out.astype(BF).reshape(4, 64, 512)

    def mixer_rows(s, jj):
        w = wv[s, :, pl.ds(pl.multiple_of(jj * 16, 16), 16), :].astype(F32).reshape(16, 2, 8, 512)
        w = jnp.concatenate([w[:, 0].reshape(128, 512), w[:, 1].reshape(128, 512)], axis=0)
        rows = pl.ds(pl.multiple_of(jj * 256, 256), 256)
        gate = jax.nn.sigmoid(gain * x[s, rows, :].astype(F32) + shift)
        return w, gate

    def gate_chunk(q):
        s = q // 2

        @pl.loop((q % 2) * 2, (q % 2) * 2 + 2)
        def _(jj):
            w, gate = mixer_rows(s, jj)
            rows = pl.ds(pl.multiple_of(s * 1024 + jj * 256, 256), 256)
            mixa[mine, rows, :] = (gate * w).astype(BF)

        ycopy(1, q).start()

    def mlp(q):
        rows = pl.ds(q * 512, 512)
        s = q // 2

        @pl.loop(0, 8)
        def _(f):
            cols = pl.ds(pl.multiple_of(f * 256, 256), 256)
            pre = mm(mixa[0, rows, :], wt[0, pl.ds(0, 512), cols]) + mm(mixa[1, rows, :], wt[0, pl.ds(512, 512), cols])
            dh = mm(cota[0, rows, :], wt[1, pl.ds(0, 512), cols]) + mm(cota[1, rows, :], wt[1, pl.ds(512, 512), cols])
            sig = jax.nn.sigmoid(pre)
            h[rows, cols] = (pre * sig).astype(BF)
            da[rows, cols] = (dh * sig * (1.0 + pre * (1.0 - sig))).astype(BF)

        @pl.loop(0, 2)
        def _(n):
            cols = pl.ds(pl.multiple_of(n * 256, 256), 256)
            chans = pl.ds(pl.multiple_of(oth * 512 + n * 256, 256), 256)
            out = mm(da[rows, :], wt[0, chans, :], NT)
            dms[s, pl.ds((q % 2) * 8, 8), :, cols] = out.astype(BF).reshape(8, 64, 256)

        ycopy(2, q).start()

    def own_dm(q):
        rows = pl.ds(q * 512, 512)

        @pl.loop(0, 2)
        def _(n):
            cols = pl.ds(pl.multiple_of(n * 256, 256), 256)
            chans = pl.ds(pl.multiple_of(mine * 512 + n * 256, 256), 256)
            out = mm(da[rows, :], wt[0, chans, :], NT)
            dmk[rows, cols] = (out + cota[mine, rows, cols].astype(F32)).astype(BF)

    def res_part(q):
        rows = pl.ds(q * 512, 512)

        @pl.loop(0, 2)
        def _(n):
            cols = pl.ds(pl.multiple_of(n * 256, 256), 256)
            chans = pl.ds(pl.multiple_of(oth * 512 + n * 256, 256), 256)
            rs[rows, cols] = mm(h[rows, :], wt[1, chans, :], NT).astype(BF)

    def res_own(q):
        rows = pl.ds(q * 512, 512)

        @pl.loop(0, 2)
        def _(n):
            cols = pl.ds(pl.multiple_of(n * 256, 256), 256)
            chans = pl.ds(pl.multiple_of(mine * 512 + n * 256, 256), 256)
            out = mm(h[rows, :], wt[1, chans, :], NT)
            rk[rows, cols] = (out + mixa[mine, rows, cols].astype(F32)).astype(BF)

    def finish_dm(s):
        a2a_sent(0, s)
        for q in (2 * s, 2 * s + 1):
            ycopy(2, q).wait()

        @pl.loop(0, 4)
        def _(jj):
            w, gate = mixer_rows(s, jj)
            rows = pl.ds(pl.multiple_of(s * 1024 + jj * 256, 256), 256)
            slab = pl.ds(jj * 4, 4)
            dm = dmk[rows, :].astype(F32) + dmr[s, slab].astype(F32).reshape(256, 512)
            dm = dm.astype(BF)
            dmr[s, slab] = dm.reshape(4, 64, 512)
            dw = (dm.astype(F32) * gate).reshape(2, 16, 8, 512)
            dw = jnp.concatenate([dw[0], dw[1]], axis=1)
            dms[s, :, pl.ds(pl.multiple_of(jj * 16, 16), 16), :] = dw.astype(BF)

        a2a(2, s)

    def finish_grad(s):
        @pl.loop(0, 4)
        def _(jj):
            w, gate = mixer_rows(s, jj)
            slab = pl.ds(jj * 4, 4)
            dm = dmr[s, slab].astype(F32).reshape(256, 512)
            term = dm * w * gate * (1.0 - gate) * gain
            cols = pl.ds(pl.multiple_of(jj * 256, 256), 256)
            out = mm(bf[:, cols], ub[s].reshape(1024, 512), TN)
            uv[s, slab] = (out + term).astype(BF).reshape(4, 64, 512)

        return pltpu.make_async_copy(uv.at[s], ig_out.at[s], o_sem.at[s])

    def finish_res(s):
        for q in (2 * s, 2 * s + 1):
            ycopy(3, q).wait()

        @pl.loop(0, 4)
        def _(jj):
            rows = pl.ds(pl.multiple_of(s * 1024 + jj * 256, 256), 256)
            rk[rows, :] = (rk[rows, :].astype(F32) + rr[rows, :].astype(F32)).astype(BF)

        return pltpu.make_async_copy(rk.at[pl.ds(s * 1024, 1024)], res_out.at[s], o_sem.at[2 + s])

    def weight_grad(g, ts):
        src, rhs = (mixa, da) if g == 0 else (cota, h)
        for t in ts:
            @pl.loop(0, 8)
            def _(i):
                rows = pl.ds(pl.multiple_of(i * 256, 256), 256)
                lt[:, rows] = src[t // 2, rows, pl.ds((t % 2) * 256, 256)].T

            @pl.loop(0, 4)
            def _(f):
                cols = pl.ds(pl.multiple_of(f * 512, 512), 512)
                out = mm(lt[...], rhs[:, cols]).astype(BF)
                for xi in range(2):
                    for ci in range(2):
                        at = (2 * xi + ci) * 64
                        one, two = (t % 2, xi) if g == 0 else (xi, t % 2)
                        slot = ci * 512 + one * 256 + two * 128 + (t // 2) * 64
                        wt[g, pl.ds(slot, 64), cols] = out[at : at + 64]

    def add_rows(g, base, off, count):
        @pl.loop(0, count)
        def _(i):
            rows = pl.ds(pl.multiple_of(base + i * 64, 64), 64)
            more = h[pl.ds(pl.multiple_of(off + i * 64, 64), 64), :].astype(F32)
            wt[g, rows, :] = (wt[g, rows, :].astype(F32) + more).astype(BF)

    def halving(g, step):
        bits = (cc, xc, odd, high) if g else (cc, odd, xc, high)
        partner = (cpeer, xpeer, znear, zfar) if g else (cpeer, znear, xpeer, zfar)
        size = 512 >> step
        keep = 0
        for k in range(step):
            keep = keep + bits[k] * (512 >> k)
        send = keep + (1 - bits[step]) * size
        keep = keep + bits[step] * size
        land = 2048 - (2048 >> step) + g * size
        copy = remote(
            wt.at[g, pl.ds(send, size)], h.at[pl.ds(land, size)],
            g_send.at[step, g], g_recv.at[step, g], seqdev(partner[step]),
        )
        return copy, keep, land, size

    def scatter_step(g, step):
        if step > 0:
            copy, keep, land, size = halving(g, step - 1)
            copy.wait()
            if step < 4:
                add_rows(g, keep, land, size // 64)
            else:
                out = gi_out if g == 0 else go_out
                own = wt[g, pl.ds(pl.multiple_of(keep, 64), 64), :].astype(F32)
                out[...] = (own + h[pl.ds(land, 64), :].astype(F32)) * (1.0 / 128)
        if step < 4:
            halving(g, step)[0].start()

    plain = (((1,), (0,)), ((), ()))

    def build_pick():
        @pl.loop(0, 4)
        def _(t):
            row = lax.broadcasted_iota(jnp.int32, (256, 1024), 0) + t * 256
            col = lax.broadcasted_iota(jnp.int32, (256, 1024), 1)
            want = (row & 7) * 128 + (row >> 3)
            rows = pl.ds(pl.multiple_of(1024 + t * 256, 256), 256)
            da[rows, pl.ds(0, 1024)] = jnp.where(col == want, 1.0, 0.0).astype(BF)

    def pick_rows(t):
        return da[pl.ds(pl.multiple_of(1024 + t * 256, 256), 256), pl.ds(0, 1024)]

    def first(s):
        for m in range(8):
            rows = pl.ds(m * 128, 128)
            h[rows, pl.ds(0, 512)] = mm(ff[m], x[s, rows, :]).astype(BF)

        @pl.loop(0, 4)
        def _(t):
            out = mm(pick_rows(t), h[pl.ds(0, 1024), pl.ds(0, 512)])
            ub[s, pl.ds(t * 4, 4)] = out.astype(BF).reshape(4, 64, 512)

    def build_second():
        for fac, rows in ((ff, 0), (sf, 1024)):
            da[pl.ds(rows, 1024), pl.ds(1024, 1024)] = jnp.zeros((1024, 1024), BF)
            for m in range(8):
                da[pl.ds(rows + m * 128, 128), pl.ds(1024 + m * 128, 128)] = fac[m]

        @pl.loop(0, 4)
        def _(t):
            rows = pl.ds(pl.multiple_of(t * 256, 256), 256)
            bf[rows, :] = mm(pick_rows(t), da[pl.ds(0, 1024), pl.ds(1024, 1024)]).astype(BF)
            h[rows, pl.ds(1024, 1024)] = mm(pick_rows(t), da[pl.ds(1024, 1024), pl.ds(1024, 1024)]).astype(BF)

        @pl.loop(0, 4)
        def _(t):
            row = lax.broadcasted_iota(jnp.int32, (1024, 256), 0)
            col = lax.broadcasted_iota(jnp.int32, (1024, 256), 1) + t * 256
            want = ((col >> 3) & 7) * 128 + (col >> 6) * 8 + (col & 7)
            pick = jnp.where(row == want, 1.0, 0.0).astype(BF)
            cols = pl.ds(pl.multiple_of(t * 256, 256), 256)
            for r in range(2):
                rows = pl.ds(r * 512, 512)
                bs[rows, cols] = mm(h[rows, pl.ds(1024, 1024)], pick).astype(BF)

    build_pick()
    loads[0].wait()
    loads[1].wait()
    first(0)
    pl.semaphore_wait(barrier, 16)
    a2a(0, 0)
    loads[3].wait()
    loads[4].wait()
    gather_own()
    loads[5].wait()
    loads[6].wait()
    for q in range(4):
        ycopy(0, q).start()
    loads[2].wait()
    loads[7].wait()
    first(1)
    build_second()
    a2a_recv(0, 0)
    big(wb, bs, uv, 0, plain)
    a2a(1, 0)
    gather_far()
    a2a(0, 1)
    gather_mid()
    a2a_recv(1, 0)
    gate_chunk(0)
    gate_chunk(1)
    gather_last()
    for q in range(4):
        ycopy(0, q).wait()
    gather_done()
    ycopy(1, 0).wait()
    mlp(0)
    a2a_recv(0, 1)
    big(wb, bs, uv, 1, plain)
    a2a(1, 1)
    own_dm(0)
    ycopy(1, 1).wait()
    mlp(1)
    own_dm(1)
    res_own(0)
    res_own(1)
    finish_dm(0)
    a2a_recv(1, 1)
    gate_chunk(2)
    gate_chunk(3)
    res_part(0)
    res_part(1)
    ycopy(1, 2).wait()
    mlp(2)
    own_dm(2)
    a2a_recv(2, 0)
    a2a_sent(1, 0)
    big(wb, bs, uv, 0, TN)
    a2a(3, 0)
    ycopy(1, 3).wait()
    mlp(3)
    own_dm(3)
    res_part(2)
    res_part(3)
    res_own(2)
    res_own(3)
    for g in range(2):
        for k in range(4):
            count = ((64, 256, 128, 512), (64, 128, 256, 512))[g][k]
            drain(wt.at[0, pl.ds(0, count)], w_send.at[k, g])
    weight_grad(1, (0, 1))
    finish_dm(1)
    for q in range(4):
        ycopy(3, q).start()
    weight_grad(1, (2, 3))
    for peer in (xpeer, cpeer, znear, zfar):
        pl.semaphore_signal(credit, inc=1, device_id=seqdev(peer), device_id_type=MESH)
    pl.semaphore_wait(credit, 4)
    scatter_step(1, 0)
    weight_grad(0, (0, 1))
    scatter_step(1, 1)
    weight_grad(0, (2, 3))
    scatter_step(0, 0)
    a2a_recv(2, 1)
    a2a_sent(1, 1)
    big(wb, bs, uv, 1, TN)
    a2a(3, 1)
    scatter_step(0, 1)
    scatter_step(1, 2)
    a2a_recv(3, 0)
    outs = [finish_grad(0)]
    outs[0].start()
    scatter_step(0, 2)
    scatter_step(1, 3)
    scatter_step(0, 3)
    for s in range(2):
        outs.append(finish_res(s))
        outs[-1].start()
    scatter_step(1, 4)
    scatter_step(0, 4)
    a2a_recv(3, 1)
    outs.append(finish_grad(1))
    outs[-1].start()
    for kind in (2, 3):
        for s in range(2):
            a2a_sent(kind, s)
    for c in outs:
        c.wait()


def fused(
    inputs, first_factor, second_factor, gate_scale, gate_bias, in_weight, out_weight, cotangent
):
    count, rows, chan = inputs.shape
    hidden = in_weight.shape[1]
    anyspace = pl.BlockSpec(memory_space=pl.ANY)
    vmem = pl.BlockSpec(memory_space=pltpu.VMEM)
    cells = (2, 16, 64, 512)
    dma = pltpu.SemaphoreType.DMA
    buf = pltpu.VMEM
    res, ig, gi, go = pl.pallas_call(
        kernel,
        out_shape=(
            jax.ShapeDtypeStruct((2, 1024, 512), BF),
            jax.ShapeDtypeStruct(cells, BF),
            jax.ShapeDtypeStruct((64, hidden), F32),
            jax.ShapeDtypeStruct((64, hidden), F32),
        ),
        in_specs=[anyspace] * 4 + [vmem] * 2 + [anyspace] * 2,
        out_specs=(anyspace, anyspace, vmem, vmem),
        scratch_shapes=[
            buf((2, 1024, 512), BF),
            buf(first_factor.shape, BF),
            buf(second_factor.shape, BF),
            buf((1024, 1024), BF),
            buf((1024, 1024), BF),
            buf((2, 1024, 2048), BF),
            buf(cells, BF),
            buf(cells, BF),
            buf(cells, BF),
            buf(cells, BF),
            buf((2, 2048, 512), BF),
            buf((2, 2048, 512), BF),
            buf((2048, 2048), BF),
            buf((2048, 2048), BF),
            buf(cells, BF),
            buf(cells, BF),
            buf((2048, 512), BF),
            buf((2048, 512), BF),
            buf((2048, 512), BF),
            buf((2048, 512), BF),
            buf((256, 2048), BF),
            dma((8,)),
            dma((4, 2)),
            dma((4, 2)),
            dma((4, 4)),
            dma((4, 4)),
            dma((4, 2)),
            dma((4, 2)),
            dma((4, 2)),
            dma((4, 2)),
            dma((4,)),
            pltpu.SemaphoreType.REGULAR,
        ],
        compiler_params=pltpu.CompilerParams(
            collective_id=0, has_side_effects=True, vmem_limit_bytes=63 * MIB
        ),
        cost_estimate=pl.CostEstimate(flops=60 * 10**9, bytes_accessed=20 * MIB, transcendentals=0),
    )(
        inputs,
        cotangent,
        first_factor,
        second_factor,
        gate_scale.reshape(1, chan),
        gate_bias.reshape(1, chan),
        in_weight,
        out_weight.T,
    )
    return res, ig.reshape(inputs.shape), gi, go.T


def solution(mesh):
    in_specs = (
        P(None, "seq", "fsdp"),
        P("seq", None, None),
        P("seq", None, None),
        P("fsdp"),
        P("fsdp"),
        P("seq", "fsdp"),
        P("fsdp", "seq"),
        P(None, "seq", "fsdp"),
    )
    out_specs = (P(None, "seq", "fsdp"), P(None, "seq", "fsdp"), P("seq", "fsdp"), P("fsdp", "seq"))
    sizes = (mesh.shape["seq"], mesh.shape["fsdp"])
    part = fused if sizes == (16, 2) else body
    return jax.shard_map(part, mesh=mesh, in_specs=in_specs, out_specs=out_specs, check_vma=False)
```

```python
import functools

import jax
import jax.numpy as jnp
from jax import lax
from jax.experimental import pallas as pl
from jax.experimental.pallas import tpu as pltpu
from jax.sharding import PartitionSpec as P

BF = jnp.bfloat16
F32 = jnp.float32


def body(
    inputs, first_factor, second_factor, gate_scale, gate_bias, in_weight, out_weight, cotangent
):
    seq_count, tok_rows, chan = inputs.shape
    blocks, size, _ = first_factor.shape
    offs = second_factor.shape[0]
    owners = lax.axis_size("seq")
    groups = lax.axis_size("fsdp")
    mine = lax.axis_index("fsdp")
    width = chan * groups
    gain = gate_scale.reshape(1, 1, chan)
    shift = gate_bias.reshape(1, 1, chan)

    def swap(x):
        return lax.ppermute(x, "fsdp", [(0, 1), (1, 0)])

    def gather_cols(x):
        if groups != 2:
            return lax.all_gather(x, "fsdp", axis=1, tiled=True)
        return place(x, swap(x))

    def place(x, y):
        first = mine == 0
        return jnp.concatenate([jnp.where(first, x, y), jnp.where(first, y, x)], axis=1)

    def reduce_cols(left, weight, dims):
        if groups != 2:
            full = lax.dot_general(left, weight, dims, preferred_element_type=F32)
            got = lax.all_to_all(full, "fsdp", split_axis=1, concat_axis=0, tiled=True)
            return jnp.sum(got.reshape(groups, -1, chan), axis=0), None
        other = lax.dynamic_slice_in_dim(weight, (1 - mine) * chan, chan, 0)
        own = lax.dynamic_slice_in_dim(weight, mine * chan, chan, 0)
        sent = swap(lax.dot_general(left, other, dims, preferred_element_type=F32).astype(BF))
        kept = lax.dot_general(left, own, dims, preferred_element_type=F32)
        return kept, sent

    def exchange(x):
        return lax.all_to_all(x, "seq", split_axis=0, concat_axis=0, tiled=True)

    bar = lax.optimization_barrier
    nt = (((1,), (1,)), ((), ()))
    tn = (((0,), (0,)), ((), ()))
    seqs = range(seq_count)
    last = seq_count - 1
    both = jnp.stack([in_weight, out_weight.T], axis=0)
    both = lax.all_gather(both, "seq", axis=1, tiled=True)
    full_in, full_out = both[0], both[1]

    sources = [inputs[s].reshape(blocks, size, chan) for s in seqs]
    cots = [cotangent[s] for s in seqs]
    cot_all = [gather_cols(c) for c in cots]

    source = inputs.reshape(seq_count, blocks, size, chan)
    u = jnp.einsum("mkn,smnc->mksc", first_factor, source, preferred_element_type=F32)
    u = u.astype(BF).reshape(blocks, owners, offs, seq_count, chan).transpose(1, 3, 0, 2, 4)
    u, *cot_all = bar((exchange(u), *cot_all))
    turned = [u[:, s].reshape(owners * blocks, offs, chan) for s in seqs]
    mixes, seconds, mixed_all = [], [], []
    for s in seqs:
        w = jnp.einsum("kjm,mkc->kjc", second_factor, turned[s], preferred_element_type=F32)
        w = w.astype(BF).reshape(offs, owners, blocks, chan).transpose(1, 0, 2, 3)
        w = exchange(w)
        if s > 0:
            w, mixed_all[s - 1] = bar((w, mixed_all[s - 1]))
        w = bar(w.reshape(size, blocks, chan).transpose(1, 0, 2))
        gate = jax.nn.sigmoid(gain * sources[s].astype(F32) + shift)
        seconds.append(w)
        mixes.append((gate * w.astype(F32)).astype(BF).reshape(tok_rows, chan))
        if s < last or groups != 2:
            mixed_all.append(gather_cols(mixes[s]))
    swapped = swap(mixes[last]) if groups == 2 else None

    das, hs, sums = [], [], []
    for s in seqs:
        pre = jnp.dot(mixed_all[s], full_in, preferred_element_type=F32)
        dh = jnp.dot(cot_all[s], full_out, preferred_element_type=F32)
        sig = jax.nn.sigmoid(pre)
        hs.append((pre * sig).astype(BF))
        da = (dh * sig * (1.0 + pre * (1.0 - sig))).astype(BF)
        if s < last and groups == 2:
            da, swapped = bar((da, swapped))
            mixed_all.append(place(mixes[last], swapped))
        if s > 0 and groups == 2:
            kept, sent = sums[s - 1]
            da, sent = bar((da, sent))
            sums[s - 1] = kept, sent
        das.append(da)
        sums.append(reduce_cols(da, full_in, nt))

    out_term = sum(lax.dot_general(cot_all[s], hs[s], tn, preferred_element_type=F32) for s in seqs)
    out_term = out_term.astype(BF)
    if groups == 2:
        kept, sent = sums[last]
        sent, out_term = bar((sent, out_term))
        sums[last] = kept, sent
    grad_out = lax.psum_scatter(out_term, "seq", scatter_dimension=0, tiled=True)
    dms, dws, gates = [], [], []
    for s in seqs:
        gate = jax.nn.sigmoid(gain * sources[s].astype(F32) + shift)
        kept, sent = sums[s]
        dm = cots[s].astype(F32) + (kept if sent is None else kept + sent.astype(F32))
        dm = dm.astype(BF).reshape(blocks, size, chan)
        dw = (dm.astype(F32) * gate).astype(BF)
        dms.append(dm)
        gates.append(gate)
        dws.append(dw.reshape(blocks, owners, offs, chan).transpose(1, 0, 2, 3))
    dw = exchange(jnp.stack(dws, axis=1))
    in_term = sum(lax.dot_general(mixed_all[s], das[s], tn, preferred_element_type=F32) for s in seqs)
    dw, in_term = bar((dw, in_term.astype(BF)))
    scale = 1.0 / size
    grad_in = lax.psum_scatter(in_term, "seq", scatter_dimension=0, tiled=True)

    branches = [list(reduce_cols(hs[s], full_out, nt)) for s in seqs]
    dw = dw.transpose(1, 0, 2, 3, 4).reshape(seq_count, owners * blocks, offs, chan)
    du = jnp.einsum("kjm,sjkc->kmsc", second_factor, dw, preferred_element_type=F32)
    du = du.astype(BF).reshape(offs, owners, blocks, seq_count, chan).transpose(1, 3, 0, 2, 4)
    du = exchange(du)
    if groups == 2:
        du, *sents = bar((du, *[pair[1] for pair in branches]))
        branches = [[pair[0], sent] for pair, sent in zip(branches, sents)]
    grads, results = [], []
    for s in seqs:
        rows = du[:, s].reshape(size, blocks, chan)
        back = jnp.einsum("mkn,kmc->mnc", first_factor, rows, preferred_element_type=F32)
        gate = gates[s]
        gate_term = dms[s].astype(F32) * seconds[s].astype(F32) * gate * (1.0 - gate) * gain
        grads.append((back + gate_term).astype(BF).reshape(tok_rows, chan))
        kept, sent = branches[s]
        branch = kept if sent is None else kept + sent.astype(F32)
        results.append((mixes[s].astype(F32) + branch).astype(BF))
    return (
        jnp.stack(results),
        jnp.stack(grads),
        grad_in.astype(F32) * scale,
        grad_out.astype(F32).T * scale,
    )


MESH = pl.DeviceIdType.MESH
NT = (((1,), (1,)), ((), ()))
TN = (((0,), (0,)), ((), ()))
MIB = 1024 * 1024


def mm(a, b, dims=(((1,), (0,)), ((), ()))):
    return lax.dot_general(a, b, dims, preferred_element_type=F32)


def kernel(
    x_in, cot_in, f_in, s_in, gain_ref, shift_ref, wi_in, wo_in,
    res_out, ig_out, gi_out, go_out,
    x, ff, sf, bf, bs, wt, ub, uv, wb, wv, cota, mixa, h, da, dms, dmr, dmk, rs, rr, rk, lt,
    ld, a_send, a_recv, y_send, y_recv, w_send, w_recv, g_send, g_recv, o_sem, credit,
):
    me = lax.axis_index("seq")
    mine = lax.axis_index("fsdp")
    oth = 1 - mine
    zc, xc, cc = me // 4, (me // 2) % 2, me % 2
    xpeer = zc * 4 + (1 - xc) * 2 + cc
    cpeer = zc * 4 + xc * 2 + (1 - cc)

    odd, high = zc % 2, zc // 2
    znear = (zc + 1 - 2 * odd) * 4 + xc * 2 + cc
    zfar = ((zc + 2) % 4) * 4 + xc * 2 + cc

    def seqdev(i):
        return {"seq": i}

    ydev = {"fsdp": oth}

    def remote(src, dst, ss, rs_, dev):
        return pltpu.make_async_remote_copy(
            src_ref=src, dst_ref=dst, send_sem=ss, recv_sem=rs_, device_id=dev, device_id_type=MESH
        )

    def drain(ref, sem):
        pltpu.make_async_copy(ref, ref, sem).wait()

    loads = [
        pltpu.make_async_copy(x_in.at[0], x.at[0], ld.at[0]),
        pltpu.make_async_copy(f_in, ff, ld.at[1]),
        pltpu.make_async_copy(x_in.at[1], x.at[1], ld.at[2]),
        pltpu.make_async_copy(wi_in, wt.at[0, pl.ds(me * 64, 64)], ld.at[3]),
        pltpu.make_async_copy(wo_in, wt.at[1, pl.ds(me * 64, 64)], ld.at[4]),
        pltpu.make_async_copy(cot_in.at[0], cota.at[mine, pl.ds(0, 1024)], ld.at[5]),
        pltpu.make_async_copy(cot_in.at[1], cota.at[mine, pl.ds(1024, 1024)], ld.at[6]),
        pltpu.make_async_copy(s_in, sf, ld.at[7]),
    ]
    barrier = pltpu.get_barrier_semaphore()

    @pl.loop(1, 16)
    def _(d):
        pl.semaphore_signal(barrier, inc=1, device_id=seqdev((me + d) % 16), device_id_type=MESH)

    pl.semaphore_signal(barrier, inc=1, device_id=ydev, device_id_type=MESH)
    for c in loads:
        c.start()

    def yview(ref, q):
        return ref.at[mine, pl.ds(q * 512, 512)]

    def ycopy(kind, q):
        if kind == 0:
            a = b = yview(cota, q)
        elif kind == 1:
            a = b = yview(mixa, q)
        elif kind == 2:
            view = (q // 2, pl.ds((q % 2) * 8, 8))
            a, b = dms.at[view], dmr.at[view]
        else:
            a, b = rs.at[pl.ds(q * 512, 512)], rr.at[pl.ds(q * 512, 512)]
        return remote(a, b, y_send.at[kind, q], y_recv.at[kind, q], ydev)

    pairs = [(ub, uv), (wb, wv), (dms, uv), (wb, ub)]

    def a2a(kind, s):
        src, dst = pairs[kind]
        pltpu.make_async_copy(src.at[s, me], dst.at[s, me], a_recv.at[kind, s]).start()

        @pl.loop(1, 16)
        def _(d):
            e = 16 - d
            peer = ((zc + e // 4) % 4) * 4 + ((xc + (e // 2) % 2) % 2) * 2 + (cc + e % 2) % 2
            remote(src.at[s, peer], dst.at[s, me], a_send.at[kind, s], a_recv.at[kind, s], seqdev(peer)).start()

    def a2a_recv(kind, s):
        drain(pairs[kind][1].at[s], a_recv.at[kind, s])

    def a2a_sent(kind, s):
        drain(pairs[kind][0].at[s, pl.ds(0, 15)], a_send.at[kind, s])

    FAR, NEAR, NEXT, ACROSS, CORE = range(5)
    peers = (zfar, znear, znear, xpeer, cpeer)
    counts = (64, 64, 64, 256, 512)

    def shard(owner, stages):
        for g in range(2):
            rows = wt.at[g, pl.ds(owner * 64, 64)]
            for k in stages:
                remote(rows, rows, w_send.at[k, g], w_recv.at[k, g], seqdev(peers[k])).start()

    def gathered(k, sems):
        for g in range(2):
            drain(wt.at[0, pl.ds(0, counts[k])], sems.at[k, g])

    def gather_own():
        shard(me, (FAR, NEAR, ACROSS, CORE))

    def gather_far():
        gathered(NEAR, w_recv)
        shard(znear, (ACROSS, CORE))
        gathered(FAR, w_recv)
        shard(zfar, (NEXT, ACROSS, CORE))

    def gather_mid():
        gathered(NEXT, w_recv)
        shard((znear + 8) % 16, (ACROSS, CORE))

    def gather_last():
        gathered(ACROSS, w_recv)

        @pl.loop(0, 4)
        def _(i):
            shard(i * 4 + (1 - xc) * 2 + cc, (CORE,))

    def gather_done():
        gathered(CORE, w_recv)

    gain = gain_ref[...]
    shift = shift_ref[...]

    def big(dst, mat, src, s, dims):
        @pl.loop(0, 4)
        def _(t):
            if dims is TN:
                lhs = mat[:, pl.ds(pl.multiple_of(t * 256, 256), 256)]
            else:
                lhs = mat[pl.ds(pl.multiple_of(t * 256, 256), 256), :]
            out = mm(lhs, src[s].reshape(1024, 512), dims if dims is TN else (((1,), (0,)), ((), ())))
            dst[s, pl.ds(t * 4, 4)] = out.astype(BF).reshape(4, 64, 512)

    def mixer_rows(s, jj):
        w = wv[s, :, pl.ds(pl.multiple_of(jj * 16, 16), 16), :].astype(F32).reshape(16, 2, 8, 512)
        w = jnp.concatenate([w[:, 0].reshape(128, 512), w[:, 1].reshape(128, 512)], axis=0)
        rows = pl.ds(pl.multiple_of(jj * 256, 256), 256)
        gate = jax.nn.sigmoid(gain * x[s, rows, :].astype(F32) + shift)
        return w, gate

    def gate_chunk(q):
        s = q // 2

        @pl.loop((q % 2) * 2, (q % 2) * 2 + 2)
        def _(jj):
            w, gate = mixer_rows(s, jj)
            rows = pl.ds(pl.multiple_of(s * 1024 + jj * 256, 256), 256)
            mixa[mine, rows, :] = (gate * w).astype(BF)

        ycopy(1, q).start()

    def mlp(q):
        rows = pl.ds(q * 512, 512)
        s = q // 2

        @pl.loop(0, 8)
        def _(f):
            cols = pl.ds(pl.multiple_of(f * 256, 256), 256)
            pre = mm(mixa[0, rows, :], wt[0, pl.ds(0, 512), cols]) + mm(mixa[1, rows, :], wt[0, pl.ds(512, 512), cols])
            dh = mm(cota[0, rows, :], wt[1, pl.ds(0, 512), cols]) + mm(cota[1, rows, :], wt[1, pl.ds(512, 512), cols])
            sig = jax.nn.sigmoid(pre)
            h[rows, cols] = (pre * sig).astype(BF)
            da[rows, cols] = (dh * sig * (1.0 + pre * (1.0 - sig))).astype(BF)

        @pl.loop(0, 2)
        def _(n):
            cols = pl.ds(pl.multiple_of(n * 256, 256), 256)
            chans = pl.ds(pl.multiple_of(oth * 512 + n * 256, 256), 256)
            out = mm(da[rows, :], wt[0, chans, :], NT)
            dms[s, pl.ds((q % 2) * 8, 8), :, cols] = out.astype(BF).reshape(8, 64, 256)

        ycopy(2, q).start()

    def own_dm(q):
        rows = pl.ds(q * 512, 512)

        @pl.loop(0, 2)
        def _(n):
            cols = pl.ds(pl.multiple_of(n * 256, 256), 256)
            chans = pl.ds(pl.multiple_of(mine * 512 + n * 256, 256), 256)
            out = mm(da[rows, :], wt[0, chans, :], NT)
            dmk[rows, cols] = (out + cota[mine, rows, cols].astype(F32)).astype(BF)

    def res_part(q):
        rows = pl.ds(q * 512, 512)

        @pl.loop(0, 2)
        def _(n):
            cols = pl.ds(pl.multiple_of(n * 256, 256), 256)
            chans = pl.ds(pl.multiple_of(oth * 512 + n * 256, 256), 256)
            rs[rows, cols] = mm(h[rows, :], wt[1, chans, :], NT).astype(BF)

    def res_own(q):
        rows = pl.ds(q * 512, 512)

        @pl.loop(0, 2)
        def _(n):
            cols = pl.ds(pl.multiple_of(n * 256, 256), 256)
            chans = pl.ds(pl.multiple_of(mine * 512 + n * 256, 256), 256)
            out = mm(h[rows, :], wt[1, chans, :], NT)
            rk[rows, cols] = (out + mixa[mine, rows, cols].astype(F32)).astype(BF)

    def finish_dm(s):
        a2a_sent(0, s)
        for q in (2 * s, 2 * s + 1):
            ycopy(2, q).wait()

        @pl.loop(0, 4)
        def _(jj):
            w, gate = mixer_rows(s, jj)
            rows = pl.ds(pl.multiple_of(s * 1024 + jj * 256, 256), 256)
            slab = pl.ds(jj * 4, 4)
            dm = dmk[rows, :].astype(F32) + dmr[s, slab].astype(F32).reshape(256, 512)
            dm = dm.astype(BF)
            dmr[s, slab] = dm.reshape(4, 64, 512)
            dw = (dm.astype(F32) * gate).reshape(2, 16, 8, 512)
            dw = jnp.concatenate([dw[0], dw[1]], axis=1)
            dms[s, :, pl.ds(pl.multiple_of(jj * 16, 16), 16), :] = dw.astype(BF)

        a2a(2, s)

    def finish_grad(s):
        @pl.loop(0, 4)
        def _(jj):
            w, gate = mixer_rows(s, jj)
            slab = pl.ds(jj * 4, 4)
            dm = dmr[s, slab].astype(F32).reshape(256, 512)
            term = dm * w * gate * (1.0 - gate) * gain
            cols = pl.ds(pl.multiple_of(jj * 256, 256), 256)
            out = mm(bf[:, cols], ub[s].reshape(1024, 512), TN)
            uv[s, slab] = (out + term).astype(BF).reshape(4, 64, 512)

        return pltpu.make_async_copy(uv.at[s], ig_out.at[s], o_sem.at[s])

    def finish_res(s):
        for q in (2 * s, 2 * s + 1):
            ycopy(3, q).wait()

        @pl.loop(0, 4)
        def _(jj):
            rows = pl.ds(pl.multiple_of(s * 1024 + jj * 256, 256), 256)
            rk[rows, :] = (rk[rows, :].astype(F32) + rr[rows, :].astype(F32)).astype(BF)

        return pltpu.make_async_copy(rk.at[pl.ds(s * 1024, 1024)], res_out.at[s], o_sem.at[2 + s])

    def weight_grad(g):
        src, rhs = (mixa, da) if g == 0 else (cota, h)
        for y in range(2):
            @pl.loop(0, 8)
            def _(i):
                rows = pl.ds(pl.multiple_of(i * 256, 256), 256)
                lt[:, rows] = src[y, rows, :].T

            @pl.loop(0, 4)
            def _(f):
                cols = pl.ds(pl.multiple_of(f * 512, 512), 512)
                out = mm(lt[...], rhs[:, cols]).astype(BF)
                for i in range(8):
                    xi, ci = (i // 2) % 2, i % 2
                    slot = ci * 512 + xi * 256 + (i // 4) * 128 + y * 64
                    wt[g, pl.ds(slot, 64), cols] = out[i * 64 : i * 64 + 64]

    def add_rows(g, cols, base, off, count):
        @pl.loop(0, count)
        def _(i):
            rows = pl.ds(pl.multiple_of(base + i * 64, 64), 64)
            more = da[pl.ds(pl.multiple_of(off + i * 64, 64), 64), cols].astype(F32)
            wt[g, rows, cols] = (wt[g, rows, cols].astype(F32) + more).astype(BF)

    def halving(g, part, step):
        bits = (cc, xc, odd, high)
        partner = (cpeer, xpeer, znear, zfar)
        size = 512 >> step
        keep = 0
        for k in range(step):
            keep = keep + bits[k] * (512 >> k)
        send = keep + (1 - bits[step]) * size
        keep = keep + bits[step] * size
        land = 2048 - (2048 >> step) + g * size
        cols = pl.ds(part * 1024, 1024)
        copy = remote(
            wt.at[g, pl.ds(send, size), cols], da.at[pl.ds(land, size), cols],
            g_send.at[step, 2 * g + part], g_recv.at[step, 2 * g + part], seqdev(partner[step]),
        )
        return copy, keep, land, size, cols

    def scatter_step(g, part, step):
        if step > 0:
            copy, keep, land, size, cols = halving(g, part, step - 1)
            copy.wait()
            if step < 4:
                add_rows(g, cols, keep, land, size // 64)
            else:
                out = gi_out if g == 0 else go_out
                own = wt[g, pl.ds(pl.multiple_of(keep, 64), 64), cols].astype(F32)
                out[:, cols] = (own + da[pl.ds(land, 64), cols].astype(F32)) * (1.0 / 128)
        if step < 4:
            halving(g, part, step)[0].start()

    plain = (((1,), (0,)), ((), ()))

    def build_pick():
        @pl.loop(0, 4)
        def _(t):
            row = lax.broadcasted_iota(jnp.int32, (256, 1024), 0) + t * 256
            col = lax.broadcasted_iota(jnp.int32, (256, 1024), 1)
            want = (row & 7) * 128 + (row >> 3)
            rows = pl.ds(pl.multiple_of(1024 + t * 256, 256), 256)
            da[rows, pl.ds(0, 1024)] = jnp.where(col == want, 1.0, 0.0).astype(BF)

    def pick_rows(t):
        return da[pl.ds(pl.multiple_of(1024 + t * 256, 256), 256), pl.ds(0, 1024)]

    def first(s):
        for m in range(8):
            rows = pl.ds(m * 128, 128)
            h[rows, pl.ds(0, 512)] = mm(ff[m], x[s, rows, :]).astype(BF)

        @pl.loop(0, 4)
        def _(t):
            out = mm(pick_rows(t), h[pl.ds(0, 1024), pl.ds(0, 512)])
            ub[s, pl.ds(t * 4, 4)] = out.astype(BF).reshape(4, 64, 512)

    def build_second():
        for fac, rows in ((ff, 0), (sf, 1024)):
            da[pl.ds(rows, 1024), pl.ds(1024, 1024)] = jnp.zeros((1024, 1024), BF)
            for m in range(8):
                da[pl.ds(rows + m * 128, 128), pl.ds(1024 + m * 128, 128)] = fac[m]

        @pl.loop(0, 4)
        def _(t):
            rows = pl.ds(pl.multiple_of(t * 256, 256), 256)
            bf[rows, :] = mm(pick_rows(t), da[pl.ds(0, 1024), pl.ds(1024, 1024)]).astype(BF)
            h[rows, pl.ds(1024, 1024)] = mm(pick_rows(t), da[pl.ds(1024, 1024), pl.ds(1024, 1024)]).astype(BF)

        @pl.loop(0, 4)
        def _(t):
            row = lax.broadcasted_iota(jnp.int32, (1024, 256), 0)
            col = lax.broadcasted_iota(jnp.int32, (1024, 256), 1) + t * 256
            want = ((col >> 3) & 7) * 128 + (col >> 6) * 8 + (col & 7)
            pick = jnp.where(row == want, 1.0, 0.0).astype(BF)
            cols = pl.ds(pl.multiple_of(t * 256, 256), 256)
            for r in range(2):
                rows = pl.ds(r * 512, 512)
                bs[rows, cols] = mm(h[rows, pl.ds(1024, 1024)], pick).astype(BF)

    build_pick()
    loads[0].wait()
    loads[1].wait()
    first(0)
    pl.semaphore_wait(barrier, 16)
    a2a(0, 0)
    loads[3].wait()
    loads[4].wait()
    gather_own()
    loads[5].wait()
    loads[6].wait()
    for q in range(4):
        ycopy(0, q).start()
    loads[2].wait()
    loads[7].wait()
    first(1)
    build_second()
    a2a_recv(0, 0)
    big(wb, bs, uv, 0, plain)
    a2a(1, 0)
    gather_far()
    a2a(0, 1)
    gather_mid()
    a2a_recv(1, 0)
    gate_chunk(0)
    gate_chunk(1)
    gather_last()
    a2a_recv(0, 1)
    big(wb, bs, uv, 1, plain)
    a2a(1, 1)
    for q in range(4):
        ycopy(0, q).wait()
    gather_done()
    ycopy(1, 0).wait()
    mlp(0)
    own_dm(0)
    ycopy(1, 1).wait()
    mlp(1)
    own_dm(1)
    res_own(0)
    res_own(1)
    a2a_recv(1, 1)
    gate_chunk(2)
    gate_chunk(3)
    finish_dm(0)
    res_part(0)
    res_part(1)
    ycopy(1, 2).wait()
    mlp(2)
    own_dm(2)
    res_part(2)
    res_own(2)
    a2a_recv(2, 0)
    a2a_sent(1, 0)
    big(wb, bs, uv, 0, TN)
    a2a(3, 0)
    ycopy(1, 3).wait()
    mlp(3)
    own_dm(3)
    for k in range(5):
        gathered(k, w_send)
    weight_grad(0)
    for peer in (xpeer, cpeer, znear, zfar):
        pl.semaphore_signal(credit, inc=1, device_id=seqdev(peer), device_id_type=MESH)
    finish_dm(1)
    pl.semaphore_wait(credit, 4)
    scatter_step(0, 0, 0)
    scatter_step(0, 1, 0)
    res_part(3)
    res_own(3)
    scatter_step(0, 0, 1)
    scatter_step(0, 1, 1)
    for q in range(4):
        ycopy(3, q).start()
    weight_grad(1)
    scatter_step(1, 0, 0)
    scatter_step(1, 1, 0)
    a2a_recv(2, 1)
    a2a_sent(1, 1)
    big(wb, bs, uv, 1, TN)
    a2a(3, 1)
    scatter_step(1, 0, 1)
    scatter_step(1, 1, 1)
    scatter_step(0, 0, 2)
    scatter_step(0, 1, 2)
    a2a_recv(3, 0)
    outs = [finish_grad(0)]
    outs[0].start()
    scatter_step(0, 0, 3)
    scatter_step(0, 1, 3)
    scatter_step(1, 0, 2)
    scatter_step(1, 1, 2)
    scatter_step(1, 0, 3)
    scatter_step(1, 1, 3)
    for s in range(2):
        outs.append(finish_res(s))
        outs[-1].start()
    scatter_step(0, 0, 4)
    scatter_step(0, 1, 4)
    a2a_recv(3, 1)
    outs.append(finish_grad(1))
    outs[-1].start()
    scatter_step(1, 0, 4)
    scatter_step(1, 1, 4)
    for kind in (2, 3):
        for s in range(2):
            a2a_sent(kind, s)
    for c in outs:
        c.wait()


def fused(
    inputs, first_factor, second_factor, gate_scale, gate_bias, in_weight, out_weight, cotangent
):
    count, rows, chan = inputs.shape
    hidden = in_weight.shape[1]
    anyspace = pl.BlockSpec(memory_space=pl.ANY)
    vmem = pl.BlockSpec(memory_space=pltpu.VMEM)
    cells = (2, 16, 64, 512)
    dma = pltpu.SemaphoreType.DMA
    buf = pltpu.VMEM
    res, ig, gi, go = pl.pallas_call(
        kernel,
        out_shape=(
            jax.ShapeDtypeStruct((2, 1024, 512), BF),
            jax.ShapeDtypeStruct(cells, BF),
            jax.ShapeDtypeStruct((64, hidden), F32),
            jax.ShapeDtypeStruct((64, hidden), F32),
        ),
        in_specs=[anyspace] * 4 + [vmem] * 2 + [anyspace] * 2,
        out_specs=(anyspace, anyspace, vmem, vmem),
        scratch_shapes=[
            buf((2, 1024, 512), BF),
            buf(first_factor.shape, BF),
            buf(second_factor.shape, BF),
            buf((1024, 1024), BF),
            buf((1024, 1024), BF),
            buf((2, 1024, 2048), BF),
            buf(cells, BF),
            buf(cells, BF),
            buf(cells, BF),
            buf(cells, BF),
            buf((2, 2048, 512), BF),
            buf((2, 2048, 512), BF),
            buf((2048, 2048), BF),
            buf((2048, 2048), BF),
            buf(cells, BF),
            buf(cells, BF),
            buf((2048, 512), BF),
            buf((2048, 512), BF),
            buf((2048, 512), BF),
            buf((2048, 512), BF),
            buf((512, 2048), BF),
            dma((8,)),
            dma((4, 2)),
            dma((4, 2)),
            dma((4, 4)),
            dma((4, 4)),
            dma((5, 2)),
            dma((5, 2)),
            dma((4, 4)),
            dma((4, 4)),
            dma((4,)),
            pltpu.SemaphoreType.REGULAR,
        ],
        compiler_params=pltpu.CompilerParams(
            collective_id=0, has_side_effects=True, vmem_limit_bytes=63 * MIB
        ),
        cost_estimate=pl.CostEstimate(flops=60 * 10**9, bytes_accessed=20 * MIB, transcendentals=0),
    )(
        inputs,
        cotangent,
        first_factor,
        second_factor,
        gate_scale.reshape(1, chan),
        gate_bias.reshape(1, chan),
        in_weight,
        out_weight.T,
    )
    return res, ig.reshape(inputs.shape), gi, go.T


def solution(mesh):
    in_specs = (
        P(None, "seq", "fsdp"),
        P("seq", None, None),
        P("seq", None, None),
        P("fsdp"),
        P("fsdp"),
        P("seq", "fsdp"),
        P("fsdp", "seq"),
        P(None, "seq", "fsdp"),
    )
    out_specs = (P(None, "seq", "fsdp"), P(None, "seq", "fsdp"), P("seq", "fsdp"), P("fsdp", "seq"))
    sizes = (mesh.shape["seq"], mesh.shape["fsdp"])
    part = fused if sizes == (16, 2) else body
    return jax.shard_map(part, mesh=mesh, in_specs=in_specs, out_specs=out_specs, check_vma=False)
```

```python
import functools

import jax
import jax.numpy as jnp
from jax import lax
from jax.experimental import pallas as pl
from jax.experimental.pallas import tpu as pltpu
from jax.sharding import PartitionSpec as P

BF = jnp.bfloat16
F32 = jnp.float32


def body(
    inputs, first_factor, second_factor, gate_scale, gate_bias, in_weight, out_weight, cotangent
):
    seq_count, tok_rows, chan = inputs.shape
    blocks, size, _ = first_factor.shape
    offs = second_factor.shape[0]
    owners = lax.axis_size("seq")
    groups = lax.axis_size("fsdp")
    mine = lax.axis_index("fsdp")
    width = chan * groups
    gain = gate_scale.reshape(1, 1, chan)
    shift = gate_bias.reshape(1, 1, chan)

    def swap(x):
        return lax.ppermute(x, "fsdp", [(0, 1), (1, 0)])

    def gather_cols(x):
        if groups != 2:
            return lax.all_gather(x, "fsdp", axis=1, tiled=True)
        return place(x, swap(x))

    def place(x, y):
        first = mine == 0
        return jnp.concatenate([jnp.where(first, x, y), jnp.where(first, y, x)], axis=1)

    def reduce_cols(left, weight, dims):
        if groups != 2:
            full = lax.dot_general(left, weight, dims, preferred_element_type=F32)
            got = lax.all_to_all(full, "fsdp", split_axis=1, concat_axis=0, tiled=True)
            return jnp.sum(got.reshape(groups, -1, chan), axis=0), None
        other = lax.dynamic_slice_in_dim(weight, (1 - mine) * chan, chan, 0)
        own = lax.dynamic_slice_in_dim(weight, mine * chan, chan, 0)
        sent = swap(lax.dot_general(left, other, dims, preferred_element_type=F32).astype(BF))
        kept = lax.dot_general(left, own, dims, preferred_element_type=F32)
        return kept, sent

    def exchange(x):
        return lax.all_to_all(x, "seq", split_axis=0, concat_axis=0, tiled=True)

    bar = lax.optimization_barrier
    nt = (((1,), (1,)), ((), ()))
    tn = (((0,), (0,)), ((), ()))
    seqs = range(seq_count)
    last = seq_count - 1
    both = jnp.stack([in_weight, out_weight.T], axis=0)
    both = lax.all_gather(both, "seq", axis=1, tiled=True)
    full_in, full_out = both[0], both[1]

    sources = [inputs[s].reshape(blocks, size, chan) for s in seqs]
    cots = [cotangent[s] for s in seqs]
    cot_all = [gather_cols(c) for c in cots]

    source = inputs.reshape(seq_count, blocks, size, chan)
    u = jnp.einsum("mkn,smnc->mksc", first_factor, source, preferred_element_type=F32)
    u = u.astype(BF).reshape(blocks, owners, offs, seq_count, chan).transpose(1, 3, 0, 2, 4)
    u, *cot_all = bar((exchange(u), *cot_all))
    turned = [u[:, s].reshape(owners * blocks, offs, chan) for s in seqs]
    mixes, seconds, mixed_all = [], [], []
    for s in seqs:
        w = jnp.einsum("kjm,mkc->kjc", second_factor, turned[s], preferred_element_type=F32)
        w = w.astype(BF).reshape(offs, owners, blocks, chan).transpose(1, 0, 2, 3)
        w = exchange(w)
        if s > 0:
            w, mixed_all[s - 1] = bar((w, mixed_all[s - 1]))
        w = bar(w.reshape(size, blocks, chan).transpose(1, 0, 2))
        gate = jax.nn.sigmoid(gain * sources[s].astype(F32) + shift)
        seconds.append(w)
        mixes.append((gate * w.astype(F32)).astype(BF).reshape(tok_rows, chan))
        if s < last or groups != 2:
            mixed_all.append(gather_cols(mixes[s]))
    swapped = swap(mixes[last]) if groups == 2 else None

    das, hs, sums = [], [], []
    for s in seqs:
        pre = jnp.dot(mixed_all[s], full_in, preferred_element_type=F32)
        dh = jnp.dot(cot_all[s], full_out, preferred_element_type=F32)
        sig = jax.nn.sigmoid(pre)
        hs.append((pre * sig).astype(BF))
        da = (dh * sig * (1.0 + pre * (1.0 - sig))).astype(BF)
        if s < last and groups == 2:
            da, swapped = bar((da, swapped))
            mixed_all.append(place(mixes[last], swapped))
        if s > 0 and groups == 2:
            kept, sent = sums[s - 1]
            da, sent = bar((da, sent))
            sums[s - 1] = kept, sent
        das.append(da)
        sums.append(reduce_cols(da, full_in, nt))

    out_term = sum(lax.dot_general(cot_all[s], hs[s], tn, preferred_element_type=F32) for s in seqs)
    out_term = out_term.astype(BF)
    if groups == 2:
        kept, sent = sums[last]
        sent, out_term = bar((sent, out_term))
        sums[last] = kept, sent
    grad_out = lax.psum_scatter(out_term, "seq", scatter_dimension=0, tiled=True)
    dms, dws, gates = [], [], []
    for s in seqs:
        gate = jax.nn.sigmoid(gain * sources[s].astype(F32) + shift)
        kept, sent = sums[s]
        dm = cots[s].astype(F32) + (kept if sent is None else kept + sent.astype(F32))
        dm = dm.astype(BF).reshape(blocks, size, chan)
        dw = (dm.astype(F32) * gate).astype(BF)
        dms.append(dm)
        gates.append(gate)
        dws.append(dw.reshape(blocks, owners, offs, chan).transpose(1, 0, 2, 3))
    dw = exchange(jnp.stack(dws, axis=1))
    in_term = sum(lax.dot_general(mixed_all[s], das[s], tn, preferred_element_type=F32) for s in seqs)
    dw, in_term = bar((dw, in_term.astype(BF)))
    scale = 1.0 / size
    grad_in = lax.psum_scatter(in_term, "seq", scatter_dimension=0, tiled=True)

    branches = [list(reduce_cols(hs[s], full_out, nt)) for s in seqs]
    dw = dw.transpose(1, 0, 2, 3, 4).reshape(seq_count, owners * blocks, offs, chan)
    du = jnp.einsum("kjm,sjkc->kmsc", second_factor, dw, preferred_element_type=F32)
    du = du.astype(BF).reshape(offs, owners, blocks, seq_count, chan).transpose(1, 3, 0, 2, 4)
    du = exchange(du)
    if groups == 2:
        du, *sents = bar((du, *[pair[1] for pair in branches]))
        branches = [[pair[0], sent] for pair, sent in zip(branches, sents)]
    grads, results = [], []
    for s in seqs:
        rows = du[:, s].reshape(size, blocks, chan)
        back = jnp.einsum("mkn,kmc->mnc", first_factor, rows, preferred_element_type=F32)
        gate = gates[s]
        gate_term = dms[s].astype(F32) * seconds[s].astype(F32) * gate * (1.0 - gate) * gain
        grads.append((back + gate_term).astype(BF).reshape(tok_rows, chan))
        kept, sent = branches[s]
        branch = kept if sent is None else kept + sent.astype(F32)
        results.append((mixes[s].astype(F32) + branch).astype(BF))
    return (
        jnp.stack(results),
        jnp.stack(grads),
        grad_in.astype(F32) * scale,
        grad_out.astype(F32).T * scale,
    )


MESH = pl.DeviceIdType.MESH
NT = (((1,), (1,)), ((), ()))
TN = (((0,), (0,)), ((), ()))
MIB = 1024 * 1024


def mm(a, b, dims=(((1,), (0,)), ((), ()))):
    return lax.dot_general(a, b, dims, preferred_element_type=F32)


def kernel(
    x_in, cot_in, f_in, s_in, gain_ref, shift_ref, wi_in, wo_in,
    res_out, ig_out, gi_out, go_out, bf_hold,
    x, ff, sf, bs, wt, ub, uv, wb, wv, cota, mixa, h, da, dms, dmr, dmk, rs, rr, rk, lt,
    ld, a_send, a_recv, y_send, y_recv, w_send, w_recv, g_send, g_recv, o_sem, credit_a, credit_b,
):
    me = lax.axis_index("seq")
    mine = lax.axis_index("fsdp")
    oth = 1 - mine
    zc, xc, cc = me // 4, (me // 2) % 2, me % 2
    xpeer = zc * 4 + (1 - xc) * 2 + cc
    cpeer = zc * 4 + xc * 2 + (1 - cc)

    odd, high = zc % 2, zc // 2
    znear = (zc + 1 - 2 * odd) * 4 + xc * 2 + cc
    zfar = ((zc + 2) % 4) * 4 + xc * 2 + cc

    def seqdev(i):
        return {"seq": i}

    ydev = {"fsdp": oth}

    def remote(src, dst, ss, rs_, dev):
        return pltpu.make_async_remote_copy(
            src_ref=src, dst_ref=dst, send_sem=ss, recv_sem=rs_, device_id=dev, device_id_type=MESH
        )

    def drain(ref, sem):
        pltpu.make_async_copy(ref, ref, sem).wait()

    loads = [
        pltpu.make_async_copy(x_in.at[0], x.at[0], ld.at[0]),
        pltpu.make_async_copy(f_in, ff, ld.at[1]),
        pltpu.make_async_copy(x_in.at[1], x.at[1], ld.at[2]),
        pltpu.make_async_copy(wi_in, wt.at[0, pl.ds(me * 64, 64)], ld.at[3]),
        pltpu.make_async_copy(wo_in, wt.at[1, pl.ds(me * 64, 64)], ld.at[4]),
        pltpu.make_async_copy(cot_in.at[0], cota.at[mine, pl.ds(0, 1024)], ld.at[5]),
        pltpu.make_async_copy(cot_in.at[1], cota.at[mine, pl.ds(1024, 1024)], ld.at[6]),
        pltpu.make_async_copy(s_in, sf, ld.at[7]),
    ]
    barrier = pltpu.get_barrier_semaphore()

    @pl.loop(1, 16)
    def _(d):
        pl.semaphore_signal(barrier, inc=1, device_id=seqdev((me + d) % 16), device_id_type=MESH)

    pl.semaphore_signal(barrier, inc=1, device_id=ydev, device_id_type=MESH)
    for c in loads:
        c.start()

    def yview(ref, q):
        return ref.at[mine, pl.ds(q * 512, 512)]

    def ycopy(kind, q):
        if kind == 0:
            a = b = yview(cota, q)
        elif kind == 1:
            a = b = yview(mixa, q)
        else:
            view = (q // 2, pl.ds((q % 2) * 8, 8))
            a, b = rs.at[view], (dmr if kind == 2 else rr).at[view]
        return remote(a, b, y_send.at[kind, q], y_recv.at[kind, q], ydev)

    pairs = [(ub, uv), (wb, wv), (dms, uv), (wb, ub)]

    def a2a(kind, s, rows=slice(0, 64)):
        src, dst = pairs[kind]
        rows = pl.ds(rows.start, rows.stop - rows.start)
        pltpu.make_async_copy(src.at[s, me, rows], dst.at[s, me, rows], a_recv.at[kind, s]).start()

        @pl.loop(1, 16)
        def _(d):
            e = 16 - d
            peer = ((zc + e // 4) % 4) * 4 + ((xc + (e // 2) % 2) % 2) * 2 + (cc + e % 2) % 2
            remote(src.at[s, peer, rows], dst.at[s, me, rows], a_send.at[kind, s], a_recv.at[kind, s], seqdev(peer)).start()

    def a2a_recv(kind, s):
        drain(pairs[kind][1].at[s], a_recv.at[kind, s])

    def a2a_sent(kind, s):
        drain(pairs[kind][0].at[s, pl.ds(0, 15)], a_send.at[kind, s])

    FAR, NEAR, NEXT, ACROSS, CORE = range(5)
    peers = (zfar, znear, znear, xpeer, cpeer)
    counts = (64, 64, 64, 256, 512)

    def shard(owner, stages):
        for g in range(2):
            rows = wt.at[g, pl.ds(owner * 64, 64)]
            for k in stages:
                remote(rows, rows, w_send.at[k, g], w_recv.at[k, g], seqdev(peers[k])).start()

    def gathered(k, sems):
        for g in range(2):
            drain(wt.at[0, pl.ds(0, counts[k])], sems.at[k, g])

    def gather_own():
        shard(me, (FAR, NEAR, ACROSS, CORE))

    def gather_far():
        gathered(NEAR, w_recv)
        shard(znear, (ACROSS, CORE))
        gathered(FAR, w_recv)
        shard(zfar, (NEXT, ACROSS, CORE))

    def gather_mid():
        gathered(NEXT, w_recv)
        shard((znear + 8) % 16, (ACROSS, CORE))

    def gather_last():
        gathered(ACROSS, w_recv)

        @pl.loop(0, 4)
        def _(i):
            shard(i * 4 + (1 - xc) * 2 + cc, (CORE,))

    def gather_done():
        gathered(CORE, w_recv)

    gain = gain_ref[...]
    shift = shift_ref[...]

    def big(dst, mat, src, s, dims):
        @pl.loop(0, 4)
        def _(t):
            if dims is TN:
                lhs = mat[:, pl.ds(pl.multiple_of(t * 256, 256), 256)]
            else:
                lhs = mat[pl.ds(pl.multiple_of(t * 256, 256), 256), :]
            out = mm(lhs, src[s].reshape(1024, 512), dims if dims is TN else (((1,), (0,)), ((), ())))
            dst[s, pl.ds(t * 4, 4)] = out.astype(BF).reshape(4, 64, 512)

    def mixer_rows(s, jj):
        w = wv[s, :, pl.ds(pl.multiple_of(jj * 16, 16), 16), :].astype(F32).reshape(16, 2, 8, 512)
        w = jnp.concatenate([w[:, 0].reshape(128, 512), w[:, 1].reshape(128, 512)], axis=0)
        rows = pl.ds(pl.multiple_of(jj * 256, 256), 256)
        gate = jax.nn.sigmoid(gain * x[s, rows, :].astype(F32) + shift)
        return w, gate

    def gate_chunk(q):
        s = q // 2

        @pl.loop((q % 2) * 2, (q % 2) * 2 + 2)
        def _(jj):
            w, gate = mixer_rows(s, jj)
            rows = pl.ds(pl.multiple_of(s * 1024 + jj * 256, 256), 256)
            mixa[mine, rows, :] = (gate * w).astype(BF)

        ycopy(1, q).start()

    def mlp(q):
        rows = pl.ds(q * 512, 512)
        s = q // 2

        @pl.loop(0, 8)
        def _(f):
            cols = pl.ds(pl.multiple_of(f * 256, 256), 256)
            pre = mm(mixa[0, rows, :], wt[0, pl.ds(0, 512), cols]) + mm(mixa[1, rows, :], wt[0, pl.ds(512, 512), cols])
            dh = mm(cota[0, rows, :], wt[1, pl.ds(0, 512), cols]) + mm(cota[1, rows, :], wt[1, pl.ds(512, 512), cols])
            sig = jax.nn.sigmoid(pre)
            h[rows, cols] = (pre * sig).astype(BF)
            da[rows, cols] = (dh * sig * (1.0 + pre * (1.0 - sig))).astype(BF)

        @pl.loop(0, 2)
        def _(n):
            cols = pl.ds(pl.multiple_of(n * 256, 256), 256)
            chans = pl.ds(pl.multiple_of(oth * 512 + n * 256, 256), 256)
            out = mm(da[rows, :], wt[0, chans, :], NT)
            rs[s, pl.ds((q % 2) * 8, 8), :, cols] = out.astype(BF).reshape(8, 64, 256)

        ycopy(2, q).start()

    def own_dm(q):
        rows = pl.ds(q * 512, 512)

        @pl.loop(0, 2)
        def _(n):
            cols = pl.ds(pl.multiple_of(n * 256, 256), 256)
            chans = pl.ds(pl.multiple_of(mine * 512 + n * 256, 256), 256)
            out = mm(da[rows, :], wt[0, chans, :], NT)
            dmk[rows, cols] = (out + cota[mine, rows, cols].astype(F32)).astype(BF)

    def res_part(q):
        rows = pl.ds(q * 512, 512)

        @pl.loop(0, 2)
        def _(n):
            cols = pl.ds(pl.multiple_of(n * 256, 256), 256)
            chans = pl.ds(pl.multiple_of(oth * 512 + n * 256, 256), 256)
            out = mm(h[rows, :], wt[1, chans, :], NT).astype(BF)
            rs[q // 2, pl.ds((q % 2) * 8, 8), :, cols] = out.reshape(8, 64, 256)

    def res_own(q):
        rows = pl.ds(q * 512, 512)

        @pl.loop(0, 2)
        def _(n):
            cols = pl.ds(pl.multiple_of(n * 256, 256), 256)
            chans = pl.ds(pl.multiple_of(mine * 512 + n * 256, 256), 256)
            out = mm(h[rows, :], wt[1, chans, :], NT)
            rk[rows, cols] = (out + mixa[mine, rows, cols].astype(F32)).astype(BF)

    def finish_dm(q):
        s, r = q // 2, q % 2
        if r == 0:
            a2a_sent(0, s)
        ycopy(2, q).wait()

        @pl.loop(2 * r, 2 * r + 2)
        def _(jj):
            w, gate = mixer_rows(s, jj)
            rows = pl.ds(pl.multiple_of(s * 1024 + jj * 256, 256), 256)
            slab = pl.ds(jj * 4, 4)
            dm = dmk[rows, :].astype(F32) + dmr[s, slab].astype(F32).reshape(256, 512)
            dm = dm.astype(BF)
            dmr[s, slab] = dm.reshape(4, 64, 512)
            dw = (dm.astype(F32) * gate).reshape(2, 16, 8, 512)
            dw = jnp.concatenate([dw[0], dw[1]], axis=1)
            dms[s, :, pl.ds(pl.multiple_of(jj * 16, 16), 16), :] = dw.astype(BF)

        a2a(2, s, slice(32 * r, 32 * r + 32))

    def finish_grad(s):
        @pl.loop(0, 4)
        def _(jj):
            w, gate = mixer_rows(s, jj)
            slab = pl.ds(jj * 4, 4)
            dm = dmr[s, slab].astype(F32).reshape(256, 512)
            term = dm * w * gate * (1.0 - gate) * gain
            cols = pl.ds(pl.multiple_of(jj * 256, 256), 256)
            out = mm(lt[0, :, cols], ub[s].reshape(1024, 512), TN)
            uv[s, slab] = (out + term).astype(BF).reshape(4, 64, 512)

        return pltpu.make_async_copy(uv.at[s], ig_out.at[s], o_sem.at[s])

    def finish_res(s):
        for q in (2 * s, 2 * s + 1):
            ycopy(3, q).wait()

        @pl.loop(0, 4)
        def _(jj):
            rows = pl.ds(pl.multiple_of(s * 1024 + jj * 256, 256), 256)
            more = rr[s, pl.ds(jj * 4, 4)].astype(F32).reshape(256, 512)
            rk[rows, :] = (rk[rows, :].astype(F32) + more).astype(BF)

        return pltpu.make_async_copy(rk.at[pl.ds(s * 1024, 1024)], res_out.at[s], o_sem.at[2 + s])

    def turn(src):
        for y in range(2):
            for s in range(2):
                @pl.loop(0, 4)
                def _(i):
                    rows = pl.ds(pl.multiple_of(s * 1024 + i * 256, 256), 256)
                    cols = pl.ds(pl.multiple_of(i * 256, 256), 256)
                    lt[y, pl.ds(s * 512, 512), cols] = src[y, rows, :].T

    def weight_grad(g, part):
        rhs = (da, h)[g]
        for y in range(2):
            @pl.loop(0, 2)
            def _(f):
                cols = pl.ds(pl.multiple_of(part * 1024 + f * 512, 512), 512)
                out = mm(lt[y, pl.ds(0, 512), :], rhs[pl.ds(0, 1024), cols])
                out = (out + mm(lt[y, pl.ds(512, 512), :], rhs[pl.ds(1024, 1024), cols])).astype(BF)
                for i in range(8):
                    xi, ci = (i // 2) % 2, i % 2
                    slot = ci * 512 + xi * 256 + (i // 4) * 128 + y * 64
                    wt[g, pl.ds(slot, 64), cols] = out[i * 64 : i * 64 + 64]

    def give(credit):
        for peer in (xpeer, cpeer, znear, zfar):
            pl.semaphore_signal(credit, inc=1, device_id=seqdev(peer), device_id_type=MESH)

    def add_rows(g, cols, base, off, count):
        @pl.loop(0, count)
        def _(i):
            rows = pl.ds(pl.multiple_of(base + i * 64, 64), 64)
            more = da[pl.ds(pl.multiple_of(off + i * 64, 64), 64), cols].astype(F32)
            wt[g, rows, cols] = (wt[g, rows, cols].astype(F32) + more).astype(BF)

    def halving(g, part, step):
        bits = (cc, xc, odd, high)
        partner = (cpeer, xpeer, znear, zfar)
        size = 512 >> step
        keep = 0
        for k in range(step):
            keep = keep + bits[k] * (512 >> k)
        send = keep + (1 - bits[step]) * size
        keep = keep + bits[step] * size
        land = 2048 - (2048 >> step) + g * size
        cols = pl.ds(part * 1024, 1024)
        copy = remote(
            wt.at[g, pl.ds(send, size), cols], da.at[pl.ds(land, size), cols],
            g_send.at[step, 2 * g + part], g_recv.at[step, 2 * g + part], seqdev(partner[step]),
        )
        return copy, keep, land, size, cols

    def scatter_step(g, part, step):
        if step > 0:
            copy, keep, land, size, cols = halving(g, part, step - 1)
            copy.wait()
            if step < 4:
                add_rows(g, cols, keep, land, size // 64)
            else:
                out = gi_out if g == 0 else go_out
                own = wt[g, pl.ds(pl.multiple_of(keep, 64), 64), cols].astype(F32)
                out[:, cols] = (own + da[pl.ds(land, 64), cols].astype(F32)) * (1.0 / 128)
        if step < 4:
            halving(g, part, step)[0].start()

    plain = (((1,), (0,)), ((), ()))

    def build_pick():
        @pl.loop(0, 4)
        def _(t):
            row = lax.broadcasted_iota(jnp.int32, (256, 1024), 0) + t * 256
            col = lax.broadcasted_iota(jnp.int32, (256, 1024), 1)
            want = (row & 7) * 128 + (row >> 3)
            rows = pl.ds(pl.multiple_of(1024 + t * 256, 256), 256)
            da[rows, pl.ds(0, 1024)] = jnp.where(col == want, 1.0, 0.0).astype(BF)

    def pick_rows(t):
        return da[pl.ds(pl.multiple_of(1024 + t * 256, 256), 256), pl.ds(0, 1024)]

    def first(s):
        for m in range(8):
            rows = pl.ds(m * 128, 128)
            h[rows, pl.ds(0, 512)] = mm(ff[m], x[s, rows, :]).astype(BF)

        @pl.loop(0, 4)
        def _(t):
            out = mm(pick_rows(t), h[pl.ds(0, 1024), pl.ds(0, 512)])
            ub[s, pl.ds(t * 4, 4)] = out.astype(BF).reshape(4, 64, 512)

    def build_second():
        for fac, rows in ((ff, 0), (sf, 1024)):
            da[pl.ds(rows, 1024), pl.ds(1024, 1024)] = jnp.zeros((1024, 1024), BF)
            for m in range(8):
                da[pl.ds(rows + m * 128, 128), pl.ds(1024 + m * 128, 128)] = fac[m]

        @pl.loop(0, 4)
        def _(t):
            rows = pl.ds(pl.multiple_of(t * 256, 256), 256)
            lt[0, rows, :] = mm(pick_rows(t), da[pl.ds(0, 1024), pl.ds(1024, 1024)]).astype(BF)
            h[rows, pl.ds(1024, 1024)] = mm(pick_rows(t), da[pl.ds(1024, 1024), pl.ds(1024, 1024)]).astype(BF)

        @pl.loop(0, 4)
        def _(t):
            row = lax.broadcasted_iota(jnp.int32, (1024, 256), 0)
            col = lax.broadcasted_iota(jnp.int32, (1024, 256), 1) + t * 256
            want = ((col >> 3) & 7) * 128 + (col >> 6) * 8 + (col & 7)
            pick = jnp.where(row == want, 1.0, 0.0).astype(BF)
            cols = pl.ds(pl.multiple_of(t * 256, 256), 256)
            for r in range(2):
                rows = pl.ds(r * 512, 512)
                bs[rows, cols] = mm(h[rows, pl.ds(1024, 1024)], pick).astype(BF)

    build_pick()
    loads[0].wait()
    loads[1].wait()
    first(0)
    pl.semaphore_wait(barrier, 16)
    a2a(0, 0)
    loads[3].wait()
    loads[4].wait()
    gather_own()
    loads[5].wait()
    loads[6].wait()
    for q in range(4):
        ycopy(0, q).start()
    loads[2].wait()
    loads[7].wait()
    first(1)
    build_second()
    hold = pltpu.make_async_copy(lt.at[0], bf_hold, ld.at[0])
    hold.start()
    a2a_recv(0, 0)
    big(wb, bs, uv, 0, plain)
    a2a(1, 0)
    gather_far()
    a2a(0, 1)
    gather_mid()
    a2a_recv(1, 0)
    gate_chunk(0)
    gate_chunk(1)
    gather_last()
    a2a_recv(0, 1)
    big(wb, bs, uv, 1, plain)
    a2a(1, 1)
    for q in range(4):
        ycopy(0, q).wait()
    gather_done()
    ycopy(1, 0).wait()
    mlp(0)
    ycopy(1, 1).wait()
    mlp(1)
    own_dm(0)
    own_dm(1)
    finish_dm(0)
    a2a_recv(1, 1)
    gate_chunk(2)
    res_own(0)
    finish_dm(1)
    gate_chunk(3)
    res_own(1)
    res_part(0)
    res_part(1)
    ycopy(1, 2).wait()
    mlp(2)
    own_dm(2)
    res_own(2)
    a2a_recv(2, 0)
    a2a_sent(1, 0)
    big(wb, bs, uv, 0, TN)
    a2a(3, 0)
    ycopy(1, 3).wait()
    mlp(3)
    own_dm(3)
    finish_dm(2)
    for k in range(5):
        gathered(k, w_send)
    hold.wait()
    turn(mixa)
    weight_grad(0, 0)
    give(credit_a)
    weight_grad(0, 1)
    give(credit_b)
    pl.semaphore_wait(credit_a, 4)
    scatter_step(0, 0, 0)
    finish_dm(3)
    pl.semaphore_wait(credit_b, 4)
    scatter_step(0, 1, 0)
    scatter_step(0, 0, 1)
    res_part(2)
    res_part(3)
    res_own(3)
    scatter_step(0, 1, 1)
    for q in range(4):
        ycopy(3, q).start()
    turn(cota)
    weight_grad(1, 0)
    scatter_step(1, 0, 0)
    weight_grad(1, 1)
    scatter_step(1, 1, 0)
    unhold = pltpu.make_async_copy(bf_hold, lt.at[0], ld.at[0])
    unhold.start()
    scatter_step(1, 0, 1)
    scatter_step(1, 1, 1)
    a2a_recv(2, 1)
    a2a_sent(1, 1)
    big(wb, bs, uv, 1, TN)
    a2a(3, 1)
    scatter_step(0, 0, 2)
    scatter_step(0, 1, 2)
    unhold.wait()
    a2a_recv(3, 0)
    outs = [finish_grad(0)]
    outs[0].start()
    scatter_step(0, 0, 3)
    scatter_step(0, 1, 3)
    scatter_step(1, 0, 2)
    for s in range(2):
        outs.append(finish_res(s))
        outs[-1].start()
    scatter_step(1, 1, 2)
    scatter_step(0, 0, 4)
    scatter_step(0, 1, 4)
    scatter_step(1, 0, 3)
    a2a_recv(3, 1)
    outs.append(finish_grad(1))
    outs[-1].start()
    scatter_step(1, 1, 3)
    scatter_step(1, 0, 4)
    scatter_step(1, 1, 4)
    for kind in (2, 3):
        for s in range(2):
            a2a_sent(kind, s)
    for c in outs:
        c.wait()


def fused(
    inputs, first_factor, second_factor, gate_scale, gate_bias, in_weight, out_weight, cotangent
):
    count, rows, chan = inputs.shape
    hidden = in_weight.shape[1]
    anyspace = pl.BlockSpec(memory_space=pl.ANY)
    vmem = pl.BlockSpec(memory_space=pltpu.VMEM)
    cells = (2, 16, 64, 512)
    dma = pltpu.SemaphoreType.DMA
    buf = pltpu.VMEM
    res, ig, gi, go, _ = pl.pallas_call(
        kernel,
        out_shape=(
            jax.ShapeDtypeStruct((2, 1024, 512), BF),
            jax.ShapeDtypeStruct(cells, BF),
            jax.ShapeDtypeStruct((64, hidden), F32),
            jax.ShapeDtypeStruct((64, hidden), F32),
            jax.ShapeDtypeStruct((1024, 1024), BF),
        ),
        in_specs=[anyspace] * 4 + [vmem] * 2 + [anyspace] * 2,
        out_specs=(anyspace, anyspace, vmem, vmem, anyspace),
        scratch_shapes=[
            buf((2, 1024, 512), BF),
            buf(first_factor.shape, BF),
            buf(second_factor.shape, BF),
            buf((1024, 1024), BF),
            buf((2, 1024, 2048), BF),
            buf(cells, BF),
            buf(cells, BF),
            buf(cells, BF),
            buf(cells, BF),
            buf((2, 2048, 512), BF),
            buf((2, 2048, 512), BF),
            buf((2048, 2048), BF),
            buf((2048, 2048), BF),
            buf(cells, BF),
            buf(cells, BF),
            buf((2048, 512), BF),
            buf(cells, BF),
            buf(cells, BF),
            buf((2048, 512), BF),
            buf((2, 1024, 1024), BF),
            dma((8,)),
            dma((4, 2)),
            dma((4, 2)),
            dma((4, 4)),
            dma((4, 4)),
            dma((5, 2)),
            dma((5, 2)),
            dma((4, 4)),
            dma((4, 4)),
            dma((4,)),
            pltpu.SemaphoreType.REGULAR,
            pltpu.SemaphoreType.REGULAR,
        ],
        compiler_params=pltpu.CompilerParams(
            collective_id=0, has_side_effects=True, vmem_limit_bytes=63 * MIB
        ),
        cost_estimate=pl.CostEstimate(flops=60 * 10**9, bytes_accessed=20 * MIB, transcendentals=0),
    )(
        inputs,
        cotangent,
        first_factor,
        second_factor,
        gate_scale.reshape(1, chan),
        gate_bias.reshape(1, chan),
        in_weight,
        out_weight.T,
    )
    return res, ig.reshape(inputs.shape), gi, go.T


def solution(mesh):
    in_specs = (
        P(None, "seq", "fsdp"),
        P("seq", None, None),
        P("seq", None, None),
        P("fsdp"),
        P("fsdp"),
        P("seq", "fsdp"),
        P("fsdp", "seq"),
        P(None, "seq", "fsdp"),
    )
    out_specs = (P(None, "seq", "fsdp"), P(None, "seq", "fsdp"), P("seq", "fsdp"), P("fsdp", "seq"))
    sizes = (mesh.shape["seq"], mesh.shape["fsdp"])
    part = fused if sizes == (16, 2) else body
    return jax.shard_map(part, mesh=mesh, in_specs=in_specs, out_specs=out_specs, check_vma=False)
```

```python
import functools

import jax
import jax.numpy as jnp
from jax import lax
from jax.experimental import pallas as pl
from jax.experimental.pallas import tpu as pltpu
from jax.sharding import PartitionSpec as P

BF = jnp.bfloat16
F32 = jnp.float32


def body(
    inputs, first_factor, second_factor, gate_scale, gate_bias, in_weight, out_weight, cotangent
):
    seq_count, tok_rows, chan = inputs.shape
    blocks, size, _ = first_factor.shape
    offs = second_factor.shape[0]
    owners = lax.axis_size("seq")
    groups = lax.axis_size("fsdp")
    mine = lax.axis_index("fsdp")
    width = chan * groups
    gain = gate_scale.reshape(1, 1, chan)
    shift = gate_bias.reshape(1, 1, chan)

    def swap(x):
        return lax.ppermute(x, "fsdp", [(0, 1), (1, 0)])

    def gather_cols(x):
        if groups != 2:
            return lax.all_gather(x, "fsdp", axis=1, tiled=True)
        return place(x, swap(x))

    def place(x, y):
        first = mine == 0
        return jnp.concatenate([jnp.where(first, x, y), jnp.where(first, y, x)], axis=1)

    def reduce_cols(left, weight, dims):
        if groups != 2:
            full = lax.dot_general(left, weight, dims, preferred_element_type=F32)
            got = lax.all_to_all(full, "fsdp", split_axis=1, concat_axis=0, tiled=True)
            return jnp.sum(got.reshape(groups, -1, chan), axis=0), None
        other = lax.dynamic_slice_in_dim(weight, (1 - mine) * chan, chan, 0)
        own = lax.dynamic_slice_in_dim(weight, mine * chan, chan, 0)
        sent = swap(lax.dot_general(left, other, dims, preferred_element_type=F32).astype(BF))
        kept = lax.dot_general(left, own, dims, preferred_element_type=F32)
        return kept, sent

    def exchange(x):
        return lax.all_to_all(x, "seq", split_axis=0, concat_axis=0, tiled=True)

    bar = lax.optimization_barrier
    nt = (((1,), (1,)), ((), ()))
    tn = (((0,), (0,)), ((), ()))
    seqs = range(seq_count)
    last = seq_count - 1
    both = jnp.stack([in_weight, out_weight.T], axis=0)
    both = lax.all_gather(both, "seq", axis=1, tiled=True)
    full_in, full_out = both[0], both[1]

    sources = [inputs[s].reshape(blocks, size, chan) for s in seqs]
    cots = [cotangent[s] for s in seqs]
    cot_all = [gather_cols(c) for c in cots]

    source = inputs.reshape(seq_count, blocks, size, chan)
    u = jnp.einsum("mkn,smnc->mksc", first_factor, source, preferred_element_type=F32)
    u = u.astype(BF).reshape(blocks, owners, offs, seq_count, chan).transpose(1, 3, 0, 2, 4)
    u, *cot_all = bar((exchange(u), *cot_all))
    turned = [u[:, s].reshape(owners * blocks, offs, chan) for s in seqs]
    mixes, seconds, mixed_all = [], [], []
    for s in seqs:
        w = jnp.einsum("kjm,mkc->kjc", second_factor, turned[s], preferred_element_type=F32)
        w = w.astype(BF).reshape(offs, owners, blocks, chan).transpose(1, 0, 2, 3)
        w = exchange(w)
        if s > 0:
            w, mixed_all[s - 1] = bar((w, mixed_all[s - 1]))
        w = bar(w.reshape(size, blocks, chan).transpose(1, 0, 2))
        gate = jax.nn.sigmoid(gain * sources[s].astype(F32) + shift)
        seconds.append(w)
        mixes.append((gate * w.astype(F32)).astype(BF).reshape(tok_rows, chan))
        if s < last or groups != 2:
            mixed_all.append(gather_cols(mixes[s]))
    swapped = swap(mixes[last]) if groups == 2 else None

    das, hs, sums = [], [], []
    for s in seqs:
        pre = jnp.dot(mixed_all[s], full_in, preferred_element_type=F32)
        dh = jnp.dot(cot_all[s], full_out, preferred_element_type=F32)
        sig = jax.nn.sigmoid(pre)
        hs.append((pre * sig).astype(BF))
        da = (dh * sig * (1.0 + pre * (1.0 - sig))).astype(BF)
        if s < last and groups == 2:
            da, swapped = bar((da, swapped))
            mixed_all.append(place(mixes[last], swapped))
        if s > 0 and groups == 2:
            kept, sent = sums[s - 1]
            da, sent = bar((da, sent))
            sums[s - 1] = kept, sent
        das.append(da)
        sums.append(reduce_cols(da, full_in, nt))

    out_term = sum(lax.dot_general(cot_all[s], hs[s], tn, preferred_element_type=F32) for s in seqs)
    out_term = out_term.astype(BF)
    if groups == 2:
        kept, sent = sums[last]
        sent, out_term = bar((sent, out_term))
        sums[last] = kept, sent
    grad_out = lax.psum_scatter(out_term, "seq", scatter_dimension=0, tiled=True)
    dms, dws, gates = [], [], []
    for s in seqs:
        gate = jax.nn.sigmoid(gain * sources[s].astype(F32) + shift)
        kept, sent = sums[s]
        dm = cots[s].astype(F32) + (kept if sent is None else kept + sent.astype(F32))
        dm = dm.astype(BF).reshape(blocks, size, chan)
        dw = (dm.astype(F32) * gate).astype(BF)
        dms.append(dm)
        gates.append(gate)
        dws.append(dw.reshape(blocks, owners, offs, chan).transpose(1, 0, 2, 3))
    dw = exchange(jnp.stack(dws, axis=1))
    in_term = sum(lax.dot_general(mixed_all[s], das[s], tn, preferred_element_type=F32) for s in seqs)
    dw, in_term = bar((dw, in_term.astype(BF)))
    scale = 1.0 / size
    grad_in = lax.psum_scatter(in_term, "seq", scatter_dimension=0, tiled=True)

    branches = [list(reduce_cols(hs[s], full_out, nt)) for s in seqs]
    dw = dw.transpose(1, 0, 2, 3, 4).reshape(seq_count, owners * blocks, offs, chan)
    du = jnp.einsum("kjm,sjkc->kmsc", second_factor, dw, preferred_element_type=F32)
    du = du.astype(BF).reshape(offs, owners, blocks, seq_count, chan).transpose(1, 3, 0, 2, 4)
    du = exchange(du)
    if groups == 2:
        du, *sents = bar((du, *[pair[1] for pair in branches]))
        branches = [[pair[0], sent] for pair, sent in zip(branches, sents)]
    grads, results = [], []
    for s in seqs:
        rows = du[:, s].reshape(size, blocks, chan)
        back = jnp.einsum("mkn,kmc->mnc", first_factor, rows, preferred_element_type=F32)
        gate = gates[s]
        gate_term = dms[s].astype(F32) * seconds[s].astype(F32) * gate * (1.0 - gate) * gain
        grads.append((back + gate_term).astype(BF).reshape(tok_rows, chan))
        kept, sent = branches[s]
        branch = kept if sent is None else kept + sent.astype(F32)
        results.append((mixes[s].astype(F32) + branch).astype(BF))
    return (
        jnp.stack(results),
        jnp.stack(grads),
        grad_in.astype(F32) * scale,
        grad_out.astype(F32).T * scale,
    )


MESH = pl.DeviceIdType.MESH
NT = (((1,), (1,)), ((), ()))
TN = (((0,), (0,)), ((), ()))
MIB = 1024 * 1024


def mm(a, b, dims=(((1,), (0,)), ((), ()))):
    return lax.dot_general(a, b, dims, preferred_element_type=F32)


def kernel(
    x_in, cot_in, f_in, s_in, gain_ref, shift_ref, wi_in, wo_in,
    res_out, ig_out, gi_out, go_out, bf_hold,
    x, ff, sf, bs, wt, ub, uv, wb, wv, cota, mixa, h, da, dms, dmr, dmk, rs, rr, rk, lt,
    ld, a_send, a_recv, y_send, y_recv, w_send, w_recv, g_send, g_recv, o_sem, credit_a, credit_b,
):
    me = lax.axis_index("seq")
    mine = lax.axis_index("fsdp")
    oth = 1 - mine
    zc, xc, cc = me // 4, (me // 2) % 2, me % 2
    xpeer = zc * 4 + (1 - xc) * 2 + cc
    cpeer = zc * 4 + xc * 2 + (1 - cc)

    odd, high = zc % 2, zc // 2
    znear = (zc + 1 - 2 * odd) * 4 + xc * 2 + cc
    zfar = ((zc + 2) % 4) * 4 + xc * 2 + cc

    def seqdev(i):
        return {"seq": i}

    ydev = {"fsdp": oth}

    def remote(src, dst, ss, rs_, dev):
        return pltpu.make_async_remote_copy(
            src_ref=src, dst_ref=dst, send_sem=ss, recv_sem=rs_, device_id=dev, device_id_type=MESH
        )

    def drain(ref, sem):
        pltpu.make_async_copy(ref, ref, sem).wait()

    loads = [
        pltpu.make_async_copy(x_in.at[0], x.at[0], ld.at[0]),
        pltpu.make_async_copy(f_in, ff, ld.at[1]),
        pltpu.make_async_copy(x_in.at[1], x.at[1], ld.at[2]),
        pltpu.make_async_copy(wi_in, wt.at[0, pl.ds(me * 64, 64)], ld.at[3]),
        pltpu.make_async_copy(wo_in, wt.at[1, pl.ds(me * 64, 64)], ld.at[4]),
        pltpu.make_async_copy(cot_in.at[0], cota.at[mine, pl.ds(0, 1024)], ld.at[5]),
        pltpu.make_async_copy(cot_in.at[1], cota.at[mine, pl.ds(1024, 1024)], ld.at[6]),
        pltpu.make_async_copy(s_in, sf, ld.at[7]),
    ]
    barrier = pltpu.get_barrier_semaphore()

    @pl.loop(1, 16)
    def _(d):
        pl.semaphore_signal(barrier, inc=1, device_id=seqdev((me + d) % 16), device_id_type=MESH)

    pl.semaphore_signal(barrier, inc=1, device_id=ydev, device_id_type=MESH)
    for c in loads:
        c.start()

    def yview(ref, q):
        return ref.at[mine, pl.ds(q * 512, 512)]

    def ycopy(kind, q):
        if kind == 0:
            a = b = yview(cota, q)
        elif kind == 1:
            a = b = yview(mixa, q)
        else:
            view = (q // 2, pl.ds((q % 2) * 8, 8))
            a, b = rs.at[view], (dmr if kind == 2 else rr).at[view]
        return remote(a, b, y_send.at[kind, q], y_recv.at[kind, q], ydev)

    pairs = [(ub, uv), (wb, wv), (dms, uv), (wb, ub)]

    def a2a(kind, s, rows=slice(0, 64)):
        src, dst = pairs[kind]
        rows = pl.ds(rows.start, rows.stop - rows.start)
        pltpu.make_async_copy(src.at[s, me, rows], dst.at[s, me, rows], a_recv.at[kind, s]).start()

        @pl.loop(1, 16)
        def _(d):
            e = 16 - d
            far = ((high + e // 8) % 2) * 2 + (odd + (e // 4) % 2) % 2
            peer = far * 4 + ((xc + (e // 2) % 2) % 2) * 2 + (cc + e % 2) % 2
            remote(src.at[s, peer, rows], dst.at[s, me, rows], a_send.at[kind, s], a_recv.at[kind, s], seqdev(peer)).start()

    def a2a_recv(kind, s):
        drain(pairs[kind][1].at[s], a_recv.at[kind, s])

    def a2a_sent(kind, s):
        drain(pairs[kind][0].at[s, pl.ds(0, 15)], a_send.at[kind, s])

    FAR, NEAR, NEXT, ACROSS, CORE = range(5)
    peers = (zfar, znear, znear, xpeer, cpeer)
    counts = (64, 64, 64, 256, 512)

    def shard(owner, stages):
        for g in range(2):
            rows = wt.at[g, pl.ds(owner * 64, 64)]
            for k in stages:
                remote(rows, rows, w_send.at[k, g], w_recv.at[k, g], seqdev(peers[k])).start()

    def gathered(k, sems):
        for g in range(2):
            drain(wt.at[0, pl.ds(0, counts[k])], sems.at[k, g])

    def gather_own():
        shard(me, (FAR, NEAR, ACROSS, CORE))

    def gather_far():
        gathered(NEAR, w_recv)
        shard(znear, (ACROSS, CORE))
        gathered(FAR, w_recv)
        shard(zfar, (NEXT, ACROSS, CORE))

    def gather_mid():
        gathered(NEXT, w_recv)
        shard((znear + 8) % 16, (ACROSS, CORE))

    def gather_last():
        gathered(ACROSS, w_recv)

        @pl.loop(0, 4)
        def _(i):
            shard(i * 4 + (1 - xc) * 2 + cc, (CORE,))

    def gather_done():
        gathered(CORE, w_recv)

    gain = gain_ref[...]
    shift = shift_ref[...]

    def big(dst, mat, src, s, dims):
        @pl.loop(0, 4)
        def _(t):
            if dims is TN:
                lhs = mat[:, pl.ds(pl.multiple_of(t * 256, 256), 256)]
            else:
                lhs = mat[pl.ds(pl.multiple_of(t * 256, 256), 256), :]
            out = mm(lhs, src[s].reshape(1024, 512), dims if dims is TN else (((1,), (0,)), ((), ())))
            dst[s, pl.ds(t * 4, 4)] = out.astype(BF).reshape(4, 64, 512)

    def mixer_rows(s, jj):
        w = wv[s, :, pl.ds(pl.multiple_of(jj * 16, 16), 16), :].astype(F32).reshape(16, 2, 8, 512)
        w = jnp.concatenate([w[:, 0].reshape(128, 512), w[:, 1].reshape(128, 512)], axis=0)
        rows = pl.ds(pl.multiple_of(jj * 256, 256), 256)
        gate = jax.nn.sigmoid(gain * x[s, rows, :].astype(F32) + shift)
        return w, gate

    def gate_chunk(q):
        s = q // 2

        @pl.loop((q % 2) * 2, (q % 2) * 2 + 2)
        def _(jj):
            w, gate = mixer_rows(s, jj)
            rows = pl.ds(pl.multiple_of(s * 1024 + jj * 256, 256), 256)
            mixa[mine, rows, :] = (gate * w).astype(BF)

        ycopy(1, q).start()

    def mlp(q):
        rows = pl.ds(q * 512, 512)
        s = q // 2

        @pl.loop(0, 8)
        def _(f):
            cols = pl.ds(pl.multiple_of(f * 256, 256), 256)
            pre = mm(mixa[0, rows, :], wt[0, pl.ds(0, 512), cols]) + mm(mixa[1, rows, :], wt[0, pl.ds(512, 512), cols])
            dh = mm(cota[0, rows, :], wt[1, pl.ds(0, 512), cols]) + mm(cota[1, rows, :], wt[1, pl.ds(512, 512), cols])
            sig = jax.nn.sigmoid(pre)
            h[rows, cols] = (pre * sig).astype(BF)
            da[rows, cols] = (dh * sig * (1.0 + pre * (1.0 - sig))).astype(BF)

        @pl.loop(0, 2)
        def _(n):
            cols = pl.ds(pl.multiple_of(n * 256, 256), 256)
            chans = pl.ds(pl.multiple_of(oth * 512 + n * 256, 256), 256)
            out = mm(da[rows, :], wt[0, chans, :], NT)
            rs[s, pl.ds((q % 2) * 8, 8), :, cols] = out.astype(BF).reshape(8, 64, 256)

        ycopy(2, q).start()

    def own_dm(q):
        rows = pl.ds(q * 512, 512)

        @pl.loop(0, 2)
        def _(n):
            cols = pl.ds(pl.multiple_of(n * 256, 256), 256)
            chans = pl.ds(pl.multiple_of(mine * 512 + n * 256, 256), 256)
            out = mm(da[rows, :], wt[0, chans, :], NT)
            dmk[rows, cols] = (out + cota[mine, rows, cols].astype(F32)).astype(BF)

    def res_part(q):
        rows = pl.ds(q * 512, 512)

        @pl.loop(0, 2)
        def _(n):
            cols = pl.ds(pl.multiple_of(n * 256, 256), 256)
            chans = pl.ds(pl.multiple_of(oth * 512 + n * 256, 256), 256)
            out = mm(h[rows, :], wt[1, chans, :], NT).astype(BF)
            rs[q // 2, pl.ds((q % 2) * 8, 8), :, cols] = out.reshape(8, 64, 256)

    def res_own(q):
        rows = pl.ds(q * 512, 512)

        @pl.loop(0, 2)
        def _(n):
            cols = pl.ds(pl.multiple_of(n * 256, 256), 256)
            chans = pl.ds(pl.multiple_of(mine * 512 + n * 256, 256), 256)
            out = mm(h[rows, :], wt[1, chans, :], NT)
            rk[rows, cols] = (out + mixa[mine, rows, cols].astype(F32)).astype(BF)

    def finish_dm(q):
        s, r = q // 2, q % 2
        if r == 0:
            a2a_sent(0, s)
        ycopy(2, q).wait()

        @pl.loop(2 * r, 2 * r + 2)
        def _(jj):
            w, gate = mixer_rows(s, jj)
            rows = pl.ds(pl.multiple_of(s * 1024 + jj * 256, 256), 256)
            slab = pl.ds(jj * 4, 4)
            dm = dmk[rows, :].astype(F32) + dmr[s, slab].astype(F32).reshape(256, 512)
            dm = dm.astype(BF)
            dmr[s, slab] = dm.reshape(4, 64, 512)
            dw = (dm.astype(F32) * gate).reshape(2, 16, 8, 512)
            dw = jnp.concatenate([dw[0], dw[1]], axis=1)
            dms[s, :, pl.ds(pl.multiple_of(jj * 16, 16), 16), :] = dw.astype(BF)

        a2a(2, s, slice(32 * r, 32 * r + 32))

    def finish_grad(s):
        @pl.loop(0, 4)
        def _(jj):
            w, gate = mixer_rows(s, jj)
            slab = pl.ds(jj * 4, 4)
            dm = dmr[s, slab].astype(F32).reshape(256, 512)
            term = dm * w * gate * (1.0 - gate) * gain
            cols = pl.ds(pl.multiple_of(jj * 256, 256), 256)
            out = mm(lt[0, :, cols], ub[s].reshape(1024, 512), TN)
            uv[s, slab] = (out + term).astype(BF).reshape(4, 64, 512)

        return pltpu.make_async_copy(uv.at[s], ig_out.at[s], o_sem.at[s])

    def finish_res(s):
        for q in (2 * s, 2 * s + 1):
            ycopy(3, q).wait()

        @pl.loop(0, 4)
        def _(jj):
            rows = pl.ds(pl.multiple_of(s * 1024 + jj * 256, 256), 256)
            more = rr[s, pl.ds(jj * 4, 4)].astype(F32).reshape(256, 512)
            rk[rows, :] = (rk[rows, :].astype(F32) + more).astype(BF)

        return pltpu.make_async_copy(rk.at[pl.ds(s * 1024, 1024)], res_out.at[s], o_sem.at[2 + s])

    def turn(src):
        for y in range(2):
            for s in range(2):
                @pl.loop(0, 4)
                def _(i):
                    rows = pl.ds(pl.multiple_of(s * 1024 + i * 256, 256), 256)
                    cols = pl.ds(pl.multiple_of(i * 256, 256), 256)
                    lt[y, pl.ds(s * 512, 512), cols] = src[y, rows, :].T

    def weight_grad(g, part):
        rhs = (da, h)[g]
        for y in range(2):
            @pl.loop(0, 2)
            def _(f):
                cols = pl.ds(pl.multiple_of(part * 1024 + f * 512, 512), 512)
                out = mm(lt[y, pl.ds(0, 512), :], rhs[pl.ds(0, 1024), cols])
                out = (out + mm(lt[y, pl.ds(512, 512), :], rhs[pl.ds(1024, 1024), cols])).astype(BF)
                for i in range(8):
                    xi, ci = (i // 2) % 2, i % 2
                    slot = ci * 512 + xi * 256 + (i // 4) * 128 + y * 64
                    wt[g, pl.ds(slot, 64), cols] = out[i * 64 : i * 64 + 64]

    def give(credit):
        for peer in (xpeer, cpeer, znear, zfar):
            pl.semaphore_signal(credit, inc=1, device_id=seqdev(peer), device_id_type=MESH)

    def add_rows(g, cols, base, off, count):
        @pl.loop(0, count)
        def _(i):
            rows = pl.ds(pl.multiple_of(base + i * 64, 64), 64)
            more = da[pl.ds(pl.multiple_of(off + i * 64, 64), 64), cols].astype(F32)
            wt[g, rows, cols] = (wt[g, rows, cols].astype(F32) + more).astype(BF)

    def halving(g, part, step):
        bits = (cc, xc, odd, high)
        partner = (cpeer, xpeer, znear, zfar)
        size = 512 >> step
        keep = 0
        for k in range(step):
            keep = keep + bits[k] * (512 >> k)
        send = keep + (1 - bits[step]) * size
        keep = keep + bits[step] * size
        land = 2048 - (2048 >> step) + g * size
        cols = pl.ds(part * 1024, 1024)
        copy = remote(
            wt.at[g, pl.ds(send, size), cols], da.at[pl.ds(land, size), cols],
            g_send.at[step, 2 * g + part], g_recv.at[step, 2 * g + part], seqdev(partner[step]),
        )
        return copy, keep, land, size, cols

    def scatter_step(g, part, step):
        if step > 0:
            copy, keep, land, size, cols = halving(g, part, step - 1)
            copy.wait()
            if step < 4:
                add_rows(g, cols, keep, land, size // 64)
            else:
                out = gi_out if g == 0 else go_out
                own = wt[g, pl.ds(pl.multiple_of(keep, 64), 64), cols].astype(F32)
                out[:, cols] = (own + da[pl.ds(land, 64), cols].astype(F32)) * (1.0 / 128)
        if step < 4:
            halving(g, part, step)[0].start()

    plain = (((1,), (0,)), ((), ()))

    def build_pick():
        @pl.loop(0, 4)
        def _(t):
            row = lax.broadcasted_iota(jnp.int32, (256, 1024), 0) + t * 256
            col = lax.broadcasted_iota(jnp.int32, (256, 1024), 1)
            want = (row & 7) * 128 + (row >> 3)
            rows = pl.ds(pl.multiple_of(1024 + t * 256, 256), 256)
            da[rows, pl.ds(0, 1024)] = jnp.where(col == want, 1.0, 0.0).astype(BF)

    def pick_rows(t):
        return da[pl.ds(pl.multiple_of(1024 + t * 256, 256), 256), pl.ds(0, 1024)]

    def first(s):
        for m in range(8):
            rows = pl.ds(m * 128, 128)
            h[rows, pl.ds(0, 512)] = mm(ff[m], x[s, rows, :]).astype(BF)

        @pl.loop(0, 4)
        def _(t):
            out = mm(pick_rows(t), h[pl.ds(0, 1024), pl.ds(0, 512)])
            ub[s, pl.ds(t * 4, 4)] = out.astype(BF).reshape(4, 64, 512)

    def build_second():
        for fac, rows in ((ff, 0), (sf, 1024)):
            da[pl.ds(rows, 1024), pl.ds(1024, 1024)] = jnp.zeros((1024, 1024), BF)
            for m in range(8):
                da[pl.ds(rows + m * 128, 128), pl.ds(1024 + m * 128, 128)] = fac[m]

        @pl.loop(0, 4)
        def _(t):
            rows = pl.ds(pl.multiple_of(t * 256, 256), 256)
            lt[0, rows, :] = mm(pick_rows(t), da[pl.ds(0, 1024), pl.ds(1024, 1024)]).astype(BF)
            h[rows, pl.ds(1024, 1024)] = mm(pick_rows(t), da[pl.ds(1024, 1024), pl.ds(1024, 1024)]).astype(BF)

        @pl.loop(0, 4)
        def _(t):
            row = lax.broadcasted_iota(jnp.int32, (1024, 256), 0)
            col = lax.broadcasted_iota(jnp.int32, (1024, 256), 1) + t * 256
            want = ((col >> 3) & 7) * 128 + (col >> 6) * 8 + (col & 7)
            pick = jnp.where(row == want, 1.0, 0.0).astype(BF)
            cols = pl.ds(pl.multiple_of(t * 256, 256), 256)
            for r in range(2):
                rows = pl.ds(r * 512, 512)
                bs[rows, cols] = mm(h[rows, pl.ds(1024, 1024)], pick).astype(BF)

    build_pick()
    loads[0].wait()
    loads[1].wait()
    first(0)
    loads[3].wait()
    loads[4].wait()
    pl.semaphore_wait(barrier, 16)
    gather_own()
    a2a(0, 0)
    loads[5].wait()
    loads[6].wait()
    for q in range(4):
        ycopy(0, q).start()
    loads[2].wait()
    loads[7].wait()
    first(1)
    build_second()
    hold = pltpu.make_async_copy(lt.at[0], bf_hold, ld.at[0])
    hold.start()
    gather_far()
    a2a_recv(0, 0)
    big(wb, bs, uv, 0, plain)
    a2a(1, 0)
    a2a(0, 1)
    gather_mid()
    a2a_recv(1, 0)
    gate_chunk(0)
    gate_chunk(1)
    gather_last()
    a2a_recv(0, 1)
    big(wb, bs, uv, 1, plain)
    a2a(1, 1)
    for q in range(4):
        ycopy(0, q).wait()
    gather_done()
    ycopy(1, 0).wait()
    mlp(0)
    ycopy(1, 1).wait()
    mlp(1)
    own_dm(0)
    own_dm(1)
    finish_dm(0)
    a2a_recv(1, 1)
    gate_chunk(2)
    res_own(0)
    finish_dm(1)
    gate_chunk(3)
    res_own(1)
    res_part(0)
    res_part(1)
    ycopy(1, 2).wait()
    mlp(2)
    own_dm(2)
    res_own(2)
    a2a_recv(2, 0)
    a2a_sent(1, 0)
    big(wb, bs, uv, 0, TN)
    a2a(3, 0)
    ycopy(1, 3).wait()
    mlp(3)
    own_dm(3)
    finish_dm(2)
    for k in range(5):
        gathered(k, w_send)
    hold.wait()
    turn(mixa)
    weight_grad(0, 0)
    give(credit_a)
    weight_grad(0, 1)
    give(credit_b)
    pl.semaphore_wait(credit_a, 4)
    scatter_step(0, 0, 0)
    finish_dm(3)
    pl.semaphore_wait(credit_b, 4)
    scatter_step(0, 1, 0)
    scatter_step(0, 0, 1)
    res_part(2)
    res_part(3)
    res_own(3)
    scatter_step(0, 1, 1)
    for q in range(4):
        ycopy(3, q).start()
    turn(cota)
    weight_grad(1, 0)
    scatter_step(1, 0, 0)
    weight_grad(1, 1)
    scatter_step(1, 1, 0)
    unhold = pltpu.make_async_copy(bf_hold, lt.at[0], ld.at[0])
    unhold.start()
    scatter_step(1, 0, 1)
    scatter_step(1, 1, 1)
    a2a_recv(2, 1)
    a2a_sent(1, 1)
    big(wb, bs, uv, 1, TN)
    a2a(3, 1)
    scatter_step(0, 0, 2)
    scatter_step(0, 1, 2)
    unhold.wait()
    a2a_recv(3, 0)
    outs = [finish_grad(0)]
    outs[0].start()
    scatter_step(0, 0, 3)
    scatter_step(0, 1, 3)
    scatter_step(1, 0, 2)
    for s in range(2):
        outs.append(finish_res(s))
        outs[-1].start()
    scatter_step(1, 1, 2)
    scatter_step(0, 0, 4)
    scatter_step(0, 1, 4)
    scatter_step(1, 0, 3)
    a2a_recv(3, 1)
    outs.append(finish_grad(1))
    outs[-1].start()
    scatter_step(1, 1, 3)
    scatter_step(1, 0, 4)
    scatter_step(1, 1, 4)
    for kind in (2, 3):
        for s in range(2):
            a2a_sent(kind, s)
    for c in outs:
        c.wait()


def fused(
    inputs, first_factor, second_factor, gate_scale, gate_bias, in_weight, out_weight, cotangent
):
    count, rows, chan = inputs.shape
    hidden = in_weight.shape[1]
    anyspace = pl.BlockSpec(memory_space=pl.ANY)
    vmem = pl.BlockSpec(memory_space=pltpu.VMEM)
    cells = (2, 16, 64, 512)
    dma = pltpu.SemaphoreType.DMA
    buf = pltpu.VMEM
    res, ig, gi, go, _ = pl.pallas_call(
        kernel,
        out_shape=(
            jax.ShapeDtypeStruct((2, 1024, 512), BF),
            jax.ShapeDtypeStruct(cells, BF),
            jax.ShapeDtypeStruct((64, hidden), F32),
            jax.ShapeDtypeStruct((64, hidden), F32),
            jax.ShapeDtypeStruct((1024, 1024), BF),
        ),
        in_specs=[anyspace] * 4 + [vmem] * 2 + [anyspace] * 2,
        out_specs=(anyspace, anyspace, vmem, vmem, anyspace),
        scratch_shapes=[
            buf((2, 1024, 512), BF),
            buf(first_factor.shape, BF),
            buf(second_factor.shape, BF),
            buf((1024, 1024), BF),
            buf((2, 1024, 2048), BF),
            buf(cells, BF),
            buf(cells, BF),
            buf(cells, BF),
            buf(cells, BF),
            buf((2, 2048, 512), BF),
            buf((2, 2048, 512), BF),
            buf((2048, 2048), BF),
            buf((2048, 2048), BF),
            buf(cells, BF),
            buf(cells, BF),
            buf((2048, 512), BF),
            buf(cells, BF),
            buf(cells, BF),
            buf((2048, 512), BF),
            buf((2, 1024, 1024), BF),
            dma((8,)),
            dma((4, 2)),
            dma((4, 2)),
            dma((4, 4)),
            dma((4, 4)),
            dma((5, 2)),
            dma((5, 2)),
            dma((4, 4)),
            dma((4, 4)),
            dma((4,)),
            pltpu.SemaphoreType.REGULAR,
            pltpu.SemaphoreType.REGULAR,
        ],
        compiler_params=pltpu.CompilerParams(
            collective_id=0, has_side_effects=True, vmem_limit_bytes=63 * MIB
        ),
        cost_estimate=pl.CostEstimate(flops=60 * 10**9, bytes_accessed=20 * MIB, transcendentals=0),
    )(
        inputs,
        cotangent,
        first_factor,
        second_factor,
        gate_scale.reshape(1, chan),
        gate_bias.reshape(1, chan),
        in_weight,
        out_weight.T,
    )
    return res, ig.reshape(inputs.shape), gi, go.T


def solution(mesh):
    in_specs = (
        P(None, "seq", "fsdp"),
        P("seq", None, None),
        P("seq", None, None),
        P("fsdp"),
        P("fsdp"),
        P("seq", "fsdp"),
        P("fsdp", "seq"),
        P(None, "seq", "fsdp"),
    )
    out_specs = (P(None, "seq", "fsdp"), P(None, "seq", "fsdp"), P("seq", "fsdp"), P("fsdp", "seq"))
    sizes = (mesh.shape["seq"], mesh.shape["fsdp"])
    part = fused if sizes == (16, 2) else body
    return jax.shard_map(part, mesh=mesh, in_specs=in_specs, out_specs=out_specs, check_vma=False)
```

```python
import functools

import jax
import jax.numpy as jnp
from jax import lax
from jax.experimental import pallas as pl
from jax.experimental.pallas import tpu as pltpu
from jax.sharding import PartitionSpec as P

BF = jnp.bfloat16
F32 = jnp.float32


def body(
    inputs, first_factor, second_factor, gate_scale, gate_bias, in_weight, out_weight, cotangent
):
    seq_count, tok_rows, chan = inputs.shape
    blocks, size, _ = first_factor.shape
    offs = second_factor.shape[0]
    owners = lax.axis_size("seq")
    groups = lax.axis_size("fsdp")
    mine = lax.axis_index("fsdp")
    width = chan * groups
    gain = gate_scale.reshape(1, 1, chan)
    shift = gate_bias.reshape(1, 1, chan)

    def swap(x):
        return lax.ppermute(x, "fsdp", [(0, 1), (1, 0)])

    def gather_cols(x):
        if groups != 2:
            return lax.all_gather(x, "fsdp", axis=1, tiled=True)
        return place(x, swap(x))

    def place(x, y):
        first = mine == 0
        return jnp.concatenate([jnp.where(first, x, y), jnp.where(first, y, x)], axis=1)

    def reduce_cols(left, weight, dims):
        if groups != 2:
            full = lax.dot_general(left, weight, dims, preferred_element_type=F32)
            got = lax.all_to_all(full, "fsdp", split_axis=1, concat_axis=0, tiled=True)
            return jnp.sum(got.reshape(groups, -1, chan), axis=0), None
        other = lax.dynamic_slice_in_dim(weight, (1 - mine) * chan, chan, 0)
        own = lax.dynamic_slice_in_dim(weight, mine * chan, chan, 0)
        sent = swap(lax.dot_general(left, other, dims, preferred_element_type=F32).astype(BF))
        kept = lax.dot_general(left, own, dims, preferred_element_type=F32)
        return kept, sent

    def exchange(x):
        return lax.all_to_all(x, "seq", split_axis=0, concat_axis=0, tiled=True)

    bar = lax.optimization_barrier
    nt = (((1,), (1,)), ((), ()))
    tn = (((0,), (0,)), ((), ()))
    seqs = range(seq_count)
    last = seq_count - 1
    both = jnp.stack([in_weight, out_weight.T], axis=0)
    both = lax.all_gather(both, "seq", axis=1, tiled=True)
    full_in, full_out = both[0], both[1]

    sources = [inputs[s].reshape(blocks, size, chan) for s in seqs]
    cots = [cotangent[s] for s in seqs]
    cot_all = [gather_cols(c) for c in cots]

    source = inputs.reshape(seq_count, blocks, size, chan)
    u = jnp.einsum("mkn,smnc->mksc", first_factor, source, preferred_element_type=F32)
    u = u.astype(BF).reshape(blocks, owners, offs, seq_count, chan).transpose(1, 3, 0, 2, 4)
    u, *cot_all = bar((exchange(u), *cot_all))
    turned = [u[:, s].reshape(owners * blocks, offs, chan) for s in seqs]
    mixes, seconds, mixed_all = [], [], []
    for s in seqs:
        w = jnp.einsum("kjm,mkc->kjc", second_factor, turned[s], preferred_element_type=F32)
        w = w.astype(BF).reshape(offs, owners, blocks, chan).transpose(1, 0, 2, 3)
        w = exchange(w)
        if s > 0:
            w, mixed_all[s - 1] = bar((w, mixed_all[s - 1]))
        w = bar(w.reshape(size, blocks, chan).transpose(1, 0, 2))
        gate = jax.nn.sigmoid(gain * sources[s].astype(F32) + shift)
        seconds.append(w)
        mixes.append((gate * w.astype(F32)).astype(BF).reshape(tok_rows, chan))
        if s < last or groups != 2:
            mixed_all.append(gather_cols(mixes[s]))
    swapped = swap(mixes[last]) if groups == 2 else None

    das, hs, sums = [], [], []
    for s in seqs:
        pre = jnp.dot(mixed_all[s], full_in, preferred_element_type=F32)
        dh = jnp.dot(cot_all[s], full_out, preferred_element_type=F32)
        sig = jax.nn.sigmoid(pre)
        hs.append((pre * sig).astype(BF))
        da = (dh * sig * (1.0 + pre * (1.0 - sig))).astype(BF)
        if s < last and groups == 2:
            da, swapped = bar((da, swapped))
            mixed_all.append(place(mixes[last], swapped))
        if s > 0 and groups == 2:
            kept, sent = sums[s - 1]
            da, sent = bar((da, sent))
            sums[s - 1] = kept, sent
        das.append(da)
        sums.append(reduce_cols(da, full_in, nt))

    out_term = sum(lax.dot_general(cot_all[s], hs[s], tn, preferred_element_type=F32) for s in seqs)
    out_term = out_term.astype(BF)
    if groups == 2:
        kept, sent = sums[last]
        sent, out_term = bar((sent, out_term))
        sums[last] = kept, sent
    grad_out = lax.psum_scatter(out_term, "seq", scatter_dimension=0, tiled=True)
    dms, dws, gates = [], [], []
    for s in seqs:
        gate = jax.nn.sigmoid(gain * sources[s].astype(F32) + shift)
        kept, sent = sums[s]
        dm = cots[s].astype(F32) + (kept if sent is None else kept + sent.astype(F32))
        dm = dm.astype(BF).reshape(blocks, size, chan)
        dw = (dm.astype(F32) * gate).astype(BF)
        dms.append(dm)
        gates.append(gate)
        dws.append(dw.reshape(blocks, owners, offs, chan).transpose(1, 0, 2, 3))
    dw = exchange(jnp.stack(dws, axis=1))
    in_term = sum(lax.dot_general(mixed_all[s], das[s], tn, preferred_element_type=F32) for s in seqs)
    dw, in_term = bar((dw, in_term.astype(BF)))
    scale = 1.0 / size
    grad_in = lax.psum_scatter(in_term, "seq", scatter_dimension=0, tiled=True)

    branches = [list(reduce_cols(hs[s], full_out, nt)) for s in seqs]
    dw = dw.transpose(1, 0, 2, 3, 4).reshape(seq_count, owners * blocks, offs, chan)
    du = jnp.einsum("kjm,sjkc->kmsc", second_factor, dw, preferred_element_type=F32)
    du = du.astype(BF).reshape(offs, owners, blocks, seq_count, chan).transpose(1, 3, 0, 2, 4)
    du = exchange(du)
    if groups == 2:
        du, *sents = bar((du, *[pair[1] for pair in branches]))
        branches = [[pair[0], sent] for pair, sent in zip(branches, sents)]
    grads, results = [], []
    for s in seqs:
        rows = du[:, s].reshape(size, blocks, chan)
        back = jnp.einsum("mkn,kmc->mnc", first_factor, rows, preferred_element_type=F32)
        gate = gates[s]
        gate_term = dms[s].astype(F32) * seconds[s].astype(F32) * gate * (1.0 - gate) * gain
        grads.append((back + gate_term).astype(BF).reshape(tok_rows, chan))
        kept, sent = branches[s]
        branch = kept if sent is None else kept + sent.astype(F32)
        results.append((mixes[s].astype(F32) + branch).astype(BF))
    return (
        jnp.stack(results),
        jnp.stack(grads),
        grad_in.astype(F32) * scale,
        grad_out.astype(F32).T * scale,
    )


MESH = pl.DeviceIdType.MESH
NT = (((1,), (1,)), ((), ()))
TN = (((0,), (0,)), ((), ()))
MIB = 1024 * 1024


def mm(a, b, dims=(((1,), (0,)), ((), ()))):
    return lax.dot_general(a, b, dims, preferred_element_type=F32)


def kernel(
    x_in, cot_in, f_in, s_in, gain_ref, shift_ref, wi_in, wo_in,
    res_out, ig_out, gi_out, go_out, bf_hold,
    x, ff, sf, bs, wt, ub, uv, wb, wv, cota, mixa, h, da, dms, dmr, dmk, rs, rr, rk, lt,
    ld, a_send, a_recv, y_send, y_recv, w_send, w_recv, g_send, g_recv, o_sem, credit_a, credit_b,
):
    me = lax.axis_index("seq")
    mine = lax.axis_index("fsdp")
    oth = 1 - mine
    zc, xc, cc = me // 4, (me // 2) % 2, me % 2
    xpeer = zc * 4 + (1 - xc) * 2 + cc
    cpeer = zc * 4 + xc * 2 + (1 - cc)

    odd, high = zc % 2, zc // 2
    znear = (zc + 1 - 2 * odd) * 4 + xc * 2 + cc
    zfar = ((zc + 2) % 4) * 4 + xc * 2 + cc

    def seqdev(i):
        return {"seq": i}

    ydev = {"fsdp": oth}

    def remote(src, dst, ss, rs_, dev):
        return pltpu.make_async_remote_copy(
            src_ref=src, dst_ref=dst, send_sem=ss, recv_sem=rs_, device_id=dev, device_id_type=MESH
        )

    def drain(ref, sem):
        pltpu.make_async_copy(ref, ref, sem).wait()

    loads = [
        pltpu.make_async_copy(x_in.at[0], x.at[0], ld.at[0]),
        pltpu.make_async_copy(f_in, ff, ld.at[1]),
        pltpu.make_async_copy(x_in.at[1], x.at[1], ld.at[2]),
        pltpu.make_async_copy(wi_in, wt.at[0, pl.ds(me * 64, 64)], ld.at[3]),
        pltpu.make_async_copy(wo_in, wt.at[1, pl.ds(me * 64, 64)], ld.at[4]),
        pltpu.make_async_copy(cot_in.at[0], cota.at[mine, pl.ds(0, 1024)], ld.at[5]),
        pltpu.make_async_copy(cot_in.at[1], cota.at[mine, pl.ds(1024, 1024)], ld.at[6]),
        pltpu.make_async_copy(s_in, sf, ld.at[7]),
    ]
    barrier = pltpu.get_barrier_semaphore()

    @pl.loop(1, 16)
    def _(d):
        pl.semaphore_signal(barrier, inc=1, device_id=seqdev((me + d) % 16), device_id_type=MESH)

    pl.semaphore_signal(barrier, inc=1, device_id=ydev, device_id_type=MESH)
    for c in loads:
        c.start()

    def yview(ref, q):
        return ref.at[mine, pl.ds(q * 512, 512)]

    def ycopy(kind, q):
        if kind == 0:
            a = b = yview(cota, q)
        elif kind == 1:
            a = b = yview(mixa, q)
        else:
            view = (q // 2, pl.ds((q % 2) * 8, 8))
            a, b = rs.at[view], (dmr if kind == 2 else rr).at[view]
        return remote(a, b, y_send.at[kind, q], y_recv.at[kind, q], ydev)

    pairs = [(ub, uv), (wb, wv), (dms, uv), (wb, ub)]

    def a2a(kind, s, rows=slice(0, 64)):
        src, dst = pairs[kind]
        rows = pl.ds(rows.start, rows.stop - rows.start)
        pltpu.make_async_copy(src.at[s, me, rows], dst.at[s, me, rows], a_recv.at[kind, s]).start()

        @pl.loop(1, 16)
        def _(d):
            e = 16 - d
            far = ((high + e // 8) % 2) * 2 + (odd + (e // 4) % 2) % 2
            peer = far * 4 + ((xc + (e // 2) % 2) % 2) * 2 + (cc + e % 2) % 2
            remote(src.at[s, peer, rows], dst.at[s, me, rows], a_send.at[kind, s], a_recv.at[kind, s], seqdev(peer)).start()

    def a2a_recv(kind, s):
        drain(pairs[kind][1].at[s], a_recv.at[kind, s])

    def a2a_sent(kind, s):
        drain(pairs[kind][0].at[s, pl.ds(0, 15)], a_send.at[kind, s])

    FAR, NEAR, NEXT, ACROSS, CORE = range(5)
    peers = (zfar, znear, znear, xpeer, cpeer)
    counts = (64, 64, 64, 256, 512)

    def shard(owner, stages):
        for g in range(2):
            rows = wt.at[g, pl.ds(owner * 64, 64)]
            for k in stages:
                remote(rows, rows, w_send.at[k, g], w_recv.at[k, g], seqdev(peers[k])).start()

    def gathered(k, sems):
        for g in range(2):
            drain(wt.at[0, pl.ds(0, counts[k])], sems.at[k, g])

    def gather_own():
        shard(me, (FAR, NEAR, ACROSS, CORE))

    def gather_far():
        gathered(NEAR, w_recv)
        shard(znear, (ACROSS, CORE))
        gathered(FAR, w_recv)
        shard(zfar, (NEXT, ACROSS, CORE))

    def gather_mid():
        gathered(NEXT, w_recv)
        shard((znear + 8) % 16, (ACROSS, CORE))

    def gather_last():
        gathered(ACROSS, w_recv)

        @pl.loop(0, 4)
        def _(i):
            shard(i * 4 + (1 - xc) * 2 + cc, (CORE,))

    def gather_done():
        gathered(CORE, w_recv)

    gain = gain_ref[...]
    shift = shift_ref[...]

    def big(dst, mat, src, s, dims):
        @pl.loop(0, 4)
        def _(t):
            if dims is TN:
                lhs = mat[:, pl.ds(pl.multiple_of(t * 256, 256), 256)]
            else:
                lhs = mat[pl.ds(pl.multiple_of(t * 256, 256), 256), :]
            out = mm(lhs, src[s].reshape(1024, 512), dims if dims is TN else (((1,), (0,)), ((), ())))
            dst[s, pl.ds(t * 4, 4)] = out.astype(BF).reshape(4, 64, 512)

    def mixer_rows(s, jj):
        w = wv[s, :, pl.ds(pl.multiple_of(jj * 16, 16), 16), :].astype(F32).reshape(16, 2, 8, 512)
        w = jnp.concatenate([w[:, 0].reshape(128, 512), w[:, 1].reshape(128, 512)], axis=0)
        rows = pl.ds(pl.multiple_of(jj * 256, 256), 256)
        gate = jax.nn.sigmoid(gain * x[s, rows, :].astype(F32) + shift)
        return w, gate

    def gate_chunk(q):
        s = q // 2

        @pl.loop((q % 2) * 2, (q % 2) * 2 + 2)
        def _(jj):
            w, gate = mixer_rows(s, jj)
            rows = pl.ds(pl.multiple_of(s * 1024 + jj * 256, 256), 256)
            mixa[mine, rows, :] = (gate * w).astype(BF)

        ycopy(1, q).start()

    def half_copy(half):
        view = (0, pl.ds(half * 4, 4))
        return remote(rs.at[view], dmr.at[view], y_send.at[4, half], y_recv.at[4, half], ydev)

    def mlp(q, at=0, count=512):
        rows = pl.ds(q * 512 + at, count)
        s = q // 2

        @pl.loop(0, 8)
        def _(f):
            cols = pl.ds(pl.multiple_of(f * 256, 256), 256)
            pre = mm(mixa[0, rows, :], wt[0, pl.ds(0, 512), cols]) + mm(mixa[1, rows, :], wt[0, pl.ds(512, 512), cols])
            dh = mm(cota[0, rows, :], wt[1, pl.ds(0, 512), cols]) + mm(cota[1, rows, :], wt[1, pl.ds(512, 512), cols])
            sig = jax.nn.sigmoid(pre)
            h[rows, cols] = (pre * sig).astype(BF)
            da[rows, cols] = (dh * sig * (1.0 + pre * (1.0 - sig))).astype(BF)

        @pl.loop(0, 2)
        def _(n):
            cols = pl.ds(pl.multiple_of(n * 256, 256), 256)
            chans = pl.ds(pl.multiple_of(oth * 512 + n * 256, 256), 256)
            out = mm(da[rows, :], wt[0, chans, :], NT)
            slab = pl.ds((q % 2) * 8 + at // 64, count // 64)
            rs[s, slab, :, cols] = out.astype(BF).reshape(count // 64, 64, 256)

        if q > 0:
            ycopy(2, q).start()
        else:
            half_copy(at // 256).start()

    def own_dm(q):
        rows = pl.ds(q * 512, 512)

        @pl.loop(0, 2)
        def _(n):
            cols = pl.ds(pl.multiple_of(n * 256, 256), 256)
            chans = pl.ds(pl.multiple_of(mine * 512 + n * 256, 256), 256)
            out = mm(da[rows, :], wt[0, chans, :], NT)
            dmk[rows, cols] = (out + cota[mine, rows, cols].astype(F32)).astype(BF)

    def res_part(q):
        rows = pl.ds(q * 512, 512)

        @pl.loop(0, 2)
        def _(n):
            cols = pl.ds(pl.multiple_of(n * 256, 256), 256)
            chans = pl.ds(pl.multiple_of(oth * 512 + n * 256, 256), 256)
            out = mm(h[rows, :], wt[1, chans, :], NT).astype(BF)
            rs[q // 2, pl.ds((q % 2) * 8, 8), :, cols] = out.reshape(8, 64, 256)

    def res_own(q):
        rows = pl.ds(q * 512, 512)

        @pl.loop(0, 2)
        def _(n):
            cols = pl.ds(pl.multiple_of(n * 256, 256), 256)
            chans = pl.ds(pl.multiple_of(mine * 512 + n * 256, 256), 256)
            out = mm(h[rows, :], wt[1, chans, :], NT)
            rk[rows, cols] = (out + mixa[mine, rows, cols].astype(F32)).astype(BF)

    def finish_dm(q):
        s, r = q // 2, q % 2
        if r == 0:
            a2a_sent(0, s)
        if q > 0:
            ycopy(2, q).wait()
        else:
            half_copy(0).wait()
            half_copy(1).wait()

        @pl.loop(2 * r, 2 * r + 2)
        def _(jj):
            w, gate = mixer_rows(s, jj)
            rows = pl.ds(pl.multiple_of(s * 1024 + jj * 256, 256), 256)
            slab = pl.ds(jj * 4, 4)
            dm = dmk[rows, :].astype(F32) + dmr[s, slab].astype(F32).reshape(256, 512)
            dm = dm.astype(BF)
            dmr[s, slab] = dm.reshape(4, 64, 512)
            dw = (dm.astype(F32) * gate).reshape(2, 16, 8, 512)
            dw = jnp.concatenate([dw[0], dw[1]], axis=1)
            dms[s, :, pl.ds(pl.multiple_of(jj * 16, 16), 16), :] = dw.astype(BF)

        a2a(2, s, slice(32 * r, 32 * r + 32))

    def finish_grad(s):
        @pl.loop(0, 4)
        def _(jj):
            w, gate = mixer_rows(s, jj)
            slab = pl.ds(jj * 4, 4)
            dm = dmr[s, slab].astype(F32).reshape(256, 512)
            term = dm * w * gate * (1.0 - gate) * gain
            cols = pl.ds(pl.multiple_of(jj * 256, 256), 256)
            out = mm(lt[0, :, cols], ub[s].reshape(1024, 512), TN)
            uv[s, slab] = (out + term).astype(BF).reshape(4, 64, 512)

        return pltpu.make_async_copy(uv.at[s], ig_out.at[s], o_sem.at[s])

    def finish_res(s):
        for q in (2 * s, 2 * s + 1):
            ycopy(3, q).wait()

        @pl.loop(0, 4)
        def _(jj):
            rows = pl.ds(pl.multiple_of(s * 1024 + jj * 256, 256), 256)
            more = rr[s, pl.ds(jj * 4, 4)].astype(F32).reshape(256, 512)
            rk[rows, :] = (rk[rows, :].astype(F32) + more).astype(BF)

        return pltpu.make_async_copy(rk.at[pl.ds(s * 1024, 1024)], res_out.at[s], o_sem.at[2 + s])

    def turn(src, seqs=(0, 1)):
        for y in range(2):
            for s in seqs:
                @pl.loop(0, 4)
                def _(i):
                    rows = pl.ds(pl.multiple_of(s * 1024 + i * 256, 256), 256)
                    cols = pl.ds(pl.multiple_of(i * 256, 256), 256)
                    lt[y, pl.ds(s * 512, 512), cols] = src[y, rows, :].T

    def weight_grad(g, part):
        rhs = (da, h)[g]
        for y in range(2):
            @pl.loop(0, 2)
            def _(f):
                cols = pl.ds(pl.multiple_of(part * 1024 + f * 512, 512), 512)
                out = mm(lt[y, pl.ds(0, 512), :], rhs[pl.ds(0, 1024), cols])
                out = (out + mm(lt[y, pl.ds(512, 512), :], rhs[pl.ds(1024, 1024), cols])).astype(BF)
                for i in range(8):
                    xi, ci = (i // 2) % 2, i % 2
                    slot = ci * 512 + xi * 256 + (i // 4) * 128 + y * 64
                    wt[g, pl.ds(slot, 64), cols] = out[i * 64 : i * 64 + 64]

    def give(credit):
        for peer in (xpeer, cpeer, znear, zfar):
            pl.semaphore_signal(credit, inc=1, device_id=seqdev(peer), device_id_type=MESH)

    def add_rows(g, cols, base, off, count):
        @pl.loop(0, count)
        def _(i):
            rows = pl.ds(pl.multiple_of(base + i * 64, 64), 64)
            more = da[pl.ds(pl.multiple_of(off + i * 64, 64), 64), cols].astype(F32)
            wt[g, rows, cols] = (wt[g, rows, cols].astype(F32) + more).astype(BF)

    def halving(g, part, step):
        bits = (cc, xc, odd, high)
        partner = (cpeer, xpeer, znear, zfar)
        size = 512 >> step
        keep = 0
        for k in range(step):
            keep = keep + bits[k] * (512 >> k)
        send = keep + (1 - bits[step]) * size
        keep = keep + bits[step] * size
        land = 2048 - (2048 >> step) + g * size
        cols = pl.ds(part * 1024, 1024)
        copy = remote(
            wt.at[g, pl.ds(send, size), cols], da.at[pl.ds(land, size), cols],
            g_send.at[step, 2 * g + part], g_recv.at[step, 2 * g + part], seqdev(partner[step]),
        )
        return copy, keep, land, size, cols

    def scatter_step(g, part, step):
        if step > 0:
            copy, keep, land, size, cols = halving(g, part, step - 1)
            copy.wait()
            if step < 4:
                add_rows(g, cols, keep, land, size // 64)
            else:
                out = gi_out if g == 0 else go_out
                own = wt[g, pl.ds(pl.multiple_of(keep, 64), 64), cols].astype(F32)
                out[:, cols] = (own + da[pl.ds(land, 64), cols].astype(F32)) * (1.0 / 128)
        if step < 4:
            halving(g, part, step)[0].start()

    plain = (((1,), (0,)), ((), ()))

    def build_pick():
        @pl.loop(0, 4)
        def _(t):
            row = lax.broadcasted_iota(jnp.int32, (256, 1024), 0) + t * 256
            col = lax.broadcasted_iota(jnp.int32, (256, 1024), 1)
            want = (row & 7) * 128 + (row >> 3)
            rows = pl.ds(pl.multiple_of(1024 + t * 256, 256), 256)
            da[rows, pl.ds(0, 1024)] = jnp.where(col == want, 1.0, 0.0).astype(BF)

    def pick_rows(t):
        return da[pl.ds(pl.multiple_of(1024 + t * 256, 256), 256), pl.ds(0, 1024)]

    def first(s):
        for m in range(8):
            rows = pl.ds(m * 128, 128)
            h[rows, pl.ds(0, 512)] = mm(ff[m], x[s, rows, :]).astype(BF)

        @pl.loop(0, 4)
        def _(t):
            out = mm(pick_rows(t), h[pl.ds(0, 1024), pl.ds(0, 512)])
            ub[s, pl.ds(t * 4, 4)] = out.astype(BF).reshape(4, 64, 512)

    def build_second():
        for fac, rows in ((ff, 0), (sf, 1024)):
            da[pl.ds(rows, 1024), pl.ds(1024, 1024)] = jnp.zeros((1024, 1024), BF)
            for m in range(8):
                da[pl.ds(rows + m * 128, 128), pl.ds(1024 + m * 128, 128)] = fac[m]

        @pl.loop(0, 4)
        def _(t):
            rows = pl.ds(pl.multiple_of(t * 256, 256), 256)
            lt[0, rows, :] = mm(pick_rows(t), da[pl.ds(0, 1024), pl.ds(1024, 1024)]).astype(BF)
            h[rows, pl.ds(1024, 1024)] = mm(pick_rows(t), da[pl.ds(1024, 1024), pl.ds(1024, 1024)]).astype(BF)

        @pl.loop(0, 4)
        def _(t):
            row = lax.broadcasted_iota(jnp.int32, (1024, 256), 0)
            col = lax.broadcasted_iota(jnp.int32, (1024, 256), 1) + t * 256
            want = ((col >> 3) & 7) * 128 + (col >> 6) * 8 + (col & 7)
            pick = jnp.where(row == want, 1.0, 0.0).astype(BF)
            cols = pl.ds(pl.multiple_of(t * 256, 256), 256)
            for r in range(2):
                rows = pl.ds(r * 512, 512)
                bs[rows, cols] = mm(h[rows, pl.ds(1024, 1024)], pick).astype(BF)

    build_pick()
    loads[0].wait()
    loads[1].wait()
    first(0)
    loads[3].wait()
    loads[4].wait()
    pl.semaphore_wait(barrier, 16)
    gather_own()
    a2a(0, 0)
    loads[5].wait()
    loads[6].wait()
    for q in range(4):
        ycopy(0, q).start()
    loads[2].wait()
    loads[7].wait()
    first(1)
    build_second()
    hold = pltpu.make_async_copy(lt.at[0], bf_hold, ld.at[0])
    hold.start()
    gather_far()
    a2a_recv(0, 0)
    big(wb, bs, uv, 0, plain)
    a2a(1, 0)
    a2a(0, 1)
    gather_mid()
    a2a_recv(1, 0)
    gate_chunk(0)
    gate_chunk(1)
    gather_last()
    a2a_recv(0, 1)
    big(wb, bs, uv, 1, plain)
    a2a(1, 1)
    for q in range(4):
        ycopy(0, q).wait()
    gather_done()
    ycopy(1, 0).wait()
    mlp(0, 0, 256)
    mlp(0, 256, 256)
    ycopy(1, 1).wait()
    mlp(1)
    own_dm(0)
    own_dm(1)
    finish_dm(0)
    a2a_recv(1, 1)
    gate_chunk(2)
    res_own(0)
    finish_dm(1)
    gate_chunk(3)
    res_own(1)
    res_part(0)
    res_part(1)
    hold.wait()
    turn(mixa, (0,))
    ycopy(1, 2).wait()
    mlp(2)
    own_dm(2)
    res_own(2)
    a2a_recv(2, 0)
    a2a_sent(1, 0)
    big(wb, bs, uv, 0, TN)
    a2a(3, 0)
    ycopy(1, 3).wait()
    mlp(3)
    own_dm(3)
    finish_dm(2)
    for k in range(5):
        gathered(k, w_send)
    turn(mixa, (1,))
    weight_grad(0, 0)
    give(credit_a)
    weight_grad(0, 1)
    give(credit_b)
    pl.semaphore_wait(credit_a, 4)
    scatter_step(0, 0, 0)
    finish_dm(3)
    pl.semaphore_wait(credit_b, 4)
    scatter_step(0, 1, 0)
    scatter_step(0, 0, 1)
    res_part(2)
    res_part(3)
    res_own(3)
    scatter_step(0, 1, 1)
    for q in range(4):
        ycopy(3, q).start()
    turn(cota)
    weight_grad(1, 0)
    scatter_step(1, 0, 0)
    weight_grad(1, 1)
    scatter_step(1, 1, 0)
    unhold = pltpu.make_async_copy(bf_hold, lt.at[0], ld.at[0])
    unhold.start()
    scatter_step(1, 0, 1)
    scatter_step(1, 1, 1)
    a2a_recv(2, 1)
    a2a_sent(1, 1)
    big(wb, bs, uv, 1, TN)
    a2a(3, 1)
    scatter_step(0, 0, 2)
    scatter_step(0, 1, 2)
    unhold.wait()
    a2a_recv(3, 0)
    outs = [finish_grad(0)]
    outs[0].start()
    scatter_step(0, 0, 3)
    scatter_step(0, 1, 3)
    scatter_step(1, 0, 2)
    for s in range(2):
        outs.append(finish_res(s))
        outs[-1].start()
    scatter_step(1, 1, 2)
    scatter_step(0, 0, 4)
    scatter_step(0, 1, 4)
    scatter_step(1, 0, 3)
    a2a_recv(3, 1)
    outs.append(finish_grad(1))
    outs[-1].start()
    scatter_step(1, 1, 3)
    scatter_step(1, 0, 4)
    scatter_step(1, 1, 4)
    for kind in (2, 3):
        for s in range(2):
            a2a_sent(kind, s)
    for c in outs:
        c.wait()


def fused(
    inputs, first_factor, second_factor, gate_scale, gate_bias, in_weight, out_weight, cotangent
):
    count, rows, chan = inputs.shape
    hidden = in_weight.shape[1]
    anyspace = pl.BlockSpec(memory_space=pl.ANY)
    vmem = pl.BlockSpec(memory_space=pltpu.VMEM)
    cells = (2, 16, 64, 512)
    dma = pltpu.SemaphoreType.DMA
    buf = pltpu.VMEM
    res, ig, gi, go, _ = pl.pallas_call(
        kernel,
        out_shape=(
            jax.ShapeDtypeStruct((2, 1024, 512), BF),
            jax.ShapeDtypeStruct(cells, BF),
            jax.ShapeDtypeStruct((64, hidden), F32),
            jax.ShapeDtypeStruct((64, hidden), F32),
            jax.ShapeDtypeStruct((1024, 1024), BF),
        ),
        in_specs=[anyspace] * 4 + [vmem] * 2 + [anyspace] * 2,
        out_specs=(anyspace, anyspace, vmem, vmem, anyspace),
        scratch_shapes=[
            buf((2, 1024, 512), BF),
            buf(first_factor.shape, BF),
            buf(second_factor.shape, BF),
            buf((1024, 1024), BF),
            buf((2, 1024, 2048), BF),
            buf(cells, BF),
            buf(cells, BF),
            buf(cells, BF),
            buf(cells, BF),
            buf((2, 2048, 512), BF),
            buf((2, 2048, 512), BF),
            buf((2048, 2048), BF),
            buf((2048, 2048), BF),
            buf(cells, BF),
            buf(cells, BF),
            buf((2048, 512), BF),
            buf(cells, BF),
            buf(cells, BF),
            buf((2048, 512), BF),
            buf((2, 1024, 1024), BF),
            dma((8,)),
            dma((4, 2)),
            dma((4, 2)),
            dma((5, 4)),
            dma((5, 4)),
            dma((5, 2)),
            dma((5, 2)),
            dma((4, 4)),
            dma((4, 4)),
            dma((4,)),
            pltpu.SemaphoreType.REGULAR,
            pltpu.SemaphoreType.REGULAR,
        ],
        compiler_params=pltpu.CompilerParams(
            collective_id=0, has_side_effects=True, vmem_limit_bytes=63 * MIB
        ),
        cost_estimate=pl.CostEstimate(flops=60 * 10**9, bytes_accessed=20 * MIB, transcendentals=0),
    )(
        inputs,
        cotangent,
        first_factor,
        second_factor,
        gate_scale.reshape(1, chan),
        gate_bias.reshape(1, chan),
        in_weight,
        out_weight.T,
    )
    return res, ig.reshape(inputs.shape), gi, go.T


def solution(mesh):
    in_specs = (
        P(None, "seq", "fsdp"),
        P("seq", None, None),
        P("seq", None, None),
        P("fsdp"),
        P("fsdp"),
        P("seq", "fsdp"),
        P("fsdp", "seq"),
        P(None, "seq", "fsdp"),
    )
    out_specs = (P(None, "seq", "fsdp"), P(None, "seq", "fsdp"), P("seq", "fsdp"), P("fsdp", "seq"))
    sizes = (mesh.shape["seq"], mesh.shape["fsdp"])
    part = fused if sizes == (16, 2) else body
    return jax.shard_map(part, mesh=mesh, in_specs=in_specs, out_specs=out_specs, check_vma=False)
```

```python
import functools

import jax
import jax.numpy as jnp
from jax import lax
from jax.experimental import pallas as pl
from jax.experimental.pallas import tpu as pltpu
from jax.sharding import PartitionSpec as P

BF = jnp.bfloat16
F32 = jnp.float32


def body(
    inputs, first_factor, second_factor, gate_scale, gate_bias, in_weight, out_weight, cotangent
):
    seq_count, tok_rows, chan = inputs.shape
    blocks, size, _ = first_factor.shape
    offs = second_factor.shape[0]
    owners = lax.axis_size("seq")
    groups = lax.axis_size("fsdp")
    mine = lax.axis_index("fsdp")
    width = chan * groups
    gain = gate_scale.reshape(1, 1, chan)
    shift = gate_bias.reshape(1, 1, chan)

    def swap(x):
        return lax.ppermute(x, "fsdp", [(0, 1), (1, 0)])

    def gather_cols(x):
        if groups != 2:
            return lax.all_gather(x, "fsdp", axis=1, tiled=True)
        return place(x, swap(x))

    def place(x, y):
        first = mine == 0
        return jnp.concatenate([jnp.where(first, x, y), jnp.where(first, y, x)], axis=1)

    def reduce_cols(left, weight, dims):
        if groups != 2:
            full = lax.dot_general(left, weight, dims, preferred_element_type=F32)
            got = lax.all_to_all(full, "fsdp", split_axis=1, concat_axis=0, tiled=True)
            return jnp.sum(got.reshape(groups, -1, chan), axis=0), None
        other = lax.dynamic_slice_in_dim(weight, (1 - mine) * chan, chan, 0)
        own = lax.dynamic_slice_in_dim(weight, mine * chan, chan, 0)
        sent = swap(lax.dot_general(left, other, dims, preferred_element_type=F32).astype(BF))
        kept = lax.dot_general(left, own, dims, preferred_element_type=F32)
        return kept, sent

    def exchange(x):
        return lax.all_to_all(x, "seq", split_axis=0, concat_axis=0, tiled=True)

    bar = lax.optimization_barrier
    nt = (((1,), (1,)), ((), ()))
    tn = (((0,), (0,)), ((), ()))
    seqs = range(seq_count)
    last = seq_count - 1
    both = jnp.stack([in_weight, out_weight.T], axis=0)
    both = lax.all_gather(both, "seq", axis=1, tiled=True)
    full_in, full_out = both[0], both[1]

    sources = [inputs[s].reshape(blocks, size, chan) for s in seqs]
    cots = [cotangent[s] for s in seqs]
    cot_all = [gather_cols(c) for c in cots]

    source = inputs.reshape(seq_count, blocks, size, chan)
    u = jnp.einsum("mkn,smnc->mksc", first_factor, source, preferred_element_type=F32)
    u = u.astype(BF).reshape(blocks, owners, offs, seq_count, chan).transpose(1, 3, 0, 2, 4)
    u, *cot_all = bar((exchange(u), *cot_all))
    turned = [u[:, s].reshape(owners * blocks, offs, chan) for s in seqs]
    mixes, seconds, mixed_all = [], [], []
    for s in seqs:
        w = jnp.einsum("kjm,mkc->kjc", second_factor, turned[s], preferred_element_type=F32)
        w = w.astype(BF).reshape(offs, owners, blocks, chan).transpose(1, 0, 2, 3)
        w = exchange(w)
        if s > 0:
            w, mixed_all[s - 1] = bar((w, mixed_all[s - 1]))
        w = bar(w.reshape(size, blocks, chan).transpose(1, 0, 2))
        gate = jax.nn.sigmoid(gain * sources[s].astype(F32) + shift)
        seconds.append(w)
        mixes.append((gate * w.astype(F32)).astype(BF).reshape(tok_rows, chan))
        if s < last or groups != 2:
            mixed_all.append(gather_cols(mixes[s]))
    swapped = swap(mixes[last]) if groups == 2 else None

    das, hs, sums = [], [], []
    for s in seqs:
        pre = jnp.dot(mixed_all[s], full_in, preferred_element_type=F32)
        dh = jnp.dot(cot_all[s], full_out, preferred_element_type=F32)
        sig = jax.nn.sigmoid(pre)
        hs.append((pre * sig).astype(BF))
        da = (dh * sig * (1.0 + pre * (1.0 - sig))).astype(BF)
        if s < last and groups == 2:
            da, swapped = bar((da, swapped))
            mixed_all.append(place(mixes[last], swapped))
        if s > 0 and groups == 2:
            kept, sent = sums[s - 1]
            da, sent = bar((da, sent))
            sums[s - 1] = kept, sent
        das.append(da)
        sums.append(reduce_cols(da, full_in, nt))

    out_term = sum(lax.dot_general(cot_all[s], hs[s], tn, preferred_element_type=F32) for s in seqs)
    out_term = out_term.astype(BF)
    if groups == 2:
        kept, sent = sums[last]
        sent, out_term = bar((sent, out_term))
        sums[last] = kept, sent
    grad_out = lax.psum_scatter(out_term, "seq", scatter_dimension=0, tiled=True)
    dms, dws, gates = [], [], []
    for s in seqs:
        gate = jax.nn.sigmoid(gain * sources[s].astype(F32) + shift)
        kept, sent = sums[s]
        dm = cots[s].astype(F32) + (kept if sent is None else kept + sent.astype(F32))
        dm = dm.astype(BF).reshape(blocks, size, chan)
        dw = (dm.astype(F32) * gate).astype(BF)
        dms.append(dm)
        gates.append(gate)
        dws.append(dw.reshape(blocks, owners, offs, chan).transpose(1, 0, 2, 3))
    dw = exchange(jnp.stack(dws, axis=1))
    in_term = sum(lax.dot_general(mixed_all[s], das[s], tn, preferred_element_type=F32) for s in seqs)
    dw, in_term = bar((dw, in_term.astype(BF)))
    scale = 1.0 / size
    grad_in = lax.psum_scatter(in_term, "seq", scatter_dimension=0, tiled=True)

    branches = [list(reduce_cols(hs[s], full_out, nt)) for s in seqs]
    dw = dw.transpose(1, 0, 2, 3, 4).reshape(seq_count, owners * blocks, offs, chan)
    du = jnp.einsum("kjm,sjkc->kmsc", second_factor, dw, preferred_element_type=F32)
    du = du.astype(BF).reshape(offs, owners, blocks, seq_count, chan).transpose(1, 3, 0, 2, 4)
    du = exchange(du)
    if groups == 2:
        du, *sents = bar((du, *[pair[1] for pair in branches]))
        branches = [[pair[0], sent] for pair, sent in zip(branches, sents)]
    grads, results = [], []
    for s in seqs:
        rows = du[:, s].reshape(size, blocks, chan)
        back = jnp.einsum("mkn,kmc->mnc", first_factor, rows, preferred_element_type=F32)
        gate = gates[s]
        gate_term = dms[s].astype(F32) * seconds[s].astype(F32) * gate * (1.0 - gate) * gain
        grads.append((back + gate_term).astype(BF).reshape(tok_rows, chan))
        kept, sent = branches[s]
        branch = kept if sent is None else kept + sent.astype(F32)
        results.append((mixes[s].astype(F32) + branch).astype(BF))
    return (
        jnp.stack(results),
        jnp.stack(grads),
        grad_in.astype(F32) * scale,
        grad_out.astype(F32).T * scale,
    )


MESH = pl.DeviceIdType.MESH
NT = (((1,), (1,)), ((), ()))
TN = (((0,), (0,)), ((), ()))
MIB = 1024 * 1024


def mm(a, b, dims=(((1,), (0,)), ((), ()))):
    return lax.dot_general(a, b, dims, preferred_element_type=F32)


def kernel(
    x_in, cot_in, f_in, s_in, gain_ref, shift_ref, wi_in, wo_in,
    res_out, ig_out, gi_out, go_out, bf_hold,
    x, ff, sf, bs, wt, ub, uv, wb, wv, cota, mixa, h, da, dms, dmr, dmk, rs, rr, rk, lt,
    ld, a_send, a_recv, y_send, y_recv, w_send, w_recv, g_send, g_recv, o_sem, credit_a, credit_b,
):
    me = lax.axis_index("seq")
    mine = lax.axis_index("fsdp")
    oth = 1 - mine
    zc, xc, cc = me // 4, (me // 2) % 2, me % 2
    xpeer = zc * 4 + (1 - xc) * 2 + cc
    cpeer = zc * 4 + xc * 2 + (1 - cc)

    odd, high = zc % 2, zc // 2
    znear = (zc + 1 - 2 * odd) * 4 + xc * 2 + cc
    zfar = ((zc + 2) % 4) * 4 + xc * 2 + cc

    def seqdev(i):
        return {"seq": i}

    ydev = {"fsdp": oth}

    def remote(src, dst, ss, rs_, dev):
        return pltpu.make_async_remote_copy(
            src_ref=src, dst_ref=dst, send_sem=ss, recv_sem=rs_, device_id=dev, device_id_type=MESH
        )

    def drain(ref, sem):
        pltpu.make_async_copy(ref, ref, sem).wait()

    loads = [
        pltpu.make_async_copy(x_in.at[0], x.at[0], ld.at[0]),
        pltpu.make_async_copy(f_in, ff, ld.at[1]),
        pltpu.make_async_copy(x_in.at[1], x.at[1], ld.at[2]),
        pltpu.make_async_copy(wi_in, wt.at[0, pl.ds(me * 64, 64)], ld.at[3]),
        pltpu.make_async_copy(wo_in, wt.at[1, pl.ds(me * 64, 64)], ld.at[4]),
        pltpu.make_async_copy(cot_in.at[0], cota.at[mine, pl.ds(0, 1024)], ld.at[5]),
        pltpu.make_async_copy(cot_in.at[1], cota.at[mine, pl.ds(1024, 1024)], ld.at[6]),
        pltpu.make_async_copy(s_in, sf, ld.at[7]),
    ]
    barrier = pltpu.get_barrier_semaphore()

    @pl.loop(1, 16)
    def _(d):
        pl.semaphore_signal(barrier, inc=1, device_id=seqdev((me + d) % 16), device_id_type=MESH)

    pl.semaphore_signal(barrier, inc=1, device_id=ydev, device_id_type=MESH)
    for c in loads:
        c.start()

    def yview(ref, q):
        return ref.at[mine, pl.ds(q * 512, 512)]

    def ycopy(kind, q):
        if kind == 0:
            a = b = yview(cota, q)
        elif kind == 1:
            a = b = yview(mixa, q)
        else:
            view = (q // 2, pl.ds((q % 2) * 8, 8))
            a, b = rs.at[view], (dmr if kind == 2 else rr).at[view]
        return remote(a, b, y_send.at[kind, q], y_recv.at[kind, q], ydev)

    pairs = [(ub, uv), (wb, wv), (dms, uv), (wb, ub)]

    def a2a(kind, s, rows=slice(0, 64)):
        src, dst = pairs[kind]
        rows = pl.ds(rows.start, rows.stop - rows.start)
        pltpu.make_async_copy(src.at[s, me, rows], dst.at[s, me, rows], a_recv.at[kind, s]).start()

        @pl.loop(1, 16)
        def _(d):
            e = 16 - d
            far = ((high + e // 8) % 2) * 2 + (odd + (e // 4) % 2) % 2
            peer = far * 4 + ((xc + (e // 2) % 2) % 2) * 2 + (cc + e % 2) % 2
            remote(src.at[s, peer, rows], dst.at[s, me, rows], a_send.at[kind, s], a_recv.at[kind, s], seqdev(peer)).start()

    def a2a_recv(kind, s):
        drain(pairs[kind][1].at[s], a_recv.at[kind, s])

    def a2a_sent(kind, s):
        drain(pairs[kind][0].at[s, pl.ds(0, 15)], a_send.at[kind, s])

    FAR, NEAR, NEXT, ACROSS, CORE = range(5)
    peers = (zfar, znear, znear, xpeer, cpeer)
    counts = (64, 64, 64, 256, 512)

    def shard(owner, stages):
        for g in range(2):
            rows = wt.at[g, pl.ds(owner * 64, 64)]
            for k in stages:
                remote(rows, rows, w_send.at[k, g], w_recv.at[k, g], seqdev(peers[k])).start()

    def gathered(k, sems):
        for g in range(2):
            drain(wt.at[0, pl.ds(0, counts[k])], sems.at[k, g])

    def gather_own():
        shard(me, (FAR, NEAR, ACROSS, CORE))

    def gather_far():
        gathered(NEAR, w_recv)
        shard(znear, (ACROSS, CORE))
        gathered(FAR, w_recv)
        shard(zfar, (NEXT, ACROSS, CORE))

    def gather_mid():
        gathered(NEXT, w_recv)
        shard((znear + 8) % 16, (ACROSS, CORE))

    def gather_last():
        gathered(ACROSS, w_recv)

        @pl.loop(0, 4)
        def _(i):
            shard(i * 4 + (1 - xc) * 2 + cc, (CORE,))

    def gather_done():
        gathered(CORE, w_recv)

    gain = gain_ref[...]
    shift = shift_ref[...]

    def big(dst, mat, src, s, dims):
        @pl.loop(0, 4)
        def _(t):
            if dims is TN:
                lhs = mat[:, pl.ds(pl.multiple_of(t * 256, 256), 256)]
            else:
                lhs = mat[pl.ds(pl.multiple_of(t * 256, 256), 256), :]
            out = mm(lhs, src[s].reshape(1024, 512), dims if dims is TN else (((1,), (0,)), ((), ())))
            dst[s, pl.ds(t * 4, 4)] = out.astype(BF).reshape(4, 64, 512)

    def mixer_rows(s, jj):
        w = wv[s, :, pl.ds(pl.multiple_of(jj * 16, 16), 16), :].astype(F32).reshape(16, 2, 8, 512)
        w = jnp.concatenate([w[:, 0].reshape(128, 512), w[:, 1].reshape(128, 512)], axis=0)
        rows = pl.ds(pl.multiple_of(jj * 256, 256), 256)
        gate = jax.nn.sigmoid(gain * x[s, rows, :].astype(F32) + shift)
        return w, gate

    def gate_chunk(q):
        s = q // 2

        @pl.loop((q % 2) * 2, (q % 2) * 2 + 2)
        def _(jj):
            w, gate = mixer_rows(s, jj)
            rows = pl.ds(pl.multiple_of(s * 1024 + jj * 256, 256), 256)
            mixa[mine, rows, :] = (gate * w).astype(BF)

        ycopy(1, q).start()

    def half_copy(half):
        view = (0, pl.ds(half * 4, 4))
        return remote(rs.at[view], dmr.at[view], y_send.at[4, half], y_recv.at[4, half], ydev)

    def mlp(q, at=0, count=512):
        rows = pl.ds(q * 512 + at, count)
        s = q // 2

        @pl.loop(0, 8)
        def _(f):
            cols = pl.ds(pl.multiple_of(f * 256, 256), 256)
            pre = mm(mixa[0, rows, :], wt[0, pl.ds(0, 512), cols]) + mm(mixa[1, rows, :], wt[0, pl.ds(512, 512), cols])
            dh = mm(cota[0, rows, :], wt[1, pl.ds(0, 512), cols]) + mm(cota[1, rows, :], wt[1, pl.ds(512, 512), cols])
            sig = jax.nn.sigmoid(pre)
            h[rows, cols] = (pre * sig).astype(BF)
            da[rows, cols] = (dh * sig * (1.0 + pre * (1.0 - sig))).astype(BF)

        @pl.loop(0, 2)
        def _(n):
            cols = pl.ds(pl.multiple_of(n * 256, 256), 256)
            chans = pl.ds(pl.multiple_of(oth * 512 + n * 256, 256), 256)
            out = mm(da[rows, :], wt[0, chans, :], NT)
            slab = pl.ds((q % 2) * 8 + at // 64, count // 64)
            rs[s, slab, :, cols] = out.astype(BF).reshape(count // 64, 64, 256)

        if q > 0:
            ycopy(2, q).start()
        else:
            half_copy(at // 256).start()

    def own_dm(q):
        rows = pl.ds(q * 512, 512)

        @pl.loop(0, 2)
        def _(n):
            cols = pl.ds(pl.multiple_of(n * 256, 256), 256)
            chans = pl.ds(pl.multiple_of(mine * 512 + n * 256, 256), 256)
            out = mm(da[rows, :], wt[0, chans, :], NT)
            dmk[rows, cols] = (out + cota[mine, rows, cols].astype(F32)).astype(BF)

    def res_part(q):
        rows = pl.ds(q * 512, 512)

        @pl.loop(0, 2)
        def _(n):
            cols = pl.ds(pl.multiple_of(n * 256, 256), 256)
            chans = pl.ds(pl.multiple_of(oth * 512 + n * 256, 256), 256)
            out = mm(h[rows, :], wt[1, chans, :], NT).astype(BF)
            rs[q // 2, pl.ds((q % 2) * 8, 8), :, cols] = out.reshape(8, 64, 256)

    def res_own(q):
        rows = pl.ds(q * 512, 512)

        @pl.loop(0, 2)
        def _(n):
            cols = pl.ds(pl.multiple_of(n * 256, 256), 256)
            chans = pl.ds(pl.multiple_of(mine * 512 + n * 256, 256), 256)
            out = mm(h[rows, :], wt[1, chans, :], NT)
            rk[rows, cols] = (out + mixa[mine, rows, cols].astype(F32)).astype(BF)

    def finish_dm(q):
        s, r = q // 2, q % 2
        if r == 0:
            a2a_sent(0, s)
        if q > 0:
            ycopy(2, q).wait()
        else:
            half_copy(0).wait()
            half_copy(1).wait()

        @pl.loop(2 * r, 2 * r + 2)
        def _(jj):
            w, gate = mixer_rows(s, jj)
            rows = pl.ds(pl.multiple_of(s * 1024 + jj * 256, 256), 256)
            slab = pl.ds(jj * 4, 4)
            dm = dmk[rows, :].astype(F32) + dmr[s, slab].astype(F32).reshape(256, 512)
            dm = dm.astype(BF)
            dmr[s, slab] = dm.reshape(4, 64, 512)
            dw = (dm.astype(F32) * gate).reshape(2, 16, 8, 512)
            dw = jnp.concatenate([dw[0], dw[1]], axis=1)
            dms[s, :, pl.ds(pl.multiple_of(jj * 16, 16), 16), :] = dw.astype(BF)

        a2a(2, s, slice(32 * r, 32 * r + 32))

    def finish_grad(s):
        @pl.loop(0, 4)
        def _(jj):
            w, gate = mixer_rows(s, jj)
            slab = pl.ds(jj * 4, 4)
            dm = dmr[s, slab].astype(F32).reshape(256, 512)
            term = dm * w * gate * (1.0 - gate) * gain
            cols = pl.ds(pl.multiple_of(jj * 256, 256), 256)
            out = mm(lt[0, :, cols], ub[s].reshape(1024, 512), TN)
            uv[s, slab] = (out + term).astype(BF).reshape(4, 64, 512)

        return pltpu.make_async_copy(uv.at[s], ig_out.at[s], o_sem.at[s])

    def finish_res(s):
        for q in (2 * s, 2 * s + 1):
            ycopy(3, q).wait()

        @pl.loop(0, 4)
        def _(jj):
            rows = pl.ds(pl.multiple_of(s * 1024 + jj * 256, 256), 256)
            more = rr[s, pl.ds(jj * 4, 4)].astype(F32).reshape(256, 512)
            rk[rows, :] = (rk[rows, :].astype(F32) + more).astype(BF)

        return pltpu.make_async_copy(rk.at[pl.ds(s * 1024, 1024)], res_out.at[s], o_sem.at[2 + s])

    def turn(src, seqs=(0, 1)):
        for y in range(2):
            for s in seqs:
                @pl.loop(0, 4)
                def _(i):
                    rows = pl.ds(pl.multiple_of(s * 1024 + i * 256, 256), 256)
                    cols = pl.ds(pl.multiple_of(i * 256, 256), 256)
                    lt[y, pl.ds(s * 512, 512), cols] = src[y, rows, :].T

    def weight_grad(g, part):
        rhs = (da, h)[g]
        for y in range(2):
            @pl.loop(0, 2)
            def _(f):
                cols = pl.ds(pl.multiple_of(part * 1024 + f * 512, 512), 512)
                out = mm(lt[y, pl.ds(0, 512), :], rhs[pl.ds(0, 1024), cols])
                out = (out + mm(lt[y, pl.ds(512, 512), :], rhs[pl.ds(1024, 1024), cols])).astype(BF)
                for i in range(8):
                    xi, ci = (i // 2) % 2, i % 2
                    slot = ci * 512 + xi * 256 + (i // 4) * 128 + y * 64
                    wt[g, pl.ds(slot, 64), cols] = out[i * 64 : i * 64 + 64]

    def give(credit):
        for peer in (xpeer, cpeer, znear, zfar):
            pl.semaphore_signal(credit, inc=1, device_id=seqdev(peer), device_id_type=MESH)

    def add_rows(g, cols, base, off, count):
        @pl.loop(0, count)
        def _(i):
            rows = pl.ds(pl.multiple_of(base + i * 64, 64), 64)
            more = da[pl.ds(pl.multiple_of(off + i * 64, 64), 64), cols].astype(F32)
            wt[g, rows, cols] = (wt[g, rows, cols].astype(F32) + more).astype(BF)

    def halving(g, part, step):
        bits = (cc, xc, odd, high)
        partner = (cpeer, xpeer, znear, zfar)
        size = 512 >> step
        keep = 0
        for k in range(step):
            keep = keep + bits[k] * (512 >> k)
        send = keep + (1 - bits[step]) * size
        keep = keep + bits[step] * size
        land = 2048 - (2048 >> step) + g * size
        cols = pl.ds(part * 1024, 1024)
        copy = remote(
            wt.at[g, pl.ds(send, size), cols], da.at[pl.ds(land, size), cols],
            g_send.at[step, 2 * g + part], g_recv.at[step, 2 * g + part], seqdev(partner[step]),
        )
        return copy, keep, land, size, cols

    def scatter_step(g, part, step):
        if step > 0:
            copy, keep, land, size, cols = halving(g, part, step - 1)
            copy.wait()
            if step < 4:
                add_rows(g, cols, keep, land, size // 64)
            else:
                out = gi_out if g == 0 else go_out
                own = wt[g, pl.ds(pl.multiple_of(keep, 64), 64), cols].astype(F32)
                out[:, cols] = (own + da[pl.ds(land, 64), cols].astype(F32)) * (1.0 / 128)
        if step < 4:
            halving(g, part, step)[0].start()

    plain = (((1,), (0,)), ((), ()))

    def build_pick():
        @pl.loop(0, 4)
        def _(t):
            row = lax.broadcasted_iota(jnp.int32, (256, 1024), 0) + t * 256
            col = lax.broadcasted_iota(jnp.int32, (256, 1024), 1)
            want = (row & 7) * 128 + (row >> 3)
            rows = pl.ds(pl.multiple_of(1024 + t * 256, 256), 256)
            da[rows, pl.ds(0, 1024)] = jnp.where(col == want, 1.0, 0.0).astype(BF)

    def pick_rows(t):
        return da[pl.ds(pl.multiple_of(1024 + t * 256, 256), 256), pl.ds(0, 1024)]

    def first(s):
        for m in range(8):
            rows = pl.ds(m * 128, 128)
            h[rows, pl.ds(0, 512)] = mm(ff[m], x[s, rows, :]).astype(BF)

        @pl.loop(0, 4)
        def _(t):
            out = mm(pick_rows(t), h[pl.ds(0, 1024), pl.ds(0, 512)])
            ub[s, pl.ds(t * 4, 4)] = out.astype(BF).reshape(4, 64, 512)

    def build_second():
        for fac, rows in ((ff, 0), (sf, 1024)):
            da[pl.ds(rows, 1024), pl.ds(1024, 1024)] = jnp.zeros((1024, 1024), BF)
            for m in range(8):
                da[pl.ds(rows + m * 128, 128), pl.ds(1024 + m * 128, 128)] = fac[m]

        @pl.loop(0, 4)
        def _(t):
            rows = pl.ds(pl.multiple_of(t * 256, 256), 256)
            lt[0, rows, :] = mm(pick_rows(t), da[pl.ds(0, 1024), pl.ds(1024, 1024)]).astype(BF)
            h[rows, pl.ds(1024, 1024)] = mm(pick_rows(t), da[pl.ds(1024, 1024), pl.ds(1024, 1024)]).astype(BF)

        @pl.loop(0, 4)
        def _(t):
            row = lax.broadcasted_iota(jnp.int32, (1024, 256), 0)
            col = lax.broadcasted_iota(jnp.int32, (1024, 256), 1) + t * 256
            want = ((col >> 3) & 7) * 128 + (col >> 6) * 8 + (col & 7)
            pick = jnp.where(row == want, 1.0, 0.0).astype(BF)
            cols = pl.ds(pl.multiple_of(t * 256, 256), 256)
            for r in range(2):
                rows = pl.ds(r * 512, 512)
                bs[rows, cols] = mm(h[rows, pl.ds(1024, 1024)], pick).astype(BF)

    build_pick()
    loads[0].wait()
    loads[1].wait()
    first(0)
    loads[3].wait()
    loads[4].wait()
    pl.semaphore_wait(barrier, 16)
    gather_own()
    a2a(0, 0)
    loads[5].wait()
    loads[6].wait()
    for q in range(4):
        ycopy(0, q).start()
    loads[2].wait()
    loads[7].wait()
    first(1)
    build_second()
    hold = pltpu.make_async_copy(lt.at[0], bf_hold, ld.at[0])
    hold.start()
    gather_far()
    a2a_recv(0, 0)
    big(wb, bs, uv, 0, plain)
    a2a(1, 0)
    a2a(0, 1)
    gather_mid()
    a2a_recv(1, 0)
    gate_chunk(0)
    gate_chunk(1)
    gather_last()
    a2a_recv(0, 1)
    big(wb, bs, uv, 1, plain)
    a2a(1, 1)
    for q in range(4):
        ycopy(0, q).wait()
    gather_done()
    ycopy(1, 0).wait()
    mlp(0, 0, 256)
    mlp(0, 256, 256)
    ycopy(1, 1).wait()
    mlp(1)
    own_dm(0)
    own_dm(1)
    finish_dm(0)
    a2a_recv(1, 1)
    gate_chunk(2)
    res_own(0)
    finish_dm(1)
    gate_chunk(3)
    res_own(1)
    res_part(0)
    res_part(1)
    hold.wait()
    turn(mixa, (0,))
    ycopy(1, 2).wait()
    mlp(2)
    own_dm(2)
    res_own(2)
    a2a_recv(2, 0)
    a2a_sent(1, 0)
    big(wb, bs, uv, 0, TN)
    a2a(3, 0)
    ycopy(1, 3).wait()
    mlp(3)
    own_dm(3)
    finish_dm(2)
    for k in range(5):
        gathered(k, w_send)
    turn(mixa, (1,))
    weight_grad(0, 0)
    give(credit_a)
    pl.semaphore_wait(credit_a, 4)
    scatter_step(0, 0, 0)
    weight_grad(0, 1)
    give(credit_b)
    scatter_step(0, 0, 1)
    finish_dm(3)
    pl.semaphore_wait(credit_b, 4)
    scatter_step(0, 1, 0)
    res_part(2)
    res_part(3)
    res_own(3)
    scatter_step(0, 1, 1)
    for q in range(4):
        ycopy(3, q).start()
    turn(cota)
    weight_grad(1, 0)
    scatter_step(1, 0, 0)
    weight_grad(1, 1)
    scatter_step(1, 1, 0)
    unhold = pltpu.make_async_copy(bf_hold, lt.at[0], ld.at[0])
    unhold.start()
    scatter_step(1, 0, 1)
    scatter_step(1, 1, 1)
    a2a_recv(2, 1)
    a2a_sent(1, 1)
    big(wb, bs, uv, 1, TN)
    a2a(3, 1)
    scatter_step(0, 0, 2)
    scatter_step(0, 1, 2)
    unhold.wait()
    a2a_recv(3, 0)
    outs = [finish_grad(0)]
    outs[0].start()
    scatter_step(0, 0, 3)
    scatter_step(0, 1, 3)
    scatter_step(1, 0, 2)
    for s in range(2):
        outs.append(finish_res(s))
        outs[-1].start()
    scatter_step(1, 1, 2)
    scatter_step(0, 0, 4)
    scatter_step(0, 1, 4)
    scatter_step(1, 0, 3)
    a2a_recv(3, 1)
    outs.append(finish_grad(1))
    outs[-1].start()
    scatter_step(1, 1, 3)
    scatter_step(1, 0, 4)
    scatter_step(1, 1, 4)
    for kind in (2, 3):
        for s in range(2):
            a2a_sent(kind, s)
    for c in outs:
        c.wait()


def fused(
    inputs, first_factor, second_factor, gate_scale, gate_bias, in_weight, out_weight, cotangent
):
    count, rows, chan = inputs.shape
    hidden = in_weight.shape[1]
    anyspace = pl.BlockSpec(memory_space=pl.ANY)
    vmem = pl.BlockSpec(memory_space=pltpu.VMEM)
    cells = (2, 16, 64, 512)
    dma = pltpu.SemaphoreType.DMA
    buf = pltpu.VMEM
    res, ig, gi, go, _ = pl.pallas_call(
        kernel,
        out_shape=(
            jax.ShapeDtypeStruct((2, 1024, 512), BF),
            jax.ShapeDtypeStruct(cells, BF),
            jax.ShapeDtypeStruct((64, hidden), F32),
            jax.ShapeDtypeStruct((64, hidden), F32),
            jax.ShapeDtypeStruct((1024, 1024), BF),
        ),
        in_specs=[anyspace] * 4 + [vmem] * 2 + [anyspace] * 2,
        out_specs=(anyspace, anyspace, vmem, vmem, anyspace),
        scratch_shapes=[
            buf((2, 1024, 512), BF),
            buf(first_factor.shape, BF),
            buf(second_factor.shape, BF),
            buf((1024, 1024), BF),
            buf((2, 1024, 2048), BF),
            buf(cells, BF),
            buf(cells, BF),
            buf(cells, BF),
            buf(cells, BF),
            buf((2, 2048, 512), BF),
            buf((2, 2048, 512), BF),
            buf((2048, 2048), BF),
            buf((2048, 2048), BF),
            buf(cells, BF),
            buf(cells, BF),
            buf((2048, 512), BF),
            buf(cells, BF),
            buf(cells, BF),
            buf((2048, 512), BF),
            buf((2, 1024, 1024), BF),
            dma((8,)),
            dma((4, 2)),
            dma((4, 2)),
            dma((5, 4)),
            dma((5, 4)),
            dma((5, 2)),
            dma((5, 2)),
            dma((4, 4)),
            dma((4, 4)),
            dma((4,)),
            pltpu.SemaphoreType.REGULAR,
            pltpu.SemaphoreType.REGULAR,
        ],
        compiler_params=pltpu.CompilerParams(
            collective_id=0, has_side_effects=True, vmem_limit_bytes=63 * MIB
        ),
        cost_estimate=pl.CostEstimate(flops=60 * 10**9, bytes_accessed=20 * MIB, transcendentals=0),
    )(
        inputs,
        cotangent,
        first_factor,
        second_factor,
        gate_scale.reshape(1, chan),
        gate_bias.reshape(1, chan),
        in_weight,
        out_weight.T,
    )
    return res, ig.reshape(inputs.shape), gi, go.T


def solution(mesh):
    in_specs = (
        P(None, "seq", "fsdp"),
        P("seq", None, None),
        P("seq", None, None),
        P("fsdp"),
        P("fsdp"),
        P("seq", "fsdp"),
        P("fsdp", "seq"),
        P(None, "seq", "fsdp"),
    )
    out_specs = (P(None, "seq", "fsdp"), P(None, "seq", "fsdp"), P("seq", "fsdp"), P("fsdp", "seq"))
    sizes = (mesh.shape["seq"], mesh.shape["fsdp"])
    part = fused if sizes == (16, 2) else body
    return jax.shard_map(part, mesh=mesh, in_specs=in_specs, out_specs=out_specs, check_vma=False)
```
